32 devices in a mesh: owner: 8 (over z, core), helper: 4 (over y, x).
Axes of the slice: x: 2, y: 2, z: 4, core: 2. Of those that a mesh axis runs over, the one named last changes fastest.
Arguments:
- points: bfloat16 [128, 64, 512], P(('owner', 'helper')), may hold values from -1.5 to 1.5
- weights: bfloat16 [128, 16, 512], P(('owner', 'helper')), may hold values from -6 to 6
- neighbours: int32 [128, 32], P(('owner', 'helper')), may hold values from -1 to 127, as said below
- counts: int32 [128], P(('owner', 'helper')), may hold values from 1 to 32, as said below
Outputs:
- potential: float32 [128, 16, 512], P(('owner', 'helper'))
The draws below stay inside these ranges and needn't reach their ends.
Inputs may be any that keep to these rules, and one draw needn't show every extreme that they name: `neighbours`: slot 0 of a leaf's list holds the leaf itself; slots 0 to counts - 1 hold distinct leaves, each in the same group of 16 consecutive leaves as the listed leaf or in the group just before or just after it; all other slots hold -1. `counts`: some leaf has a full list in every draw.
All inputs are finite; a program needn't handle non-finite values.
Results may differ from the reference program's by a relative error of at most 0.0028.
Values may be sent and summed in bfloat16 or wider, within the bound.
A program may use at most 64 MiB of HBM per device.

```python
import jax
import jax.numpy as jnp
from jax import lax

DIM = 64
NV = 16
LEAF = 512
GROUP = 16
LEAVES = 128
MAXNB = 32


def make_lists(key):
    base_key = jax.random.fold_in(key, 31)
    heavy_key, forced_key, light_key, score_key = jax.random.split(base_key, 4)
    leaf_ids = jnp.arange(LEAVES, dtype=jnp.int32)
    heavy = jax.random.randint(heavy_key, (LEAVES,), 0, 8) == 0
    forced = jax.random.randint(forced_key, (), 0, LEAVES)
    heavy = heavy | (leaf_ids == forced)
    light = jax.random.randint(light_key, (LEAVES,), 1, MAXNB // 4 + 1)
    sizes = jnp.where(heavy, MAXNB, light).astype(jnp.int32)
    offsets = jnp.arange(3 * GROUP, dtype=jnp.int32)
    starts = (leaf_ids // GROUP - 1) * GROUP
    candidates = starts[:, None] + offsets[None, :]
    usable = (candidates >= 0) & (candidates < LEAVES) & (candidates != leaf_ids[:, None])
    scores = jax.random.randint(score_key, (LEAVES, 3 * GROUP), 0, 1 << 20) * (3 * GROUP) + offsets[None, :]
    scores = jnp.where(usable, scores, -1)
    picked_scores, picked = lax.top_k(scores, MAXNB - 1)
    chosen = jnp.take_along_axis(candidates, picked, axis=1)
    lists = jnp.concatenate([leaf_ids[:, None], chosen], axis=1)
    slots = jnp.arange(MAXNB, dtype=jnp.int32)
    lists = jnp.where(slots[None, :] < sizes[:, None], lists, -1)
    return (lists.astype(jnp.int32), sizes)


def draw_neighbours(key, part):
    lists, sizes = make_lists(key)
    return lists


def draw_counts(key, part):
    lists, sizes = make_lists(key)
    return sizes


def block_scale(rng, dims, cuts, smallest, high):
    def one(dim, shards_of):
        heights = jax.random.uniform(jax.random.fold_in(jax.random.fold_in(rng, 6), dim), (shards_of,), jnp.float32, smallest / len(cuts), high / len(cuts))
        return jnp.repeat(jnp.exp(heights), dims[dim] // shards_of).reshape((-1,) + (1,) * (len(dims) - dim - 1))

    factor_of = one(*cuts[0])
    for cut in cuts[1:]:
        factor_of = factor_of * one(*cut)
    return factor_of


def noise(key, shape, spread, reach, shards=(), held_as=jnp.bfloat16):
    entries = jax.random.normal(key, shape, jnp.float32) * spread
    if len(shards) > 0:
        entries = block_scale(key, shape, shards, -0.22, 0.18) * entries
    return jnp.clip(entries, min=-reach, max=reach).astype(held_as)


def setup_inputs(seed: int = 0) -> dict:
    key_of = jax.random.split(jax.random.key(seed), 5)
    return {
        "points": noise(key_of[0], (LEAVES, DIM, LEAF), (2.0 / DIM ** 0.5), 1.5, ((0, 32),)),
        "weights": noise(key_of[1], (LEAVES, NV, LEAF), 1.0, 6.0, ((0, 32),)),
        "neighbours": draw_neighbours(jax.random.fold_in(key_of[4], 71), 0),
        "counts": draw_counts(jax.random.fold_in(key_of[4], 71), 0),
    }


def block_sum(target_points, target_norms, source_points, source_norms, source_weights):
    inner = lax.dot_general(source_points, target_points, (((0,), (0,)), ((), ())), preferred_element_type=jnp.float32)
    kernel = jnp.exp(inner - 0.5 * source_norms[:, None] - 0.5 * target_norms[None, :]).astype(jnp.bfloat16)
    return jnp.dot(source_weights, kernel, preferred_element_type=jnp.float32)


def reference(points, weights, neighbours, counts):
    widened = points.astype(jnp.float32)
    norms = jnp.einsum("ldp,ldp->lp", widened, widened)

    def one_leaf(leaf):
        def add_pair(slot, total):
            source = neighbours[leaf, slot]
            return total + block_sum(points[leaf], norms[leaf], points[source], norms[source], weights[source])

        start = jnp.zeros((weights.shape[1], points.shape[2]), jnp.float32)
        return lax.fori_loop(0, counts[leaf], add_pair, start)

    return lax.map(one_leaf, jnp.arange(points.shape[0], dtype=jnp.int32))
```

```python
import functools

import jax
import jax.numpy as jnp
from jax import lax
from jax.experimental import pallas as pl
from jax.experimental.pallas import tpu as pltpu
from jax.sharding import PartitionSpec as P

MESH = pl.DeviceIdType.MESH
EXTRA = 16
TOGETHER = 4
VMEM_BYTES = 40 << 20


def partner_of(index, distance):
    result = index
    bit = 1
    while bit <= distance:
        if distance & bit:
            result = result + bit - 2 * bit * ((index // bit) % 2)
        bit *= 2
    return result


def list_tasks(base, helper, local, lists):
    group, slots = lists.shape
    count = 3 * local
    length = task_length(group, local)
    lists = jnp.where(lists < 0, -(1 << 20), lists)
    column = lax.broadcasted_iota(jnp.int32, (group, 128), 1)
    listed = []
    table = jnp.zeros((group, 128), jnp.float32)
    for source in range(count):
        leaf = base + (source // local) * group + helper * local + source % local
        one = jnp.max(jnp.where(lists == leaf, 1.0, 0.0), axis=1, keepdims=True)
        listed.append(one)
        table = jnp.where(column == source, one, table)
    below = lax.broadcasted_iota(jnp.int32, (group, group), 0) > lax.broadcasted_iota(jnp.int32, (group, group), 1)
    ahead = jnp.dot(
        jnp.where(below, 1.0, 0.0).astype(jnp.bfloat16), table.astype(jnp.bfloat16), preferred_element_type=jnp.float32
    )
    place = lax.broadcasted_iota(jnp.int32, (group, length), 1).astype(jnp.float32)
    row = lax.broadcasted_iota(jnp.int32, (group, length), 0).astype(jnp.float32)
    total = jnp.zeros((1, 1), jnp.float32)
    targets = jnp.zeros((group, length), jnp.float32)
    sources = jnp.zeros((group, length), jnp.float32)
    for source in range(count):
        here = jnp.where(listed[source] > 0.5, ahead[:, source:source + 1] + total, -1.0)
        targets = jnp.where(place == here, row, targets)
        sources = jnp.where(place == here, float(source), sources)
        total = total + jnp.sum(listed[source], axis=0, keepdims=True)
    target = jnp.where(place[:1] < total, jnp.sum(targets, axis=0, keepdims=True), float(group))
    source = jnp.sum(sources, axis=0, keepdims=True)
    line = lax.broadcasted_iota(jnp.int32, (8, length), 0)
    result = jnp.where(line == 0, target, jnp.where(line == 1, source, total))
    return result.astype(jnp.int32)


def task_length(group, local):
    return -(-(group * 3 * local + 3 * TOGETHER) // 128) * 128


def gather_kernel(owners, helpers, points, weights, lists, far_points, near_points, near_weights, tasks,
                  far_lists, send_sems, recv_sems):
    local = lists.shape[0]
    owner = lax.axis_index("owner")
    helper = lax.axis_index("helper")
    has_before = owner > 0
    has_after = owner < owners - 1
    barrier = pltpu.get_barrier_semaphore()
    for distance in range(1, helpers):
        pl.semaphore_signal(
            barrier, inc=1, device_id=(owner, partner_of(helper, distance)), device_id_type=MESH
        )

    @pl.when(has_before)
    def _():
        pl.semaphore_signal(barrier, inc=1, device_id=(owner - 1, helper), device_id_type=MESH)

    @pl.when(has_after)
    def _():
        pl.semaphore_signal(barrier, inc=1, device_id=(owner + 1, helper), device_id_type=MESH)

    neighbours = lax.min(owner, 1) + lax.min(owners - 1 - owner, 1)
    pl.semaphore_wait(barrier, helpers - 1 + neighbours)

    def copy(number, src, dst, device):
        return pltpu.make_async_remote_copy(
            src_ref=src,
            dst_ref=dst,
            send_sem=send_sems.at[number],
            recv_sem=recv_sems.at[number],
            device_id=device,
            device_id_type=MESH,
        )

    def beside(distance):
        return (owner, partner_of(helper, distance))

    number = 0
    list_copies = []
    for distance in range(1, helpers):
        list_copies.append(copy(number, lists, far_lists.at[distance - 1], beside(distance)))
        number += 1
    sent, relayed = [], []
    if helpers == 4 and local % 2 == 0:
        half = local // 2
        parts = (pl.ds(0, half), pl.ds(half, half))
        for order in (0, 1):
            for distance in (1, 2):
                part = parts[order if distance == 1 else 1 - order]
                one = copy(number, points.at[part], far_points.at[distance - 1, part], beside(distance))
                number += 1
                sent.append(one)
        for distance in (1, 2):
            part = parts[distance - 1]
            block = far_points.at[distance - 1, part]
            one = copy(number, block, far_points.at[2, part], beside(3 - distance))
            number += 1
            relayed.append(one)
    else:
        for distance in range(1, helpers):
            sent.append(copy(number, points, far_points.at[distance - 1], beside(distance)))
            number += 1
    up = [
        copy(number, points, near_points.at[0], (owner + 1, helper)),
        copy(number + 1, weights, near_weights.at[0], (owner + 1, helper)),
    ]
    down = [
        copy(number + 2, points, near_points.at[1], (owner - 1, helper)),
        copy(number + 3, weights, near_weights.at[1], (owner - 1, helper)),
    ]
    for one in list_copies + sent:
        one.start()

    @pl.when(has_after)
    def _():
        for one in up:
            one.start()

    @pl.when(has_before)
    def _():
        for one in down:
            one.start()

    for place, one in enumerate(relayed):
        sent[place].wait_recv()
        one.start()
    for one in list_copies:
        one.wait_recv()
    whole = jnp.concatenate([lists[...]] + [far_lists[i] for i in range(helpers - 1)], axis=0)
    tasks[...] = list_tasks((owner - 1) * local * helpers, helper, local, whole)
    for one in sent[len(relayed):] + relayed:
        one.wait_recv()
    for one in list_copies + sent + relayed:
        one.wait_send()

    @pl.when(has_after)
    def _():
        for one in up:
            one.wait_send()
        for one in down:
            one.wait_recv()

    @pl.when(has_before)
    def _():
        for one in down:
            one.wait_send()
        for one in up:
            one.wait_recv()


def gather_window(owners, helpers, points, weights, lists):
    local = points.shape[0]
    copies = 2 * (helpers - 1) + 10
    vmem = pl.BlockSpec(memory_space=pltpu.VMEM)
    any_space = pl.BlockSpec(memory_space=pl.ANY)
    return pl.pallas_call(
        functools.partial(gather_kernel, owners, helpers),
        out_shape=(
            jax.ShapeDtypeStruct((helpers - 1,) + points.shape, points.dtype),
            jax.ShapeDtypeStruct((2,) + points.shape, points.dtype),
            jax.ShapeDtypeStruct((2,) + weights.shape, weights.dtype),
            jax.ShapeDtypeStruct((8, task_length(local * helpers, local)), jnp.int32),
        ),
        in_specs=[any_space, any_space, vmem],
        out_specs=(any_space, any_space, any_space, vmem),
        scratch_shapes=[
            pltpu.VMEM((helpers - 1,) + lists.shape, lists.dtype),
            pltpu.SemaphoreType.DMA((copies,)),
            pltpu.SemaphoreType.DMA((copies,)),
        ],
        compiler_params=pltpu.CompilerParams(collective_id=0, has_side_effects=True),
        name="gather_window",
    )(points, weights, lists)


def pieces_of(value, count):
    parts = []
    for _ in range(count):
        part = value.astype(jnp.bfloat16).astype(jnp.float32)
        parts.append(part)
        value = value - part
    return parts


def extra_rows(first, second, rows, width):
    row = lax.broadcasted_iota(jnp.int32, (rows, width), 0)
    result = jnp.zeros((rows, width), jnp.float32)
    for i, value in enumerate(list(first) + list(second)):
        result = jnp.where(row == i, value, result)
    return result


def pairs_kernel(local, helpers, tasks, points, weights, far_points, near_points, near_weights,
                 own_sums, far_sums, out, targets, sources, held_weights, exponents, kernels):
    dims, width = points.shape[1:]
    group = local * helpers
    depth = targets.shape[1]
    ones = [jnp.ones((1, width), jnp.float32)] * 3

    def half_norm(value):
        return pieces_of(-0.5 * jnp.sum(value * value, axis=0, keepdims=True), 3)

    def prepare_target(index, block):
        targets[index, pl.ds(0, dims), :] = block
        targets[index, pl.ds(dims, depth - dims), :] = extra_rows(
            ones, half_norm(block.astype(jnp.float32)), depth - dims, width
        ).astype(jnp.bfloat16)

    def prepare_source(index, block):
        value = block.astype(jnp.float32)
        rows = [value, extra_rows(half_norm(value), ones, depth - dims, width)]
        sources[index] = jnp.concatenate(rows, axis=0).T.astype(jnp.bfloat16)

    def each_leaf(leaf, carry):
        prepare_target(leaf, points[leaf])
        prepare_source(local + leaf, points[leaf])
        prepare_source(leaf, near_points[0, leaf])
        prepare_source(2 * local + leaf, near_points[1, leaf])
        held_weights[leaf] = near_weights[0, leaf]
        held_weights[local + leaf] = weights[leaf]
        held_weights[2 * local + leaf] = near_weights[1, leaf]
        return carry

    for leaf in range(local):
        each_leaf(leaf, 0)

    def each_far(distance, carry):
        for leaf in range(local):
            prepare_target((distance + 1) * local + leaf, far_points[distance, leaf])
        return carry

    lax.fori_loop(0, helpers - 1, each_far, 0)

    total = tasks[2, 0]
    out[...] = jnp.zeros(out.shape, jnp.float32)

    def add_products(step):
        for part in range(TOGETHER):
            number = step * TOGETHER + part
            source, target = tasks[1, number], tasks[0, number]
            out[target] += jnp.dot(held_weights[source], kernels[part], preferred_element_type=jnp.float32)

    def take_exponentials():
        for part in range(TOGETHER):
            kernels[part] = jnp.exp(exponents[part]).astype(jnp.bfloat16)

    def find_exponents(step):
        for part in range(TOGETHER):
            number = step * TOGETHER + part
            source, target = tasks[1, number], tasks[0, number]
            exponents[part] = jnp.dot(sources[source], targets[target], preferred_element_type=jnp.float32)

    find_exponents(0)
    take_exponentials()
    find_exponents(1)

    def each_step(step, carry):
        add_products(step)
        take_exponentials()
        find_exponents(step + 2)
        return carry

    steps = lax.div(total + TOGETHER - 1, TOGETHER)
    lax.fori_loop(0, steps - 1, each_step, 0)

    @pl.when(total > 0)
    def _():
        add_products(steps - 1)

    own_sums[...] = out[pl.ds(0, local)]
    far_sums[...] = out[pl.ds(local, group - local)].astype(jnp.bfloat16).reshape(far_sums.shape)


def sum_pairs(helpers, points, weights, far_points, near_points, near_weights, tasks):
    local, dims, width = points.shape
    vectors = weights.shape[1]
    group = local * helpers
    vmem = pl.BlockSpec(memory_space=pltpu.VMEM)
    smem = pl.BlockSpec(memory_space=pltpu.SMEM)
    return pl.pallas_call(
        functools.partial(pairs_kernel, local, helpers),
        out_shape=(
            jax.ShapeDtypeStruct((local, vectors, width), jnp.float32),
            jax.ShapeDtypeStruct((helpers - 1, local, vectors, width), jnp.bfloat16),
        ),
        in_specs=[smem] + [vmem] * 5,
        out_specs=(vmem, vmem),
        scratch_shapes=[
            pltpu.VMEM((group + 1, vectors, width), jnp.float32),
            pltpu.VMEM((group + 1, dims + EXTRA, width), jnp.bfloat16),
            pltpu.VMEM((3 * local, width, dims + EXTRA), jnp.bfloat16),
            pltpu.VMEM((3 * local, vectors, width), jnp.bfloat16),
            pltpu.VMEM((TOGETHER, width, width), jnp.float32),
            pltpu.VMEM((TOGETHER, width, width), jnp.bfloat16),
        ],
        name="sum_pairs",
    )(tasks, points, weights, far_points, near_points, near_weights)


def return_kernel(helpers, far_sums, landed, send_sems, recv_sems):
    owner = lax.axis_index("owner")
    helper = lax.axis_index("helper")
    barrier = pltpu.get_barrier_semaphore()
    for distance in range(1, helpers):
        pl.semaphore_signal(
            barrier, inc=1, device_id=(owner, partner_of(helper, distance)), device_id_type=MESH
        )
    pl.semaphore_wait(barrier, helpers - 1)
    copies = []
    for distance in range(1, helpers):
        one = pltpu.make_async_remote_copy(
            src_ref=far_sums.at[distance - 1],
            dst_ref=landed.at[distance - 1],
            send_sem=send_sems.at[distance - 1],
            recv_sem=recv_sems.at[distance - 1],
            device_id=(owner, partner_of(helper, distance)),
            device_id_type=MESH,
        )
        one.start()
        copies.append(one)
    for one in copies:
        one.wait()


def return_sums(helpers, far_sums):
    any_space = pl.BlockSpec(memory_space=pl.ANY)
    return pl.pallas_call(
        functools.partial(return_kernel, helpers),
        out_shape=jax.ShapeDtypeStruct(far_sums.shape, far_sums.dtype),
        in_specs=[any_space],
        out_specs=any_space,
        scratch_shapes=[pltpu.SemaphoreType.DMA((helpers - 1,)), pltpu.SemaphoreType.DMA((helpers - 1,))],
        compiler_params=pltpu.CompilerParams(collective_id=1, has_side_effects=True),
        name="return_sums",
    )(far_sums)


ALONE, FIRST, SECOND, THIRD = 4, 4, 8, 4


def slot_count(local):
    return local + FIRST + SECOND + THIRD


def phase_of(target, source, local):
    half = local // 2
    own = target < local
    early = own | ((target >= local) & (target < local + half)) | ((target >= 2 * local + half) & (target < 3 * local))
    phase = jnp.where(target < 3 * local, 2, 3)
    phase = jnp.where(early, 1, phase)
    return jnp.where(own & (source < 2 * local), 0, phase)


def order_tasks(bases, local, lists):
    group, slots = lists.shape
    count = 3 * local
    length = task_length(group, local)
    lists = jnp.where(lists < 0, -(1 << 20), lists)
    row = lax.broadcasted_iota(jnp.int32, (group, 128), 0)
    column = lax.broadcasted_iota(jnp.int32, (group, 128), 1)
    table = jnp.zeros((group, 128), jnp.float32)
    for source in range(count):
        leaf = bases[source // local] + source % local
        one = jnp.max(jnp.where(lists == leaf, 1.0, 0.0), axis=1, keepdims=True)
        table = jnp.where(column == source, one, table)
    table = jnp.where((row == column) & (row < local), 0.0, table)
    phase = phase_of(row, column, local)
    phased = jnp.concatenate([jnp.where(phase == p, table, 0.0) for p in range(4)], axis=0)
    rows = 4 * group
    counted = phased.astype(jnp.bfloat16)
    above = lax.broadcasted_iota(jnp.int32, (rows, rows), 0) > lax.broadcasted_iota(jnp.int32, (rows, rows), 1)
    left = lax.broadcasted_iota(jnp.int32, (128, 128), 0) < lax.broadcasted_iota(jnp.int32, (128, 128), 1)
    inside = jnp.dot(counted, jnp.where(left, 1.0, 0.0).astype(jnp.bfloat16), preferred_element_type=jnp.float32)
    before = jnp.dot(jnp.where(above, 1.0, 0.0).astype(jnp.bfloat16), counted, preferred_element_type=jnp.float32)
    rank = inside + jnp.sum(before, axis=1, keepdims=True)
    rank = jnp.where(phased > 0.5, rank + 1.0, 0.0)
    rank = sum(rank[p * group:(p + 1) * group] for p in range(4)) - 1.0
    in_row = jnp.sum(phased, axis=1, keepdims=True)
    ends = [jnp.sum(in_row[:(p + 1) * group], axis=0, keepdims=True) for p in range(4)]
    place = lax.broadcasted_iota(jnp.int32, (group, length), 1).astype(jnp.float32)
    code_row = lax.broadcasted_iota(jnp.int32, (group, length), 0).astype(jnp.float32) * 256.0
    codes = jnp.zeros((group, length), jnp.float32)
    for source in range(count):
        codes = jnp.where(place == rank[:, source:source + 1], code_row + float(source), codes)
    codes = jnp.sum(codes, axis=0, keepdims=True)
    codes = jnp.where(place[:1] < ends[3], codes, float(group * 256)).astype(jnp.int32)
    line = lax.broadcasted_iota(jnp.int32, (8, length), 0)
    result = jnp.where(line == 0, codes // 256, codes % 256)
    for p in range(4):
        result = jnp.where(line == 2 + p, ends[p].astype(jnp.int32), result)
    return result


def within(value, last):
    return lax.max(lax.min(value, last), 0)


def slot_starts(tasks):
    second = lax.min(tasks[2, 0], FIRST)
    third = lax.min(tasks[3, 0], second + SECOND)
    rest = lax.min(tasks[4, 0], third + THIRD)
    return 0, second, third, rest


def slot_task(tasks, group, start, end, slot):
    number = within(start + slot, tasks.shape[1] - 1)
    inside = number < end
    target = jnp.where(inside, tasks[0, number], group)
    return within(tasks[1, number], 3 * group // 4 - 1), within(target, group)


def window_kernel(owners, points, weights, lists, sources, targets, held_weights, tasks, results,
                  own_points, own_weights, lists_here, far_lists, far_points, near_points, near_weights,
                  kernels, task_scalars, send_sems, recv_sems, local_sems):
    local, dims, width = points.shape
    helpers = 4
    group = local * helpers
    half = local // 2
    depth = targets.shape[1]
    owner = lax.axis_index("owner")
    helper = lax.axis_index("helper")
    odd = lax.rem(owner, 2)
    chip_owner = owner + 1 - 2 * odd
    next_owner = owner - 1 + 2 * odd
    has_next = (next_owner >= 0) & (next_owner < owners)

    fetches = [
        pltpu.make_async_copy(src, dst, local_sems.at[i])
        for i, (src, dst) in enumerate(
            ((points, own_points), (weights, own_weights), (lists, lists_here))
        )
    ]
    for one in fetches:
        one.start()

    def beside(distance):
        return (owner, partner_of(helper, distance))

    barrier = pltpu.get_barrier_semaphore()
    for device in [beside(1), beside(2), beside(3), (chip_owner, helper)]:
        pl.semaphore_signal(barrier, inc=1, device_id=device, device_id_type=MESH)

    @pl.when(has_next)
    def _():
        pl.semaphore_signal(barrier, inc=1, device_id=(next_owner, helper), device_id_type=MESH)

    pl.semaphore_wait(barrier, helpers + jnp.where(has_next, 1, 0))

    def copy(number, src, dst, device):
        return pltpu.make_async_remote_copy(
            src_ref=src,
            dst_ref=dst,
            send_sem=send_sems.at[number],
            recv_sem=recv_sems.at[number],
            device_id=device,
            device_id_type=MESH,
        )

    parts = (pl.ds(0, half), pl.ds(half, half))
    list_copies = [copy(d - 1, lists, far_lists.at[d - 1], beside(d)) for d in (1, 2, 3)]
    sent = []
    for order in (0, 1):
        for distance in (1, 2):
            part = parts[order if distance == 1 else 1 - order]
            sent.append(
                copy(3 + len(sent), points.at[part], far_points.at[distance - 1, part], beside(distance))
            )
    relayed = []
    for distance in (1, 2):
        part = parts[distance - 1]
        relayed.append(
            copy(6 + distance, far_points.at[distance - 1, part], far_points.at[2, part], beside(3 - distance))
        )
    chip = [
        copy(9, points, near_points.at[0], (chip_owner, helper)),
        copy(10, weights, near_weights.at[0], (chip_owner, helper)),
    ]
    beyond = [
        copy(11, points, near_points.at[1], (next_owner, helper)),
        copy(12, weights, near_weights.at[1], (next_owner, helper)),
    ]
    for one in list_copies + sent[:2] + chip:
        one.start()

    @pl.when(has_next)
    def _():
        for one in beyond:
            one.start()

    for one in sent[2:]:
        one.start()

    ones = [jnp.ones((1, width), jnp.float32)] * 3

    def half_norm(value):
        return pieces_of(-0.5 * jnp.sum(value * value, axis=0, keepdims=True), 3)

    def prepare_target(index, block):
        targets[index, pl.ds(0, dims), :] = block
        targets[index, pl.ds(dims, depth - dims), :] = extra_rows(
            ones, half_norm(block.astype(jnp.float32)), depth - dims, width
        ).astype(jnp.bfloat16)

    def prepare_source(index, block):
        value = block.astype(jnp.float32)
        rows = [value, extra_rows(half_norm(value), ones, depth - dims, width)]
        sources[index] = jnp.concatenate(rows, axis=0).T.astype(jnp.bfloat16)

    def work(pairs, base):
        for i, (source, target) in enumerate(pairs):
            exponents = jnp.dot(sources[source], targets[target], preferred_element_type=jnp.float32)
            kernels[i] = jnp.exp(exponents).astype(jnp.bfloat16)
        for i, (source, target) in enumerate(pairs):
            results[base + i] = jnp.dot(held_weights[source], kernels[i], preferred_element_type=jnp.float32)

    def work_slots(start, end, slots, base):
        def batch(step, carry):
            pairs = [slot_task(task_scalars, group, start, end, step * ALONE + i) for i in range(ALONE)]
            work(pairs, base + step * ALONE)
            return carry

        lax.fori_loop(0, slots // ALONE, batch, 0)

    for one in fetches[:2]:
        one.wait()
    for leaf in range(local):
        prepare_target(leaf, own_points[leaf])
        prepare_source(leaf, own_points[leaf])
        held_weights[leaf] = own_weights[leaf]
    targets[group] = jnp.zeros(targets.shape[1:], jnp.bfloat16)
    work([(leaf, leaf) for leaf in range(local)], 0)

    fetches[2].wait()
    for one in list_copies:
        one.wait_recv()
    whole = jnp.concatenate([lists_here[...]] + [far_lists[i] for i in range(helpers - 1)], axis=0)
    bases = [o * group + helper * local for o in (owner, chip_owner, next_owner)]
    tasks[...] = order_tasks(bases, local, whole)
    to_scalars = pltpu.make_async_copy(tasks, task_scalars, local_sems.at[3])
    to_scalars.start()
    for one in chip:
        one.wait_recv()
    for leaf in range(local):
        prepare_source(local + leaf, near_points[0, leaf])
        held_weights[local + leaf] = near_weights[0, leaf]
    to_scalars.wait()
    starts = slot_starts(task_scalars)
    work_slots(starts[0], task_scalars[2, 0], FIRST, local)

    for place, one in enumerate(relayed):
        sent[place].wait_recv()
        one.start()
    for leaf in range(half):
        prepare_target(local + leaf, far_points[0, leaf])
        prepare_target(2 * local + half + leaf, far_points[1, half + leaf])

    @pl.when(has_next)
    def _():
        for one in beyond:
            one.wait_recv()
        for leaf in range(local):
            prepare_source(2 * local + leaf, near_points[1, leaf])
            held_weights[2 * local + leaf] = near_weights[1, leaf]

    work_slots(starts[1], task_scalars[3, 0], SECOND, local + FIRST)

    for one in sent[2:]:
        one.wait_recv()
    for leaf in range(half):
        prepare_target(local + half + leaf, far_points[0, half + leaf])
        prepare_target(2 * local + leaf, far_points[1, leaf])
    work_slots(starts[2], task_scalars[4, 0], THIRD, local + FIRST + SECOND)

    for one in relayed:
        one.wait_recv()
    for leaf in range(local):
        prepare_target(3 * local + leaf, far_points[2, leaf])
    for one in list_copies + sent + relayed + chip:
        one.wait_send()

    @pl.when(has_next)
    def _():
        for one in beyond:
            one.wait_send()


def gather_and_begin(owners, points, weights, lists):
    local, dims, width = points.shape
    vectors = weights.shape[1]
    group = 4 * local
    depth = dims + EXTRA
    vmem = pl.BlockSpec(memory_space=pltpu.VMEM)
    hbm = pl.BlockSpec(memory_space=pltpu.HBM)
    length = task_length(group, local)
    return pl.pallas_call(
        functools.partial(window_kernel, owners),
        out_shape=(
            pltpu.VMEM((3 * local, width, depth), jnp.bfloat16),
            pltpu.VMEM((group + 1, depth, width), jnp.bfloat16),
            pltpu.VMEM((3 * local, vectors, width), jnp.bfloat16),
            pltpu.VMEM((8, length), jnp.int32),
            pltpu.VMEM((slot_count(local), vectors, width), jnp.float32),
        ),
        in_specs=[hbm, hbm, hbm],
        out_specs=(vmem,) * 5,
        scratch_shapes=[
            pltpu.VMEM(points.shape, points.dtype),
            pltpu.VMEM(weights.shape, weights.dtype),
            pltpu.VMEM(lists.shape, lists.dtype),
            pltpu.VMEM((3,) + lists.shape, lists.dtype),
            pltpu.VMEM((3,) + points.shape, points.dtype),
            pltpu.VMEM((2,) + points.shape, points.dtype),
            pltpu.VMEM((2,) + weights.shape, weights.dtype),
            pltpu.VMEM((ALONE, width, width), jnp.bfloat16),
            pltpu.SMEM((8, length), jnp.int32),
            pltpu.SemaphoreType.DMA((13,)),
            pltpu.SemaphoreType.DMA((13,)),
            pltpu.SemaphoreType.DMA((4,)),
        ],
        compiler_params=pltpu.CompilerParams(
            collective_id=2, has_side_effects=True, vmem_limit_bytes=VMEM_BYTES
        ),
        name="gather_and_begin",
    )(*(pltpu.with_memory_space_constraint(one, pltpu.HBM) for one in (points, weights, lists)))


def rest_kernel(local, tasks, sources, targets, held_weights, results, own_sums, far_sums, out, exponents, kernels):
    width = targets.shape[2]
    group = 4 * local
    starts = slot_starts(tasks)
    first = starts[3]
    total = tasks[5, 0] - first

    def add_products(step):
        for part in range(TOGETHER):
            number = first + step * TOGETHER + part
            source, target = tasks[1, number], tasks[0, number]
            out[target] += jnp.dot(held_weights[source], kernels[part], preferred_element_type=jnp.float32)

    def take_exponentials():
        for part in range(TOGETHER):
            kernels[part] = jnp.exp(exponents[part]).astype(jnp.bfloat16)

    def find_exponents(step):
        for part in range(TOGETHER):
            number = first + step * TOGETHER + part
            source, target = tasks[1, number], tasks[0, number]
            exponents[part] = jnp.dot(sources[source], targets[target], preferred_element_type=jnp.float32)

    find_exponents(0)
    for leaf in range(local):
        out[leaf] = results[leaf]
    out[pl.ds(local, group + 1 - local)] = jnp.zeros((group + 1 - local,) + out.shape[1:], jnp.float32)
    base = local
    for phase, slots in enumerate((FIRST, SECOND, THIRD)):
        for slot in range(slots):
            _, target = slot_task(tasks, group, starts[phase], tasks[2 + phase, 0], slot)
            out[target] += results[base + slot]
        base += slots
    take_exponentials()
    find_exponents(1)

    def each_step(step, carry):
        add_products(step)
        take_exponentials()
        find_exponents(step + 2)
        return carry

    steps = lax.div(total + TOGETHER - 1, TOGETHER)
    lax.fori_loop(0, steps - 1, each_step, 0)

    @pl.when(total > 0)
    def _():
        add_products(steps - 1)

    own_sums[...] = out[pl.ds(0, local)]
    far_sums[...] = out[pl.ds(local, group - local)].astype(jnp.bfloat16).reshape(far_sums.shape)


def sum_rest(local, sources, targets, held_weights, tasks, results):
    width = targets.shape[2]
    vectors = held_weights.shape[1]
    group = 4 * local
    vmem = pl.BlockSpec(memory_space=pltpu.VMEM)
    smem = pl.BlockSpec(memory_space=pltpu.SMEM)
    return pl.pallas_call(
        functools.partial(rest_kernel, local),
        out_shape=(
            pltpu.VMEM((local, vectors, width), jnp.float32),
            pltpu.VMEM((3, local, vectors, width), jnp.bfloat16),
        ),
        in_specs=[smem] + [vmem] * 4,
        out_specs=(vmem, vmem),
        scratch_shapes=[
            pltpu.VMEM((group + 1, vectors, width), jnp.float32),
            pltpu.VMEM((TOGETHER, width, width), jnp.float32),
            pltpu.VMEM((TOGETHER, width, width), jnp.bfloat16),
        ],
        compiler_params=pltpu.CompilerParams(vmem_limit_bytes=VMEM_BYTES),
        name="sum_rest",
    )(tasks, sources, targets, held_weights, results)


def return_in_vmem(far_sums):
    vmem = pl.BlockSpec(memory_space=pltpu.VMEM)
    return pl.pallas_call(
        functools.partial(return_kernel, 4),
        out_shape=pltpu.VMEM(far_sums.shape, far_sums.dtype),
        in_specs=[vmem],
        out_specs=vmem,
        scratch_shapes=[pltpu.SemaphoreType.DMA((3,)), pltpu.SemaphoreType.DMA((3,))],
        compiler_params=pltpu.CompilerParams(
            collective_id=3, has_side_effects=True, vmem_limit_bytes=VMEM_BYTES
        ),
        name="return_in_vmem",
    )(far_sums)


def on_device(points, weights, neighbours, counts):
    owners = lax.axis_size("owner")
    helpers = lax.axis_size("helper")
    local = points.shape[0]
    if helpers == 4 and local == ALONE and owners % 2 == 0:
        sources, targets, held_weights, tasks, results = gather_and_begin(owners, points, weights, neighbours)
        own_sums, far_sums = sum_rest(local, sources, targets, held_weights, tasks, results)
        landed = return_in_vmem(far_sums)
        return own_sums + (landed[0].astype(jnp.float32) + landed[1].astype(jnp.float32) + landed[2].astype(jnp.float32))
    far_points, near_points, near_weights, tasks = gather_window(owners, helpers, points, weights, neighbours)
    own_sums, far_sums = sum_pairs(helpers, points, weights, far_points, near_points, near_weights, tasks)
    landed = return_sums(helpers, far_sums)
    return own_sums + jnp.sum(landed.astype(jnp.float32), axis=0)


def solution(mesh):
    placed = (
        P(("owner", "helper"), None, None),
        P(("owner", "helper"), None, None),
        P(("owner", "helper"), None),
        P(("owner", "helper")),
    )
    return jax.shard_map(
        on_device,
        mesh=mesh,
        in_specs=placed,
        out_specs=P(("owner", "helper"), None, None),
        check_vma=False,
    )
```

```python
import functools

import jax
import jax.numpy as jnp
from jax import lax
from jax.experimental import pallas as pl
from jax.experimental.pallas import tpu as pltpu
from jax.sharding import PartitionSpec as P

MESH = pl.DeviceIdType.MESH
EXTRA = 16
TOGETHER = 4
VMEM_BYTES = 40 << 20


def partner_of(index, distance):
    result = index
    bit = 1
    while bit <= distance:
        if distance & bit:
            result = result + bit - 2 * bit * ((index // bit) % 2)
        bit *= 2
    return result


def list_tasks(base, helper, local, lists):
    group, slots = lists.shape
    count = 3 * local
    length = task_length(group, local)
    lists = jnp.where(lists < 0, -(1 << 20), lists)
    column = lax.broadcasted_iota(jnp.int32, (group, 128), 1)
    listed = []
    table = jnp.zeros((group, 128), jnp.float32)
    for source in range(count):
        leaf = base + (source // local) * group + helper * local + source % local
        one = jnp.max(jnp.where(lists == leaf, 1.0, 0.0), axis=1, keepdims=True)
        listed.append(one)
        table = jnp.where(column == source, one, table)
    below = lax.broadcasted_iota(jnp.int32, (group, group), 0) > lax.broadcasted_iota(jnp.int32, (group, group), 1)
    ahead = jnp.dot(
        jnp.where(below, 1.0, 0.0).astype(jnp.bfloat16), table.astype(jnp.bfloat16), preferred_element_type=jnp.float32
    )
    place = lax.broadcasted_iota(jnp.int32, (group, length), 1).astype(jnp.float32)
    row = lax.broadcasted_iota(jnp.int32, (group, length), 0).astype(jnp.float32)
    total = jnp.zeros((1, 1), jnp.float32)
    targets = jnp.zeros((group, length), jnp.float32)
    sources = jnp.zeros((group, length), jnp.float32)
    for source in range(count):
        here = jnp.where(listed[source] > 0.5, ahead[:, source:source + 1] + total, -1.0)
        targets = jnp.where(place == here, row, targets)
        sources = jnp.where(place == here, float(source), sources)
        total = total + jnp.sum(listed[source], axis=0, keepdims=True)
    target = jnp.where(place[:1] < total, jnp.sum(targets, axis=0, keepdims=True), float(group))
    source = jnp.sum(sources, axis=0, keepdims=True)
    line = lax.broadcasted_iota(jnp.int32, (8, length), 0)
    result = jnp.where(line == 0, target, jnp.where(line == 1, source, total))
    return result.astype(jnp.int32)


def task_length(group, local):
    return -(-(group * 3 * local + 3 * TOGETHER) // 128) * 128


def gather_kernel(owners, helpers, points, weights, lists, far_points, near_points, near_weights, tasks,
                  far_lists, send_sems, recv_sems):
    local = lists.shape[0]
    owner = lax.axis_index("owner")
    helper = lax.axis_index("helper")
    has_before = owner > 0
    has_after = owner < owners - 1
    barrier = pltpu.get_barrier_semaphore()
    for distance in range(1, helpers):
        pl.semaphore_signal(
            barrier, inc=1, device_id=(owner, partner_of(helper, distance)), device_id_type=MESH
        )

    @pl.when(has_before)
    def _():
        pl.semaphore_signal(barrier, inc=1, device_id=(owner - 1, helper), device_id_type=MESH)

    @pl.when(has_after)
    def _():
        pl.semaphore_signal(barrier, inc=1, device_id=(owner + 1, helper), device_id_type=MESH)

    neighbours = lax.min(owner, 1) + lax.min(owners - 1 - owner, 1)
    pl.semaphore_wait(barrier, helpers - 1 + neighbours)

    def copy(number, src, dst, device):
        return pltpu.make_async_remote_copy(
            src_ref=src,
            dst_ref=dst,
            send_sem=send_sems.at[number],
            recv_sem=recv_sems.at[number],
            device_id=device,
            device_id_type=MESH,
        )

    def beside(distance):
        return (owner, partner_of(helper, distance))

    number = 0
    list_copies = []
    for distance in range(1, helpers):
        list_copies.append(copy(number, lists, far_lists.at[distance - 1], beside(distance)))
        number += 1
    sent, relayed = [], []
    if helpers == 4 and local % 2 == 0:
        half = local // 2
        parts = (pl.ds(0, half), pl.ds(half, half))
        for order in (0, 1):
            for distance in (1, 2):
                part = parts[order if distance == 1 else 1 - order]
                one = copy(number, points.at[part], far_points.at[distance - 1, part], beside(distance))
                number += 1
                sent.append(one)
        for distance in (1, 2):
            part = parts[distance - 1]
            block = far_points.at[distance - 1, part]
            one = copy(number, block, far_points.at[2, part], beside(3 - distance))
            number += 1
            relayed.append(one)
    else:
        for distance in range(1, helpers):
            sent.append(copy(number, points, far_points.at[distance - 1], beside(distance)))
            number += 1
    up = [
        copy(number, points, near_points.at[0], (owner + 1, helper)),
        copy(number + 1, weights, near_weights.at[0], (owner + 1, helper)),
    ]
    down = [
        copy(number + 2, points, near_points.at[1], (owner - 1, helper)),
        copy(number + 3, weights, near_weights.at[1], (owner - 1, helper)),
    ]
    for one in list_copies + sent:
        one.start()

    @pl.when(has_after)
    def _():
        for one in up:
            one.start()

    @pl.when(has_before)
    def _():
        for one in down:
            one.start()

    for place, one in enumerate(relayed):
        sent[place].wait_recv()
        one.start()
    for one in list_copies:
        one.wait_recv()
    whole = jnp.concatenate([lists[...]] + [far_lists[i] for i in range(helpers - 1)], axis=0)
    tasks[...] = list_tasks((owner - 1) * local * helpers, helper, local, whole)
    for one in sent[len(relayed):] + relayed:
        one.wait_recv()
    for one in list_copies + sent + relayed:
        one.wait_send()

    @pl.when(has_after)
    def _():
        for one in up:
            one.wait_send()
        for one in down:
            one.wait_recv()

    @pl.when(has_before)
    def _():
        for one in down:
            one.wait_send()
        for one in up:
            one.wait_recv()


def gather_window(owners, helpers, points, weights, lists):
    local = points.shape[0]
    copies = 2 * (helpers - 1) + 10
    vmem = pl.BlockSpec(memory_space=pltpu.VMEM)
    any_space = pl.BlockSpec(memory_space=pl.ANY)
    return pl.pallas_call(
        functools.partial(gather_kernel, owners, helpers),
        out_shape=(
            jax.ShapeDtypeStruct((helpers - 1,) + points.shape, points.dtype),
            jax.ShapeDtypeStruct((2,) + points.shape, points.dtype),
            jax.ShapeDtypeStruct((2,) + weights.shape, weights.dtype),
            jax.ShapeDtypeStruct((8, task_length(local * helpers, local)), jnp.int32),
        ),
        in_specs=[any_space, any_space, vmem],
        out_specs=(any_space, any_space, any_space, vmem),
        scratch_shapes=[
            pltpu.VMEM((helpers - 1,) + lists.shape, lists.dtype),
            pltpu.SemaphoreType.DMA((copies,)),
            pltpu.SemaphoreType.DMA((copies,)),
        ],
        compiler_params=pltpu.CompilerParams(collective_id=0, has_side_effects=True),
        name="gather_window",
    )(points, weights, lists)


def pieces_of(value, count):
    parts = []
    for _ in range(count):
        part = value.astype(jnp.bfloat16).astype(jnp.float32)
        parts.append(part)
        value = value - part
    return parts


def extra_rows(first, second, rows, width):
    row = lax.broadcasted_iota(jnp.int32, (rows, width), 0)
    result = jnp.zeros((rows, width), jnp.float32)
    for i, value in enumerate(list(first) + list(second)):
        result = jnp.where(row == i, value, result)
    return result


def pairs_kernel(local, helpers, tasks, points, weights, far_points, near_points, near_weights,
                 own_sums, far_sums, out, targets, sources, held_weights, exponents, kernels):
    dims, width = points.shape[1:]
    group = local * helpers
    depth = targets.shape[1]
    ones = [jnp.ones((1, width), jnp.float32)] * 3

    def half_norm(value):
        return pieces_of(-0.5 * jnp.sum(value * value, axis=0, keepdims=True), 3)

    def prepare_target(index, block):
        targets[index, pl.ds(0, dims), :] = block
        targets[index, pl.ds(dims, depth - dims), :] = extra_rows(
            ones, half_norm(block.astype(jnp.float32)), depth - dims, width
        ).astype(jnp.bfloat16)

    def prepare_source(index, block):
        value = block.astype(jnp.float32)
        rows = [value, extra_rows(half_norm(value), ones, depth - dims, width)]
        sources[index] = jnp.concatenate(rows, axis=0).T.astype(jnp.bfloat16)

    def each_leaf(leaf, carry):
        prepare_target(leaf, points[leaf])
        prepare_source(local + leaf, points[leaf])
        prepare_source(leaf, near_points[0, leaf])
        prepare_source(2 * local + leaf, near_points[1, leaf])
        held_weights[leaf] = near_weights[0, leaf]
        held_weights[local + leaf] = weights[leaf]
        held_weights[2 * local + leaf] = near_weights[1, leaf]
        return carry

    for leaf in range(local):
        each_leaf(leaf, 0)

    def each_far(distance, carry):
        for leaf in range(local):
            prepare_target((distance + 1) * local + leaf, far_points[distance, leaf])
        return carry

    lax.fori_loop(0, helpers - 1, each_far, 0)

    total = tasks[2, 0]
    out[...] = jnp.zeros(out.shape, jnp.float32)

    def add_products(step):
        for part in range(TOGETHER):
            number = step * TOGETHER + part
            source, target = tasks[1, number], tasks[0, number]
            out[target] += jnp.dot(held_weights[source], kernels[part], preferred_element_type=jnp.float32)

    def take_exponentials():
        for part in range(TOGETHER):
            kernels[part] = jnp.exp(exponents[part]).astype(jnp.bfloat16)

    def find_exponents(step):
        for part in range(TOGETHER):
            number = step * TOGETHER + part
            source, target = tasks[1, number], tasks[0, number]
            exponents[part] = jnp.dot(sources[source], targets[target], preferred_element_type=jnp.float32)

    find_exponents(0)
    take_exponentials()
    find_exponents(1)

    def each_step(step, carry):
        add_products(step)
        take_exponentials()
        find_exponents(step + 2)
        return carry

    steps = lax.div(total + TOGETHER - 1, TOGETHER)
    lax.fori_loop(0, steps - 1, each_step, 0)

    @pl.when(total > 0)
    def _():
        add_products(steps - 1)

    own_sums[...] = out[pl.ds(0, local)]
    far_sums[...] = out[pl.ds(local, group - local)].astype(jnp.bfloat16).reshape(far_sums.shape)


def sum_pairs(helpers, points, weights, far_points, near_points, near_weights, tasks):
    local, dims, width = points.shape
    vectors = weights.shape[1]
    group = local * helpers
    vmem = pl.BlockSpec(memory_space=pltpu.VMEM)
    smem = pl.BlockSpec(memory_space=pltpu.SMEM)
    return pl.pallas_call(
        functools.partial(pairs_kernel, local, helpers),
        out_shape=(
            jax.ShapeDtypeStruct((local, vectors, width), jnp.float32),
            jax.ShapeDtypeStruct((helpers - 1, local, vectors, width), jnp.bfloat16),
        ),
        in_specs=[smem] + [vmem] * 5,
        out_specs=(vmem, vmem),
        scratch_shapes=[
            pltpu.VMEM((group + 1, vectors, width), jnp.float32),
            pltpu.VMEM((group + 1, dims + EXTRA, width), jnp.bfloat16),
            pltpu.VMEM((3 * local, width, dims + EXTRA), jnp.bfloat16),
            pltpu.VMEM((3 * local, vectors, width), jnp.bfloat16),
            pltpu.VMEM((TOGETHER, width, width), jnp.float32),
            pltpu.VMEM((TOGETHER, width, width), jnp.bfloat16),
        ],
        name="sum_pairs",
    )(tasks, points, weights, far_points, near_points, near_weights)


def return_kernel(helpers, far_sums, landed, send_sems, recv_sems):
    owner = lax.axis_index("owner")
    helper = lax.axis_index("helper")
    barrier = pltpu.get_barrier_semaphore()
    for distance in range(1, helpers):
        pl.semaphore_signal(
            barrier, inc=1, device_id=(owner, partner_of(helper, distance)), device_id_type=MESH
        )
    pl.semaphore_wait(barrier, helpers - 1)
    copies = []
    for distance in range(1, helpers):
        one = pltpu.make_async_remote_copy(
            src_ref=far_sums.at[distance - 1],
            dst_ref=landed.at[distance - 1],
            send_sem=send_sems.at[distance - 1],
            recv_sem=recv_sems.at[distance - 1],
            device_id=(owner, partner_of(helper, distance)),
            device_id_type=MESH,
        )
        copies.append(one)
    for one in reversed(copies):
        one.start()
    for one in copies:
        one.wait()


def return_sums(helpers, far_sums):
    any_space = pl.BlockSpec(memory_space=pl.ANY)
    return pl.pallas_call(
        functools.partial(return_kernel, helpers),
        out_shape=jax.ShapeDtypeStruct(far_sums.shape, far_sums.dtype),
        in_specs=[any_space],
        out_specs=any_space,
        scratch_shapes=[pltpu.SemaphoreType.DMA((helpers - 1,)), pltpu.SemaphoreType.DMA((helpers - 1,))],
        compiler_params=pltpu.CompilerParams(collective_id=1, has_side_effects=True),
        name="return_sums",
    )(far_sums)


ALONE, FIRST, SECOND, THIRD = 4, 4, 12, 8


def slot_count(local):
    return local + FIRST + SECOND + THIRD


def phase_of(target, source, local):
    half = local // 2
    own = target < local
    early = own | ((target >= local) & (target < local + half)) | ((target >= 2 * local + half) & (target < 3 * local))
    phase = jnp.where(target < 3 * local, 2, 3)
    phase = jnp.where(early, 1, phase)
    return jnp.where(own & (source < 2 * local), 0, phase)


def order_tasks(bases, local, lists):
    group, slots = lists.shape
    count = 3 * local
    length = task_length(group, local)
    lists = jnp.where(lists < 0, -(1 << 20), lists)
    row = lax.broadcasted_iota(jnp.int32, (group, 128), 0)
    column = lax.broadcasted_iota(jnp.int32, (group, 128), 1)
    table = jnp.zeros((group, 128), jnp.float32)
    for source in range(count):
        leaf = bases[source // local] + source % local
        one = jnp.max(jnp.where(lists == leaf, 1.0, 0.0), axis=1, keepdims=True)
        table = jnp.where(column == source, one, table)
    table = jnp.where((row == column) & (row < local), 0.0, table)
    phase = phase_of(row, column, local)
    phased = jnp.concatenate([jnp.where(phase == p, table, 0.0) for p in range(4)], axis=0)
    rows = 4 * group
    counted = phased.astype(jnp.bfloat16)
    above = lax.broadcasted_iota(jnp.int32, (rows, rows), 0) > lax.broadcasted_iota(jnp.int32, (rows, rows), 1)
    left = lax.broadcasted_iota(jnp.int32, (128, 128), 0) < lax.broadcasted_iota(jnp.int32, (128, 128), 1)
    inside = jnp.dot(counted, jnp.where(left, 1.0, 0.0).astype(jnp.bfloat16), preferred_element_type=jnp.float32)
    before = jnp.dot(jnp.where(above, 1.0, 0.0).astype(jnp.bfloat16), counted, preferred_element_type=jnp.float32)
    rank = inside + jnp.sum(before, axis=1, keepdims=True)
    rank = jnp.where(phased > 0.5, rank + 1.0, 0.0)
    rank = sum(rank[p * group:(p + 1) * group] for p in range(4)) - 1.0
    in_row = jnp.sum(phased, axis=1, keepdims=True)
    ends = [jnp.sum(in_row[:(p + 1) * group], axis=0, keepdims=True) for p in range(4)]
    place = lax.broadcasted_iota(jnp.int32, (group, length), 1).astype(jnp.float32)
    code_row = lax.broadcasted_iota(jnp.int32, (group, length), 0).astype(jnp.float32) * 256.0
    codes = jnp.zeros((group, length), jnp.float32)
    for source in range(count):
        codes = jnp.where(place == rank[:, source:source + 1], code_row + float(source), codes)
    codes = jnp.sum(codes, axis=0, keepdims=True)
    codes = jnp.where(place[:1] < ends[3], codes, float(group * 256)).astype(jnp.int32)
    line = lax.broadcasted_iota(jnp.int32, (8, length), 0)
    result = jnp.where(line == 0, codes // 256, codes % 256)
    for p in range(4):
        result = jnp.where(line == 2 + p, ends[p].astype(jnp.int32), result)
    return result


def within(value, last):
    return lax.max(lax.min(value, last), 0)


def slot_starts(tasks):
    second = lax.min(tasks[2, 0], FIRST)
    third = lax.min(tasks[3, 0], second + SECOND)
    rest = lax.min(tasks[4, 0], third + THIRD)
    return 0, second, third, rest


def slot_task(tasks, group, start, end, slot):
    number = within(start + slot, tasks.shape[1] - 1)
    inside = number < end
    target = jnp.where(inside, tasks[0, number], group)
    return within(tasks[1, number], 3 * group // 4 - 1), within(target, group)


def window_kernel(owners, points, weights, lists, sources, targets, held_weights, tasks, results,
                  own_points, own_weights, lists_here, far_lists, far_points, near_points, near_weights,
                  kernels, task_scalars, send_sems, recv_sems, local_sems):
    local, dims, width = points.shape
    helpers = 4
    group = local * helpers
    half = local // 2
    depth = targets.shape[1]
    owner = lax.axis_index("owner")
    helper = lax.axis_index("helper")
    odd = lax.rem(owner, 2)
    chip_owner = owner + 1 - 2 * odd
    next_owner = owner - 1 + 2 * odd
    has_next = (next_owner >= 0) & (next_owner < owners)

    fetches = [
        pltpu.make_async_copy(src, dst, local_sems.at[i])
        for i, (src, dst) in enumerate(
            ((points, own_points), (weights, own_weights), (lists, lists_here))
        )
    ]
    for one in fetches:
        one.start()

    def beside(distance):
        return (owner, partner_of(helper, distance))

    barrier = pltpu.get_barrier_semaphore()
    for device in [beside(1), beside(2), beside(3), (chip_owner, helper)]:
        pl.semaphore_signal(barrier, inc=1, device_id=device, device_id_type=MESH)

    @pl.when(has_next)
    def _():
        pl.semaphore_signal(barrier, inc=1, device_id=(next_owner, helper), device_id_type=MESH)

    pl.semaphore_wait(barrier, helpers + jnp.where(has_next, 1, 0))

    def copy(number, src, dst, device):
        return pltpu.make_async_remote_copy(
            src_ref=src,
            dst_ref=dst,
            send_sem=send_sems.at[number],
            recv_sem=recv_sems.at[number],
            device_id=device,
            device_id_type=MESH,
        )

    parts = (pl.ds(0, half), pl.ds(half, half))
    list_copies = [copy(d - 1, lists, far_lists.at[d - 1], beside(d)) for d in (1, 2, 3)]
    sent = []
    for order in (0, 1):
        for distance in (1, 2):
            part = parts[order if distance == 1 else 1 - order]
            sent.append(
                copy(3 + len(sent), points.at[part], far_points.at[distance - 1, part], beside(distance))
            )
    relayed = []
    for distance in (1, 2):
        part = parts[distance - 1]
        relayed.append(
            copy(6 + distance, far_points.at[distance - 1, part], far_points.at[2, part], beside(3 - distance))
        )
    chip = [
        copy(9, points, near_points.at[0], (chip_owner, helper)),
        copy(10, weights, near_weights.at[0], (chip_owner, helper)),
    ]
    beyond = [
        copy(11, points, near_points.at[1], (next_owner, helper)),
        copy(12, weights, near_weights.at[1], (next_owner, helper)),
    ]
    for one in list_copies + sent[:2] + chip:
        one.start()

    @pl.when(has_next)
    def _():
        for one in beyond:
            one.start()

    for one in sent[2:]:
        one.start()

    ones = [jnp.ones((1, width), jnp.float32)] * 3

    def half_norm(value):
        return pieces_of(-0.5 * jnp.sum(value * value, axis=0, keepdims=True), 3)

    def prepare_target(index, block):
        targets[index, pl.ds(0, dims), :] = block
        targets[index, pl.ds(dims, depth - dims), :] = extra_rows(
            ones, half_norm(block.astype(jnp.float32)), depth - dims, width
        ).astype(jnp.bfloat16)

    def prepare_source(index, block):
        value = block.astype(jnp.float32)
        rows = [value, extra_rows(half_norm(value), ones, depth - dims, width)]
        sources[index] = jnp.concatenate(rows, axis=0).T.astype(jnp.bfloat16)

    waiting = []

    def multiply():
        for source, slot, place in waiting:
            results[place] = jnp.dot(held_weights[source], kernels[slot], preferred_element_type=jnp.float32)
        waiting.clear()

    def work(pairs, base):
        side = base // ALONE % 2 * ALONE
        for i, (source, target) in enumerate(pairs):
            exponents = jnp.dot(sources[source], targets[target], preferred_element_type=jnp.float32)
            kernels[side + i] = jnp.exp(exponents).astype(jnp.bfloat16)
        multiply()
        waiting.extend((source, side + i, base + i) for i, (source, _) in enumerate(pairs))

    def work_slots(start, end, slots, base):
        for first in range(0, slots, ALONE):
            work([slot_task(task_scalars, group, start, end, first + i) for i in range(ALONE)], base + first)

    for one in fetches[:2]:
        one.wait()
    for leaf in range(local):
        prepare_target(leaf, own_points[leaf])
        prepare_source(leaf, own_points[leaf])
        held_weights[leaf] = own_weights[leaf]
    targets[group] = jnp.zeros(targets.shape[1:], jnp.bfloat16)
    work([(leaf, leaf) for leaf in range(local)], 0)

    fetches[2].wait()
    for one in list_copies:
        one.wait_recv()
    whole = jnp.concatenate([lists_here[...]] + [far_lists[i] for i in range(helpers - 1)], axis=0)
    bases = [o * group + helper * local for o in (owner, chip_owner, next_owner)]
    tasks[...] = order_tasks(bases, local, whole)
    to_scalars = pltpu.make_async_copy(tasks, task_scalars, local_sems.at[3])
    to_scalars.start()
    for one in chip:
        one.wait_recv()
    for leaf in range(local):
        prepare_source(local + leaf, near_points[0, leaf])
        held_weights[local + leaf] = near_weights[0, leaf]
    to_scalars.wait()
    starts = slot_starts(task_scalars)
    work_slots(starts[0], task_scalars[2, 0], FIRST, local)

    for place, one in enumerate(relayed):
        sent[place].wait_recv()
        one.start()
    for leaf in range(half):
        prepare_target(local + leaf, far_points[0, leaf])
        prepare_target(2 * local + half + leaf, far_points[1, half + leaf])

    @pl.when(has_next)
    def _():
        for one in beyond:
            one.wait_recv()
        for leaf in range(local):
            prepare_source(2 * local + leaf, near_points[1, leaf])
            held_weights[2 * local + leaf] = near_weights[1, leaf]

    work_slots(starts[1], task_scalars[3, 0], SECOND, local + FIRST)

    for one in sent[2:]:
        one.wait_recv()
    for leaf in range(half):
        prepare_target(local + half + leaf, far_points[0, half + leaf])
        prepare_target(2 * local + leaf, far_points[1, leaf])
    work_slots(starts[2], task_scalars[4, 0], THIRD, local + FIRST + SECOND)

    for one in relayed:
        one.wait_recv()
    for leaf in range(local):
        prepare_target(3 * local + leaf, far_points[2, leaf])
    multiply()
    for one in list_copies + sent + relayed + chip:
        one.wait_send()

    @pl.when(has_next)
    def _():
        for one in beyond:
            one.wait_send()


def gather_and_begin(owners, points, weights, lists):
    local, dims, width = points.shape
    vectors = weights.shape[1]
    group = 4 * local
    depth = dims + EXTRA
    vmem = pl.BlockSpec(memory_space=pltpu.VMEM)
    hbm = pl.BlockSpec(memory_space=pltpu.HBM)
    length = task_length(group, local)
    return pl.pallas_call(
        functools.partial(window_kernel, owners),
        out_shape=(
            pltpu.VMEM((3 * local, width, depth), jnp.bfloat16),
            pltpu.VMEM((group + 1, depth, width), jnp.bfloat16),
            pltpu.VMEM((3 * local, vectors, width), jnp.bfloat16),
            pltpu.VMEM((8, length), jnp.int32),
            pltpu.VMEM((slot_count(local), vectors, width), jnp.float32),
        ),
        in_specs=[hbm, hbm, hbm],
        out_specs=(vmem,) * 5,
        scratch_shapes=[
            pltpu.VMEM(points.shape, points.dtype),
            pltpu.VMEM(weights.shape, weights.dtype),
            pltpu.VMEM(lists.shape, lists.dtype),
            pltpu.VMEM((3,) + lists.shape, lists.dtype),
            pltpu.VMEM((3,) + points.shape, points.dtype),
            pltpu.VMEM((2,) + points.shape, points.dtype),
            pltpu.VMEM((2,) + weights.shape, weights.dtype),
            pltpu.VMEM((2 * ALONE, width, width), jnp.bfloat16),
            pltpu.SMEM((8, length), jnp.int32),
            pltpu.SemaphoreType.DMA((13,)),
            pltpu.SemaphoreType.DMA((13,)),
            pltpu.SemaphoreType.DMA((4,)),
        ],
        compiler_params=pltpu.CompilerParams(
            collective_id=2, has_side_effects=True, vmem_limit_bytes=VMEM_BYTES
        ),
        name="gather_and_begin",
    )(*(pltpu.with_memory_space_constraint(one, pltpu.HBM) for one in (points, weights, lists)))


def rest_kernel(local, *refs):
    width = refs[2].shape[2]
    vectors = refs[3].shape[1]
    half = width // 2
    accumulators = [
        pltpu.ACC(unit)((rows, half), jnp.float32)
        for rows in (half, half, vectors, vectors)
        for unit in (0, 1)
    ]
    pl.run_scoped(functools.partial(rest_body, local, *refs), *accumulators)


def rest_body(local, tasks, sources, targets, held_weights, results, own_sums, far_sums, out, kernels, *accumulators):
    width = targets.shape[2]
    half = width // 2
    group = 4 * local
    starts = slot_starts(tasks)
    first = starts[3]
    total = tasks[5, 0] - first
    units = (0, 1)
    exponents = (accumulators[0:2], accumulators[2:4])
    products = (accumulators[4:6], accumulators[6:8])

    def task(number):
        place = lax.max(number, 0) + first
        return tasks[1, place], tasks[0, place]

    def columns(unit):
        return pl.ds(unit * half, half)

    def widened(value, axis):
        missing = list(value.shape)
        missing[axis] = half - value.shape[axis]
        return jnp.concatenate([value, jnp.zeros(missing, value.dtype)], axis=axis)

    def stage_target(number):
        _, target = task(number)
        for unit in units:
            pltpu.matmul_push_rhs(widened(targets[target, :, columns(unit)], 0), 0, unit)

    def find_exponents(number, part):
        source, _ = task(number)
        for unit in units:
            pltpu.matmul_acc_lhs(
                exponents[part][unit],
                widened(sources[source, pl.ds(part * half, half), :], 1),
                0 if part == 0 else None,
            )

    def take_exponentials(part, slot):
        for unit in units:
            kernels[slot, pl.ds(part * half, half), columns(unit)] = jnp.exp(
                pltpu.matmul_pop(exponents[part][unit])
            ).astype(jnp.bfloat16)

    def stage_kernel(slot, part):
        for unit in units:
            pltpu.matmul_push_rhs(kernels[slot, pl.ds(part * half, half), columns(unit)], 1, unit)

    def multiply(number, part, side):
        source, _ = task(number)
        for unit in units:
            pltpu.matmul_acc_lhs(products[side][unit], held_weights[source, :, pl.ds(part * half, half)], 1)

    def add_product(number, side):
        _, target = task(number)
        for unit in units:
            out[target, :, columns(unit)] += pltpu.matmul_pop(products[side][unit])

    stage_target(0)
    for leaf in range(local):
        out[leaf] = results[leaf]
    out[pl.ds(local, group + 1 - local)] = jnp.zeros((group + 1 - local,) + out.shape[1:], jnp.float32)
    base = local
    for phase, slots in enumerate((FIRST, SECOND, THIRD)):
        for slot in range(slots):
            _, target = slot_task(tasks, group, starts[phase], tasks[2 + phase, 0], slot)
            out[target] += results[base + slot]
        base += slots

    def advance(number, slot, age):
        find_exponents(number, 0)
        if age >= 1:
            take_exponentials(1, (slot - 1) % TOGETHER)
        stage_target(number + 1)
        if age >= 2:
            stage_kernel((slot - 2) % TOGETHER, 0)
        find_exponents(number, 1)
        if age >= 2:
            multiply(number - 2, 0, slot % 2)
            stage_kernel((slot - 2) % TOGETHER, 1)
        take_exponentials(0, slot)
        if age >= 2:
            multiply(number - 2, 1, slot % 2)
        if age >= 3:
            add_product(number - 3, (slot - 1) % 2)

    for number in range(TOGETHER):
        advance(number, number, number)

    def each_step(step, carry):
        for part in range(TOGETHER):
            advance(step * TOGETHER + part, part, TOGETHER)
        return carry

    steps = lax.max(lax.div(total + TOGETHER - 1, TOGETHER), 1)
    lax.fori_loop(1, steps, each_step, 0)

    last = steps * TOGETHER
    find_exponents(last, 0)
    take_exponentials(1, TOGETHER - 1)
    for age in (2, 1):
        slot = TOGETHER - age
        stage_kernel(slot, 0)
        multiply(last - age, 0, slot % 2)
        stage_kernel(slot, 1)
        multiply(last - age, 1, slot % 2)
        add_product(last - age - 1, (slot - 1) % 2)
    add_product(last - 1, (TOGETHER - 1) % 2)
    for unit in units:
        kernels[0, pl.ds(0, half), columns(unit)] = pltpu.matmul_pop(exponents[0][unit]).astype(jnp.bfloat16)

    own_sums[...] = out[pl.ds(0, local)]
    far_sums[...] = out[pl.ds(local, group - local)].astype(jnp.bfloat16).reshape(far_sums.shape)


def sum_rest(local, sources, targets, held_weights, tasks, results):
    width = targets.shape[2]
    vectors = held_weights.shape[1]
    group = 4 * local
    vmem = pl.BlockSpec(memory_space=pltpu.VMEM)
    smem = pl.BlockSpec(memory_space=pltpu.SMEM)
    return pl.pallas_call(
        functools.partial(rest_kernel, local),
        out_shape=(
            pltpu.VMEM((local, vectors, width), jnp.float32),
            pltpu.VMEM((3, local, vectors, width), jnp.bfloat16),
        ),
        in_specs=[smem] + [vmem] * 4,
        out_specs=(vmem, vmem),
        scratch_shapes=[
            pltpu.VMEM((group + 1, vectors, width), jnp.float32),
            pltpu.VMEM((TOGETHER, width, width), jnp.bfloat16),
        ],
        compiler_params=pltpu.CompilerParams(vmem_limit_bytes=VMEM_BYTES),
        name="sum_rest",
    )(tasks, sources, targets, held_weights, results)


def return_in_vmem(far_sums):
    vmem = pl.BlockSpec(memory_space=pltpu.VMEM)
    return pl.pallas_call(
        functools.partial(return_kernel, 4),
        out_shape=pltpu.VMEM(far_sums.shape, far_sums.dtype),
        in_specs=[vmem],
        out_specs=vmem,
        scratch_shapes=[pltpu.SemaphoreType.DMA((3,)), pltpu.SemaphoreType.DMA((3,))],
        compiler_params=pltpu.CompilerParams(
            collective_id=3, has_side_effects=True, vmem_limit_bytes=VMEM_BYTES
        ),
        name="return_in_vmem",
    )(far_sums)


def on_device(points, weights, neighbours, counts):
    owners = lax.axis_size("owner")
    helpers = lax.axis_size("helper")
    local = points.shape[0]
    if helpers == 4 and local == ALONE and owners % 2 == 0:
        sources, targets, held_weights, tasks, results = gather_and_begin(owners, points, weights, neighbours)
        own_sums, far_sums = sum_rest(local, sources, targets, held_weights, tasks, results)
        landed = return_in_vmem(far_sums)
        return own_sums + (landed[0].astype(jnp.float32) + landed[1].astype(jnp.float32) + landed[2].astype(jnp.float32))
    far_points, near_points, near_weights, tasks = gather_window(owners, helpers, points, weights, neighbours)
    own_sums, far_sums = sum_pairs(helpers, points, weights, far_points, near_points, near_weights, tasks)
    landed = return_sums(helpers, far_sums)
    return own_sums + jnp.sum(landed.astype(jnp.float32), axis=0)


def solution(mesh):
    placed = (
        P(("owner", "helper"), None, None),
        P(("owner", "helper"), None, None),
        P(("owner", "helper"), None),
        P(("owner", "helper")),
    )
    return jax.shard_map(
        on_device,
        mesh=mesh,
        in_specs=placed,
        out_specs=P(("owner", "helper"), None, None),
        check_vma=False,
    )
```

```python
import functools

import jax
import jax.numpy as jnp
from jax import lax
from jax.experimental import pallas as pl
from jax.experimental.pallas import tpu as pltpu
from jax.sharding import PartitionSpec as P

MESH = pl.DeviceIdType.MESH
EXTRA = 16
TOGETHER = 4
VMEM_BYTES = 40 << 20


def partner_of(index, distance):
    result = index
    bit = 1
    while bit <= distance:
        if distance & bit:
            result = result + bit - 2 * bit * ((index // bit) % 2)
        bit *= 2
    return result


def list_tasks(base, helper, local, lists):
    group, slots = lists.shape
    count = 3 * local
    length = task_length(group, local)
    lists = jnp.where(lists < 0, -(1 << 20), lists)
    column = lax.broadcasted_iota(jnp.int32, (group, 128), 1)
    listed = []
    table = jnp.zeros((group, 128), jnp.float32)
    for source in range(count):
        leaf = base + (source // local) * group + helper * local + source % local
        one = jnp.max(jnp.where(lists == leaf, 1.0, 0.0), axis=1, keepdims=True)
        listed.append(one)
        table = jnp.where(column == source, one, table)
    below = lax.broadcasted_iota(jnp.int32, (group, group), 0) > lax.broadcasted_iota(jnp.int32, (group, group), 1)
    ahead = jnp.dot(
        jnp.where(below, 1.0, 0.0).astype(jnp.bfloat16), table.astype(jnp.bfloat16), preferred_element_type=jnp.float32
    )
    place = lax.broadcasted_iota(jnp.int32, (group, length), 1).astype(jnp.float32)
    row = lax.broadcasted_iota(jnp.int32, (group, length), 0).astype(jnp.float32)
    total = jnp.zeros((1, 1), jnp.float32)
    targets = jnp.zeros((group, length), jnp.float32)
    sources = jnp.zeros((group, length), jnp.float32)
    for source in range(count):
        here = jnp.where(listed[source] > 0.5, ahead[:, source:source + 1] + total, -1.0)
        targets = jnp.where(place == here, row, targets)
        sources = jnp.where(place == here, float(source), sources)
        total = total + jnp.sum(listed[source], axis=0, keepdims=True)
    target = jnp.where(place[:1] < total, jnp.sum(targets, axis=0, keepdims=True), float(group))
    source = jnp.sum(sources, axis=0, keepdims=True)
    line = lax.broadcasted_iota(jnp.int32, (8, length), 0)
    result = jnp.where(line == 0, target, jnp.where(line == 1, source, total))
    return result.astype(jnp.int32)


def task_length(group, local):
    return -(-(group * 3 * local + 3 * TOGETHER) // 128) * 128


def gather_kernel(owners, helpers, points, weights, lists, far_points, near_points, near_weights, tasks,
                  far_lists, send_sems, recv_sems):
    local = lists.shape[0]
    owner = lax.axis_index("owner")
    helper = lax.axis_index("helper")
    has_before = owner > 0
    has_after = owner < owners - 1
    barrier = pltpu.get_barrier_semaphore()
    for distance in range(1, helpers):
        pl.semaphore_signal(
            barrier, inc=1, device_id=(owner, partner_of(helper, distance)), device_id_type=MESH
        )

    @pl.when(has_before)
    def _():
        pl.semaphore_signal(barrier, inc=1, device_id=(owner - 1, helper), device_id_type=MESH)

    @pl.when(has_after)
    def _():
        pl.semaphore_signal(barrier, inc=1, device_id=(owner + 1, helper), device_id_type=MESH)

    neighbours = lax.min(owner, 1) + lax.min(owners - 1 - owner, 1)
    pl.semaphore_wait(barrier, helpers - 1 + neighbours)

    def copy(number, src, dst, device):
        return pltpu.make_async_remote_copy(
            src_ref=src,
            dst_ref=dst,
            send_sem=send_sems.at[number],
            recv_sem=recv_sems.at[number],
            device_id=device,
            device_id_type=MESH,
        )

    def beside(distance):
        return (owner, partner_of(helper, distance))

    number = 0
    list_copies = []
    for distance in range(1, helpers):
        list_copies.append(copy(number, lists, far_lists.at[distance - 1], beside(distance)))
        number += 1
    sent, relayed = [], []
    if helpers == 4 and local % 2 == 0:
        half = local // 2
        parts = (pl.ds(0, half), pl.ds(half, half))
        for order in (0, 1):
            for distance in (1, 2):
                part = parts[order if distance == 1 else 1 - order]
                one = copy(number, points.at[part], far_points.at[distance - 1, part], beside(distance))
                number += 1
                sent.append(one)
        for distance in (1, 2):
            part = parts[distance - 1]
            block = far_points.at[distance - 1, part]
            one = copy(number, block, far_points.at[2, part], beside(3 - distance))
            number += 1
            relayed.append(one)
    else:
        for distance in range(1, helpers):
            sent.append(copy(number, points, far_points.at[distance - 1], beside(distance)))
            number += 1
    up = [
        copy(number, points, near_points.at[0], (owner + 1, helper)),
        copy(number + 1, weights, near_weights.at[0], (owner + 1, helper)),
    ]
    down = [
        copy(number + 2, points, near_points.at[1], (owner - 1, helper)),
        copy(number + 3, weights, near_weights.at[1], (owner - 1, helper)),
    ]
    for one in list_copies + sent:
        one.start()

    @pl.when(has_after)
    def _():
        for one in up:
            one.start()

    @pl.when(has_before)
    def _():
        for one in down:
            one.start()

    for place, one in enumerate(relayed):
        sent[place].wait_recv()
        one.start()
    for one in list_copies:
        one.wait_recv()
    whole = jnp.concatenate([lists[...]] + [far_lists[i] for i in range(helpers - 1)], axis=0)
    tasks[...] = list_tasks((owner - 1) * local * helpers, helper, local, whole)
    for one in sent[len(relayed):] + relayed:
        one.wait_recv()
    for one in list_copies + sent + relayed:
        one.wait_send()

    @pl.when(has_after)
    def _():
        for one in up:
            one.wait_send()
        for one in down:
            one.wait_recv()

    @pl.when(has_before)
    def _():
        for one in down:
            one.wait_send()
        for one in up:
            one.wait_recv()


def gather_window(owners, helpers, points, weights, lists):
    local = points.shape[0]
    copies = 2 * (helpers - 1) + 10
    vmem = pl.BlockSpec(memory_space=pltpu.VMEM)
    any_space = pl.BlockSpec(memory_space=pl.ANY)
    return pl.pallas_call(
        functools.partial(gather_kernel, owners, helpers),
        out_shape=(
            jax.ShapeDtypeStruct((helpers - 1,) + points.shape, points.dtype),
            jax.ShapeDtypeStruct((2,) + points.shape, points.dtype),
            jax.ShapeDtypeStruct((2,) + weights.shape, weights.dtype),
            jax.ShapeDtypeStruct((8, task_length(local * helpers, local)), jnp.int32),
        ),
        in_specs=[any_space, any_space, vmem],
        out_specs=(any_space, any_space, any_space, vmem),
        scratch_shapes=[
            pltpu.VMEM((helpers - 1,) + lists.shape, lists.dtype),
            pltpu.SemaphoreType.DMA((copies,)),
            pltpu.SemaphoreType.DMA((copies,)),
        ],
        compiler_params=pltpu.CompilerParams(collective_id=0, has_side_effects=True),
        name="gather_window",
    )(points, weights, lists)


def pieces_of(value, count):
    parts = []
    for _ in range(count):
        part = value.astype(jnp.bfloat16).astype(jnp.float32)
        parts.append(part)
        value = value - part
    return parts


def extra_rows(first, second, rows, width):
    row = lax.broadcasted_iota(jnp.int32, (rows, width), 0)
    result = jnp.zeros((rows, width), jnp.float32)
    for i, value in enumerate(list(first) + list(second)):
        result = jnp.where(row == i, value, result)
    return result


def pairs_kernel(local, helpers, tasks, points, weights, far_points, near_points, near_weights,
                 own_sums, far_sums, out, targets, sources, held_weights, exponents, kernels):
    dims, width = points.shape[1:]
    group = local * helpers
    depth = targets.shape[1]
    ones = [jnp.ones((1, width), jnp.float32)] * 3

    def half_norm(value):
        return pieces_of(-0.5 * jnp.sum(value * value, axis=0, keepdims=True), 3)

    def prepare_target(index, block):
        targets[index, pl.ds(0, dims), :] = block
        targets[index, pl.ds(dims, depth - dims), :] = extra_rows(
            ones, half_norm(block.astype(jnp.float32)), depth - dims, width
        ).astype(jnp.bfloat16)

    def prepare_source(index, block):
        value = block.astype(jnp.float32)
        rows = [value, extra_rows(half_norm(value), ones, depth - dims, width)]
        sources[index] = jnp.concatenate(rows, axis=0).T.astype(jnp.bfloat16)

    def each_leaf(leaf, carry):
        prepare_target(leaf, points[leaf])
        prepare_source(local + leaf, points[leaf])
        prepare_source(leaf, near_points[0, leaf])
        prepare_source(2 * local + leaf, near_points[1, leaf])
        held_weights[leaf] = near_weights[0, leaf]
        held_weights[local + leaf] = weights[leaf]
        held_weights[2 * local + leaf] = near_weights[1, leaf]
        return carry

    for leaf in range(local):
        each_leaf(leaf, 0)

    def each_far(distance, carry):
        for leaf in range(local):
            prepare_target((distance + 1) * local + leaf, far_points[distance, leaf])
        return carry

    lax.fori_loop(0, helpers - 1, each_far, 0)

    total = tasks[2, 0]
    out[...] = jnp.zeros(out.shape, jnp.float32)

    def add_products(step):
        for part in range(TOGETHER):
            number = step * TOGETHER + part
            source, target = tasks[1, number], tasks[0, number]
            out[target] += jnp.dot(held_weights[source], kernels[part], preferred_element_type=jnp.float32)

    def take_exponentials():
        for part in range(TOGETHER):
            kernels[part] = jnp.exp(exponents[part]).astype(jnp.bfloat16)

    def find_exponents(step):
        for part in range(TOGETHER):
            number = step * TOGETHER + part
            source, target = tasks[1, number], tasks[0, number]
            exponents[part] = jnp.dot(sources[source], targets[target], preferred_element_type=jnp.float32)

    find_exponents(0)
    take_exponentials()
    find_exponents(1)

    def each_step(step, carry):
        add_products(step)
        take_exponentials()
        find_exponents(step + 2)
        return carry

    steps = lax.div(total + TOGETHER - 1, TOGETHER)
    lax.fori_loop(0, steps - 1, each_step, 0)

    @pl.when(total > 0)
    def _():
        add_products(steps - 1)

    own_sums[...] = out[pl.ds(0, local)]
    far_sums[...] = out[pl.ds(local, group - local)].astype(jnp.bfloat16).reshape(far_sums.shape)


def sum_pairs(helpers, points, weights, far_points, near_points, near_weights, tasks):
    local, dims, width = points.shape
    vectors = weights.shape[1]
    group = local * helpers
    vmem = pl.BlockSpec(memory_space=pltpu.VMEM)
    smem = pl.BlockSpec(memory_space=pltpu.SMEM)
    return pl.pallas_call(
        functools.partial(pairs_kernel, local, helpers),
        out_shape=(
            jax.ShapeDtypeStruct((local, vectors, width), jnp.float32),
            jax.ShapeDtypeStruct((helpers - 1, local, vectors, width), jnp.bfloat16),
        ),
        in_specs=[smem] + [vmem] * 5,
        out_specs=(vmem, vmem),
        scratch_shapes=[
            pltpu.VMEM((group + 1, vectors, width), jnp.float32),
            pltpu.VMEM((group + 1, dims + EXTRA, width), jnp.bfloat16),
            pltpu.VMEM((3 * local, width, dims + EXTRA), jnp.bfloat16),
            pltpu.VMEM((3 * local, vectors, width), jnp.bfloat16),
            pltpu.VMEM((TOGETHER, width, width), jnp.float32),
            pltpu.VMEM((TOGETHER, width, width), jnp.bfloat16),
        ],
        name="sum_pairs",
    )(tasks, points, weights, far_points, near_points, near_weights)


def return_kernel(helpers, far_sums, landed, send_sems, recv_sems):
    owner = lax.axis_index("owner")
    helper = lax.axis_index("helper")
    barrier = pltpu.get_barrier_semaphore()
    for distance in range(1, helpers):
        pl.semaphore_signal(
            barrier, inc=1, device_id=(owner, partner_of(helper, distance)), device_id_type=MESH
        )
    pl.semaphore_wait(barrier, helpers - 1)
    copies = []
    for distance in range(1, helpers):
        one = pltpu.make_async_remote_copy(
            src_ref=far_sums.at[distance - 1],
            dst_ref=landed.at[distance - 1],
            send_sem=send_sems.at[distance - 1],
            recv_sem=recv_sems.at[distance - 1],
            device_id=(owner, partner_of(helper, distance)),
            device_id_type=MESH,
        )
        copies.append(one)
    for one in reversed(copies):
        one.start()
    for one in copies:
        one.wait()


def return_sums(helpers, far_sums):
    any_space = pl.BlockSpec(memory_space=pl.ANY)
    return pl.pallas_call(
        functools.partial(return_kernel, helpers),
        out_shape=jax.ShapeDtypeStruct(far_sums.shape, far_sums.dtype),
        in_specs=[any_space],
        out_specs=any_space,
        scratch_shapes=[pltpu.SemaphoreType.DMA((helpers - 1,)), pltpu.SemaphoreType.DMA((helpers - 1,))],
        compiler_params=pltpu.CompilerParams(collective_id=1, has_side_effects=True),
        name="return_sums",
    )(far_sums)


ALONE, FIRST, SECOND, THIRD = 4, 8, 12, 8


def slot_count(local):
    return local + FIRST + SECOND + THIRD


def phase_of(target, source, local):
    half = local // 2
    quarter = half // 2
    first = (target < local) | ((target >= local) & (target < local + quarter))
    first = first | ((target >= 2 * local + half) & (target < 2 * local + half + quarter))
    early = first | ((target >= local) & (target < local + half)) | ((target >= 2 * local + half) & (target < 3 * local))
    phase = jnp.where(target < 3 * local, 2, 3)
    phase = jnp.where(early, 1, phase)
    return jnp.where(first & (source < 2 * local), 0, phase)


def order_tasks(bases, local, lists):
    group, slots = lists.shape
    count = 3 * local
    length = task_length(group, local)
    lists = jnp.where(lists < 0, -(1 << 20), lists)
    row = lax.broadcasted_iota(jnp.int32, (group, 128), 0)
    column = lax.broadcasted_iota(jnp.int32, (group, 128), 1)
    table = jnp.zeros((group, 128), jnp.float32)
    for source in range(count):
        leaf = bases[source // local] + source % local
        one = jnp.max(jnp.where(lists == leaf, 1.0, 0.0), axis=1, keepdims=True)
        table = jnp.where(column == source, one, table)
    table = jnp.where((row == column) & (row < local), 0.0, table)
    phase = phase_of(row, column, local)
    phased = jnp.concatenate([jnp.where(phase == p, table, 0.0) for p in range(4)], axis=0)
    rows = 4 * group
    counted = phased.astype(jnp.bfloat16)
    above = lax.broadcasted_iota(jnp.int32, (rows, rows), 0) > lax.broadcasted_iota(jnp.int32, (rows, rows), 1)
    left = lax.broadcasted_iota(jnp.int32, (128, 128), 0) < lax.broadcasted_iota(jnp.int32, (128, 128), 1)
    inside = jnp.dot(counted, jnp.where(left, 1.0, 0.0).astype(jnp.bfloat16), preferred_element_type=jnp.float32)
    before = jnp.dot(jnp.where(above, 1.0, 0.0).astype(jnp.bfloat16), counted, preferred_element_type=jnp.float32)
    rank = inside + jnp.sum(before, axis=1, keepdims=True)
    rank = jnp.where(phased > 0.5, rank + 1.0, 0.0)
    rank = sum(rank[p * group:(p + 1) * group] for p in range(4)) - 1.0
    in_row = jnp.sum(phased, axis=1, keepdims=True)
    ends = [jnp.sum(in_row[:(p + 1) * group], axis=0, keepdims=True) for p in range(4)]
    place = lax.broadcasted_iota(jnp.int32, (group, length), 1).astype(jnp.float32)
    code_row = lax.broadcasted_iota(jnp.int32, (group, length), 0).astype(jnp.float32) * 256.0
    codes = jnp.zeros((group, length), jnp.float32)
    for source in range(count):
        codes = jnp.where(place == rank[:, source:source + 1], code_row + float(source), codes)
    codes = jnp.sum(codes, axis=0, keepdims=True)
    codes = jnp.where(place[:1] < ends[3], codes, float(group * 256)).astype(jnp.int32)
    line = lax.broadcasted_iota(jnp.int32, (8, length), 0)
    result = jnp.where(line == 0, codes // 256, codes % 256)
    for p in range(4):
        result = jnp.where(line == 2 + p, ends[p].astype(jnp.int32), result)
    return result


def within(value, last):
    return lax.max(lax.min(value, last), 0)


def slot_starts(tasks):
    second = lax.min(tasks[2, 0], FIRST)
    third = lax.min(tasks[3, 0], second + SECOND)
    rest = lax.min(tasks[4, 0], third + THIRD)
    return 0, second, third, rest


def slot_task(tasks, group, start, end, slot):
    number = within(start + slot, tasks.shape[1] - 1)
    inside = number < end
    target = jnp.where(inside, tasks[0, number], group)
    return within(tasks[1, number], 3 * group // 4 - 1), within(target, group)


def window_kernel(owners, points, weights, lists, sources, targets, held_weights, task_scalars, results,
                  own_points, own_weights, lists_here, far_lists, far_points, near_points, near_weights,
                  kernels, tasks, send_sems, recv_sems, local_sems):
    local, dims, width = points.shape
    helpers = 4
    group = local * helpers
    half = local // 2
    depth = targets.shape[1]
    owner = lax.axis_index("owner")
    helper = lax.axis_index("helper")
    odd = lax.rem(owner, 2)
    chip_owner = owner + 1 - 2 * odd
    next_owner = owner - 1 + 2 * odd
    has_next = (next_owner >= 0) & (next_owner < owners)

    fetches = [
        pltpu.make_async_copy(src, dst, local_sems.at[i])
        for i, (src, dst) in enumerate(
            ((points, own_points), (weights, own_weights), (lists, lists_here))
        )
    ]
    for one in fetches:
        one.start()

    def beside(distance):
        return (owner, partner_of(helper, distance))

    barrier = pltpu.get_barrier_semaphore()
    for device in [beside(1), beside(2), beside(3), (chip_owner, helper)]:
        pl.semaphore_signal(barrier, inc=1, device_id=device, device_id_type=MESH)

    @pl.when(has_next)
    def _():
        pl.semaphore_signal(barrier, inc=1, device_id=(next_owner, helper), device_id_type=MESH)

    pl.semaphore_wait(barrier, helpers + jnp.where(has_next, 1, 0))

    def copy(number, src, dst, device):
        return pltpu.make_async_remote_copy(
            src_ref=src,
            dst_ref=dst,
            send_sem=send_sems.at[number],
            recv_sem=recv_sems.at[number],
            device_id=device,
            device_id_type=MESH,
        )

    list_copies = [copy(d - 1, lists, far_lists.at[d - 1], beside(d)) for d in (1, 2, 3)]
    quarter = half // 2
    sent = []
    for begin, size in ((0, quarter), (quarter, half - quarter), (half, half)):
        for distance in (1, 2):
            part = pl.ds((begin + half * (distance - 1)) % local, size)
            sent.append(
                copy(3 + len(sent), points.at[part], far_points.at[distance - 1, part], beside(distance))
            )
    relayed = []
    for distance in (1, 2):
        part = pl.ds(half * (distance - 1), half)
        relayed.append(
            copy(12 + distance, far_points.at[distance - 1, part], far_points.at[2, part], beside(3 - distance))
        )
    chip = [
        copy(9, points, near_points.at[0], (chip_owner, helper)),
        copy(10, weights, near_weights.at[0], (chip_owner, helper)),
    ]
    beyond = [
        copy(11, points, near_points.at[1], (next_owner, helper)),
        copy(12, weights, near_weights.at[1], (next_owner, helper)),
    ]
    for one in list_copies + sent[:2] + chip:
        one.start()

    @pl.when(has_next)
    def _():
        for one in beyond:
            one.start()

    for one in sent[2:]:
        one.start()

    ones = [jnp.ones((1, width), jnp.float32)] * 3

    def half_norm(value):
        return pieces_of(-0.5 * jnp.sum(value * value, axis=0, keepdims=True), 3)

    def prepare_target(index, block):
        targets[index, pl.ds(0, dims), :] = block
        targets[index, pl.ds(dims, depth - dims), :] = extra_rows(
            ones, half_norm(block.astype(jnp.float32)), depth - dims, width
        ).astype(jnp.bfloat16)

    def prepare_source(index, block):
        value = block.astype(jnp.float32)
        rows = [value, extra_rows(half_norm(value), ones, depth - dims, width)]
        sources[index] = jnp.concatenate(rows, axis=0).T.astype(jnp.bfloat16)

    waiting = []

    def multiply():
        for source, slot, place in waiting:
            results[place] = jnp.dot(held_weights[source], kernels[slot], preferred_element_type=jnp.float32)
        waiting.clear()

    def work(pairs, base):
        side = base // ALONE % 2 * ALONE
        for i, (source, target) in enumerate(pairs):
            exponents = jnp.dot(sources[source], targets[target], preferred_element_type=jnp.float32)
            kernels[side + i] = jnp.exp(exponents).astype(jnp.bfloat16)
        multiply()
        waiting.extend((source, side + i, base + i) for i, (source, _) in enumerate(pairs))

    def work_slots(start, end, slots, base):
        for first in range(0, slots, ALONE):
            work([slot_task(task_scalars, group, start, end, first + i) for i in range(ALONE)], base + first)

    for one in fetches[:2]:
        one.wait()
    for leaf in range(local):
        prepare_target(leaf, own_points[leaf])
        prepare_source(leaf, own_points[leaf])
        held_weights[leaf] = own_weights[leaf]
    targets[group] = jnp.zeros(targets.shape[1:], jnp.bfloat16)
    work([(leaf, leaf) for leaf in range(local)], 0)

    fetches[2].wait()
    for one in list_copies:
        one.wait_recv()
    whole = jnp.concatenate([lists_here[...]] + [far_lists[i] for i in range(helpers - 1)], axis=0)
    bases = [o * group + helper * local for o in (owner, chip_owner, next_owner)]
    tasks[...] = order_tasks(bases, local, whole)
    to_scalars = pltpu.make_async_copy(tasks, task_scalars, local_sems.at[3])
    to_scalars.start()
    for one in chip:
        one.wait_recv()
    for leaf in range(local):
        prepare_source(local + leaf, near_points[0, leaf])
        held_weights[local + leaf] = near_weights[0, leaf]
    to_scalars.wait()
    starts = slot_starts(task_scalars)
    for one in sent[:2]:
        one.wait_recv()
    for leaf in range(quarter):
        prepare_target(local + leaf, far_points[0, leaf])
        prepare_target(2 * local + half + leaf, far_points[1, half + leaf])
    work_slots(starts[0], task_scalars[2, 0], FIRST, local)

    for place, one in enumerate(relayed):
        sent[2 + place].wait_recv()
        one.start()
    for leaf in range(quarter, half):
        prepare_target(local + leaf, far_points[0, leaf])
        prepare_target(2 * local + half + leaf, far_points[1, half + leaf])

    @pl.when(has_next)
    def _():
        for one in beyond:
            one.wait_recv()
        for leaf in range(local):
            prepare_source(2 * local + leaf, near_points[1, leaf])
            held_weights[2 * local + leaf] = near_weights[1, leaf]

    work_slots(starts[1], task_scalars[3, 0], SECOND, local + FIRST)

    for one in sent[4:]:
        one.wait_recv()
    for leaf in range(half):
        prepare_target(local + half + leaf, far_points[0, half + leaf])
        prepare_target(2 * local + leaf, far_points[1, leaf])
    work_slots(starts[2], task_scalars[4, 0], THIRD, local + FIRST + SECOND)

    for one in relayed:
        one.wait_recv()
    for leaf in range(local):
        prepare_target(3 * local + leaf, far_points[2, leaf])
    multiply()
    for one in list_copies + sent + relayed + chip:
        one.wait_send()

    @pl.when(has_next)
    def _():
        for one in beyond:
            one.wait_send()


def gather_and_begin(owners, points, weights, lists):
    local, dims, width = points.shape
    vectors = weights.shape[1]
    group = 4 * local
    depth = dims + EXTRA
    vmem = pl.BlockSpec(memory_space=pltpu.VMEM)
    hbm = pl.BlockSpec(memory_space=pltpu.HBM)
    length = task_length(group, local)
    return pl.pallas_call(
        functools.partial(window_kernel, owners),
        out_shape=(
            pltpu.VMEM((3 * local, width, depth), jnp.bfloat16),
            pltpu.VMEM((group + 1, depth, width), jnp.bfloat16),
            pltpu.VMEM((3 * local, vectors, width), jnp.bfloat16),
            pltpu.SMEM((8, length), jnp.int32),
            pltpu.VMEM((slot_count(local), vectors, width), jnp.float32),
        ),
        in_specs=[hbm, hbm, hbm],
        out_specs=(vmem,) * 3 + (pl.BlockSpec(memory_space=pltpu.SMEM), vmem),
        scratch_shapes=[
            pltpu.VMEM(points.shape, points.dtype),
            pltpu.VMEM(weights.shape, weights.dtype),
            pltpu.VMEM(lists.shape, lists.dtype),
            pltpu.VMEM((3,) + lists.shape, lists.dtype),
            pltpu.VMEM((3,) + points.shape, points.dtype),
            pltpu.VMEM((2,) + points.shape, points.dtype),
            pltpu.VMEM((2,) + weights.shape, weights.dtype),
            pltpu.VMEM((2 * ALONE, width, width), jnp.bfloat16),
            pltpu.VMEM((8, length), jnp.int32),
            pltpu.SemaphoreType.DMA((15,)),
            pltpu.SemaphoreType.DMA((15,)),
            pltpu.SemaphoreType.DMA((4,)),
        ],
        compiler_params=pltpu.CompilerParams(
            collective_id=2, has_side_effects=True, vmem_limit_bytes=VMEM_BYTES
        ),
        name="gather_and_begin",
    )(*(pltpu.with_memory_space_constraint(one, pltpu.HBM) for one in (points, weights, lists)))


def rest_kernel(local, *refs):
    width = refs[2].shape[2]
    vectors = refs[3].shape[1]
    half = width // 2
    accumulators = [
        pltpu.ACC(unit)((rows, half), jnp.float32)
        for rows in (half, half, vectors, vectors)
        for unit in (0, 1)
    ]
    pl.run_scoped(functools.partial(rest_body, local, *refs), *accumulators)


def rest_body(local, tasks, sources, targets, held_weights, results, own_sums, far_sums, out, kernels, *accumulators):
    width = targets.shape[2]
    half = width // 2
    group = 4 * local
    starts = slot_starts(tasks)
    first = starts[3]
    total = tasks[5, 0] - first
    units = (0, 1)
    exponents = (accumulators[0:2], accumulators[2:4])
    products = (accumulators[4:6], accumulators[6:8])

    def task(number):
        place = lax.max(number, 0) + first
        return tasks[1, place], tasks[0, place]

    def columns(unit):
        return pl.ds(unit * half, half)

    def widened(value, axis):
        missing = list(value.shape)
        missing[axis] = half - value.shape[axis]
        return jnp.concatenate([value, jnp.zeros(missing, value.dtype)], axis=axis)

    def stage_target(number):
        _, target = task(number)
        for unit in units:
            pltpu.matmul_push_rhs(widened(targets[target, :, columns(unit)], 0), 0, unit)

    def find_exponents(number, part):
        source, _ = task(number)
        for unit in units:
            pltpu.matmul_acc_lhs(
                exponents[part][unit],
                widened(sources[source, pl.ds(part * half, half), :], 1),
                0 if part == 0 else None,
            )

    def take_exponentials(part, slot):
        for unit in units:
            kernels[slot, pl.ds(part * half, half), columns(unit)] = jnp.exp(
                pltpu.matmul_pop(exponents[part][unit])
            ).astype(jnp.bfloat16)

    def stage_kernel(slot, part):
        for unit in units:
            pltpu.matmul_push_rhs(kernels[slot, pl.ds(part * half, half), columns(unit)], 1, unit)

    def multiply(number, part, side):
        source, _ = task(number)
        for unit in units:
            pltpu.matmul_acc_lhs(products[side][unit], held_weights[source, :, pl.ds(part * half, half)], 1)

    def add_product(number, side):
        _, target = task(number)
        for unit in units:
            out[target, :, columns(unit)] += pltpu.matmul_pop(products[side][unit])

    stage_target(0)
    for leaf in range(local):
        out[leaf] = results[leaf]
    out[pl.ds(local, group + 1 - local)] = jnp.zeros((group + 1 - local,) + out.shape[1:], jnp.float32)
    base = local
    for phase, slots in enumerate((FIRST, SECOND, THIRD)):
        for slot in range(slots):
            _, target = slot_task(tasks, group, starts[phase], tasks[2 + phase, 0], slot)
            out[target] += results[base + slot]
        base += slots

    def advance(number, slot, age):
        find_exponents(number, 0)
        if age >= 1:
            take_exponentials(1, (slot - 1) % TOGETHER)
        stage_target(number + 1)
        if age >= 2:
            stage_kernel((slot - 2) % TOGETHER, 0)
        find_exponents(number, 1)
        if age >= 2:
            multiply(number - 2, 0, slot % 2)
            stage_kernel((slot - 2) % TOGETHER, 1)
        take_exponentials(0, slot)
        if age >= 2:
            multiply(number - 2, 1, slot % 2)
        if age >= 3:
            add_product(number - 3, (slot - 1) % 2)

    for number in range(TOGETHER):
        advance(number, number, number)

    def each_step(step, carry):
        for part in range(TOGETHER):
            advance(step * TOGETHER + part, part, TOGETHER)
        return carry

    steps = lax.max(lax.div(total + TOGETHER - 1, TOGETHER), 1)
    lax.fori_loop(1, steps, each_step, 0)

    last = steps * TOGETHER
    find_exponents(last, 0)
    take_exponentials(1, TOGETHER - 1)
    for age in (2, 1):
        slot = TOGETHER - age
        stage_kernel(slot, 0)
        multiply(last - age, 0, slot % 2)
        stage_kernel(slot, 1)
        multiply(last - age, 1, slot % 2)
        add_product(last - age - 1, (slot - 1) % 2)
    add_product(last - 1, (TOGETHER - 1) % 2)
    for unit in units:
        kernels[0, pl.ds(0, half), columns(unit)] = pltpu.matmul_pop(exponents[0][unit]).astype(jnp.bfloat16)

    own_sums[...] = out[pl.ds(0, local)]
    far_sums[...] = out[pl.ds(local, group - local)].astype(jnp.bfloat16).reshape(far_sums.shape)


def sum_rest(local, sources, targets, held_weights, tasks, results):
    width = targets.shape[2]
    vectors = held_weights.shape[1]
    group = 4 * local
    vmem = pl.BlockSpec(memory_space=pltpu.VMEM)
    smem = pl.BlockSpec(memory_space=pltpu.SMEM)
    return pl.pallas_call(
        functools.partial(rest_kernel, local),
        out_shape=(
            pltpu.VMEM((local, vectors, width), jnp.float32),
            pltpu.VMEM((3, local, vectors, width), jnp.bfloat16),
        ),
        in_specs=[smem] + [vmem] * 4,
        out_specs=(vmem, vmem),
        scratch_shapes=[
            pltpu.VMEM((group + 1, vectors, width), jnp.float32),
            pltpu.VMEM((TOGETHER, width, width), jnp.bfloat16),
        ],
        compiler_params=pltpu.CompilerParams(vmem_limit_bytes=VMEM_BYTES),
        name="sum_rest",
    )(tasks, sources, targets, held_weights, results)


def return_in_vmem(far_sums):
    vmem = pl.BlockSpec(memory_space=pltpu.VMEM)
    return pl.pallas_call(
        functools.partial(return_kernel, 4),
        out_shape=pltpu.VMEM(far_sums.shape, far_sums.dtype),
        in_specs=[vmem],
        out_specs=vmem,
        scratch_shapes=[pltpu.SemaphoreType.DMA((3,)), pltpu.SemaphoreType.DMA((3,))],
        compiler_params=pltpu.CompilerParams(
            collective_id=3, has_side_effects=True, vmem_limit_bytes=VMEM_BYTES
        ),
        name="return_in_vmem",
    )(far_sums)


def on_device(points, weights, neighbours, counts):
    owners = lax.axis_size("owner")
    helpers = lax.axis_size("helper")
    local = points.shape[0]
    if helpers == 4 and local == ALONE and owners % 2 == 0:
        sources, targets, held_weights, tasks, results = gather_and_begin(owners, points, weights, neighbours)
        own_sums, far_sums = sum_rest(local, sources, targets, held_weights, tasks, results)
        landed = return_in_vmem(far_sums)
        return own_sums + (landed[0].astype(jnp.float32) + landed[1].astype(jnp.float32) + landed[2].astype(jnp.float32))
    far_points, near_points, near_weights, tasks = gather_window(owners, helpers, points, weights, neighbours)
    own_sums, far_sums = sum_pairs(helpers, points, weights, far_points, near_points, near_weights, tasks)
    landed = return_sums(helpers, far_sums)
    return own_sums + jnp.sum(landed.astype(jnp.float32), axis=0)


def solution(mesh):
    placed = (
        P(("owner", "helper"), None, None),
        P(("owner", "helper"), None, None),
        P(("owner", "helper"), None),
        P(("owner", "helper")),
    )
    return jax.shard_map(
        on_device,
        mesh=mesh,
        in_specs=placed,
        out_specs=P(("owner", "helper"), None, None),
        check_vma=False,
    )
```

```python
import functools

import jax
import jax.numpy as jnp
from jax import lax
from jax.experimental import pallas as pl
from jax.experimental.pallas import tpu as pltpu
from jax.sharding import PartitionSpec as P

MESH = pl.DeviceIdType.MESH
EXTRA = 16
TOGETHER = 4
VMEM_BYTES = 40 << 20
RING = 2
KEPT = 8


def partner_of(index, distance):
    result = index
    bit = 1
    while bit <= distance:
        if distance & bit:
            result = result + bit - 2 * bit * ((index // bit) % 2)
        bit *= 2
    return result


def list_tasks(base, helper, local, lists):
    group, slots = lists.shape
    count = 3 * local
    length = task_length(group, local)
    lists = jnp.where(lists < 0, -(1 << 20), lists)
    column = lax.broadcasted_iota(jnp.int32, (group, 128), 1)
    listed = []
    table = jnp.zeros((group, 128), jnp.float32)
    for source in range(count):
        leaf = base + (source // local) * group + helper * local + source % local
        one = jnp.max(jnp.where(lists == leaf, 1.0, 0.0), axis=1, keepdims=True)
        listed.append(one)
        table = jnp.where(column == source, one, table)
    below = lax.broadcasted_iota(jnp.int32, (group, group), 0) > lax.broadcasted_iota(jnp.int32, (group, group), 1)
    ahead = jnp.dot(
        jnp.where(below, 1.0, 0.0).astype(jnp.bfloat16), table.astype(jnp.bfloat16), preferred_element_type=jnp.float32
    )
    place = lax.broadcasted_iota(jnp.int32, (group, length), 1).astype(jnp.float32)
    row = lax.broadcasted_iota(jnp.int32, (group, length), 0).astype(jnp.float32)
    total = jnp.zeros((1, 1), jnp.float32)
    targets = jnp.zeros((group, length), jnp.float32)
    sources = jnp.zeros((group, length), jnp.float32)
    for source in range(count):
        here = jnp.where(listed[source] > 0.5, ahead[:, source:source + 1] + total, -1.0)
        targets = jnp.where(place == here, row, targets)
        sources = jnp.where(place == here, float(source), sources)
        total = total + jnp.sum(listed[source], axis=0, keepdims=True)
    target = jnp.where(place[:1] < total, jnp.sum(targets, axis=0, keepdims=True), float(group))
    source = jnp.sum(sources, axis=0, keepdims=True)
    line = lax.broadcasted_iota(jnp.int32, (8, length), 0)
    result = jnp.where(line == 0, target, jnp.where(line == 1, source, total))
    return result.astype(jnp.int32)


def task_length(group, local):
    return -(-(group * 3 * local + 3 * TOGETHER) // 128) * 128


def gather_kernel(owners, helpers, points, weights, lists, far_points, near_points, near_weights, tasks,
                  far_lists, send_sems, recv_sems):
    local = lists.shape[0]
    owner = lax.axis_index("owner")
    helper = lax.axis_index("helper")
    has_before = owner > 0
    has_after = owner < owners - 1
    barrier = pltpu.get_barrier_semaphore()
    for distance in range(1, helpers):
        pl.semaphore_signal(
            barrier, inc=1, device_id=(owner, partner_of(helper, distance)), device_id_type=MESH
        )

    @pl.when(has_before)
    def _():
        pl.semaphore_signal(barrier, inc=1, device_id=(owner - 1, helper), device_id_type=MESH)

    @pl.when(has_after)
    def _():
        pl.semaphore_signal(barrier, inc=1, device_id=(owner + 1, helper), device_id_type=MESH)

    neighbours = lax.min(owner, 1) + lax.min(owners - 1 - owner, 1)
    pl.semaphore_wait(barrier, helpers - 1 + neighbours)

    def copy(number, src, dst, device):
        return pltpu.make_async_remote_copy(
            src_ref=src,
            dst_ref=dst,
            send_sem=send_sems.at[number],
            recv_sem=recv_sems.at[number],
            device_id=device,
            device_id_type=MESH,
        )

    def beside(distance):
        return (owner, partner_of(helper, distance))

    number = 0
    list_copies = []
    for distance in range(1, helpers):
        list_copies.append(copy(number, lists, far_lists.at[distance - 1], beside(distance)))
        number += 1
    sent, relayed = [], []
    if helpers == 4 and local % 2 == 0:
        half = local // 2
        parts = (pl.ds(0, half), pl.ds(half, half))
        for order in (0, 1):
            for distance in (1, 2):
                part = parts[order if distance == 1 else 1 - order]
                one = copy(number, points.at[part], far_points.at[distance - 1, part], beside(distance))
                number += 1
                sent.append(one)
        for distance in (1, 2):
            part = parts[distance - 1]
            block = far_points.at[distance - 1, part]
            one = copy(number, block, far_points.at[2, part], beside(3 - distance))
            number += 1
            relayed.append(one)
    else:
        for distance in range(1, helpers):
            sent.append(copy(number, points, far_points.at[distance - 1], beside(distance)))
            number += 1
    up = [
        copy(number, points, near_points.at[0], (owner + 1, helper)),
        copy(number + 1, weights, near_weights.at[0], (owner + 1, helper)),
    ]
    down = [
        copy(number + 2, points, near_points.at[1], (owner - 1, helper)),
        copy(number + 3, weights, near_weights.at[1], (owner - 1, helper)),
    ]
    for one in list_copies + sent:
        one.start()

    @pl.when(has_after)
    def _():
        for one in up:
            one.start()

    @pl.when(has_before)
    def _():
        for one in down:
            one.start()

    for place, one in enumerate(relayed):
        sent[place].wait_recv()
        one.start()
    for one in list_copies:
        one.wait_recv()
    whole = jnp.concatenate([lists[...]] + [far_lists[i] for i in range(helpers - 1)], axis=0)
    tasks[...] = list_tasks((owner - 1) * local * helpers, helper, local, whole)
    for one in sent[len(relayed):] + relayed:
        one.wait_recv()
    for one in list_copies + sent + relayed:
        one.wait_send()

    @pl.when(has_after)
    def _():
        for one in up:
            one.wait_send()
        for one in down:
            one.wait_recv()

    @pl.when(has_before)
    def _():
        for one in down:
            one.wait_send()
        for one in up:
            one.wait_recv()


def gather_window(owners, helpers, points, weights, lists):
    local = points.shape[0]
    copies = 2 * (helpers - 1) + 10
    vmem = pl.BlockSpec(memory_space=pltpu.VMEM)
    any_space = pl.BlockSpec(memory_space=pl.ANY)
    return pl.pallas_call(
        functools.partial(gather_kernel, owners, helpers),
        out_shape=(
            jax.ShapeDtypeStruct((helpers - 1,) + points.shape, points.dtype),
            jax.ShapeDtypeStruct((2,) + points.shape, points.dtype),
            jax.ShapeDtypeStruct((2,) + weights.shape, weights.dtype),
            jax.ShapeDtypeStruct((8, task_length(local * helpers, local)), jnp.int32),
        ),
        in_specs=[any_space, any_space, vmem],
        out_specs=(any_space, any_space, any_space, vmem),
        scratch_shapes=[
            pltpu.VMEM((helpers - 1,) + lists.shape, lists.dtype),
            pltpu.SemaphoreType.DMA((copies,)),
            pltpu.SemaphoreType.DMA((copies,)),
        ],
        compiler_params=pltpu.CompilerParams(collective_id=0, has_side_effects=True),
        name="gather_window",
    )(points, weights, lists)


def pieces_of(value, count):
    parts = []
    for _ in range(count):
        part = value.astype(jnp.bfloat16).astype(jnp.float32)
        parts.append(part)
        value = value - part
    return parts


def extra_rows(first, second, rows, width):
    row = lax.broadcasted_iota(jnp.int32, (rows, width), 0)
    result = jnp.zeros((rows, width), jnp.float32)
    for i, value in enumerate(list(first) + list(second)):
        result = jnp.where(row == i, value, result)
    return result


def pairs_kernel(local, helpers, tasks, points, weights, far_points, near_points, near_weights,
                 own_sums, far_sums, out, targets, sources, held_weights, exponents, kernels):
    dims, width = points.shape[1:]
    group = local * helpers
    depth = targets.shape[1]
    ones = [jnp.ones((1, width), jnp.float32)] * 3

    def half_norm(value):
        return pieces_of(-0.5 * jnp.sum(value * value, axis=0, keepdims=True), 3)

    def prepare_target(index, block):
        targets[index, pl.ds(0, dims), :] = block
        targets[index, pl.ds(dims, depth - dims), :] = extra_rows(
            ones, half_norm(block.astype(jnp.float32)), depth - dims, width
        ).astype(jnp.bfloat16)

    def prepare_source(index, block):
        value = block.astype(jnp.float32)
        rows = [value, extra_rows(half_norm(value), ones, depth - dims, width)]
        sources[index] = jnp.concatenate(rows, axis=0).T.astype(jnp.bfloat16)

    def each_leaf(leaf, carry):
        prepare_target(leaf, points[leaf])
        prepare_source(local + leaf, points[leaf])
        prepare_source(leaf, near_points[0, leaf])
        prepare_source(2 * local + leaf, near_points[1, leaf])
        held_weights[leaf] = near_weights[0, leaf]
        held_weights[local + leaf] = weights[leaf]
        held_weights[2 * local + leaf] = near_weights[1, leaf]
        return carry

    for leaf in range(local):
        each_leaf(leaf, 0)

    def each_far(distance, carry):
        for leaf in range(local):
            prepare_target((distance + 1) * local + leaf, far_points[distance, leaf])
        return carry

    lax.fori_loop(0, helpers - 1, each_far, 0)

    total = tasks[2, 0]
    out[...] = jnp.zeros(out.shape, jnp.float32)

    def add_products(step):
        for part in range(TOGETHER):
            number = step * TOGETHER + part
            source, target = tasks[1, number], tasks[0, number]
            out[target] += jnp.dot(held_weights[source], kernels[part], preferred_element_type=jnp.float32)

    def take_exponentials():
        for part in range(TOGETHER):
            kernels[part] = jnp.exp(exponents[part]).astype(jnp.bfloat16)

    def find_exponents(step):
        for part in range(TOGETHER):
            number = step * TOGETHER + part
            source, target = tasks[1, number], tasks[0, number]
            exponents[part] = jnp.dot(sources[source], targets[target], preferred_element_type=jnp.float32)

    find_exponents(0)
    take_exponentials()
    find_exponents(1)

    def each_step(step, carry):
        add_products(step)
        take_exponentials()
        find_exponents(step + 2)
        return carry

    steps = lax.div(total + TOGETHER - 1, TOGETHER)
    lax.fori_loop(0, steps - 1, each_step, 0)

    @pl.when(total > 0)
    def _():
        add_products(steps - 1)

    own_sums[...] = out[pl.ds(0, local)]
    far_sums[...] = out[pl.ds(local, group - local)].astype(jnp.bfloat16).reshape(far_sums.shape)


def sum_pairs(helpers, points, weights, far_points, near_points, near_weights, tasks):
    local, dims, width = points.shape
    vectors = weights.shape[1]
    group = local * helpers
    vmem = pl.BlockSpec(memory_space=pltpu.VMEM)
    smem = pl.BlockSpec(memory_space=pltpu.SMEM)
    return pl.pallas_call(
        functools.partial(pairs_kernel, local, helpers),
        out_shape=(
            jax.ShapeDtypeStruct((local, vectors, width), jnp.float32),
            jax.ShapeDtypeStruct((helpers - 1, local, vectors, width), jnp.bfloat16),
        ),
        in_specs=[smem] + [vmem] * 5,
        out_specs=(vmem, vmem),
        scratch_shapes=[
            pltpu.VMEM((group + 1, vectors, width), jnp.float32),
            pltpu.VMEM((group + 1, dims + EXTRA, width), jnp.bfloat16),
            pltpu.VMEM((3 * local, width, dims + EXTRA), jnp.bfloat16),
            pltpu.VMEM((3 * local, vectors, width), jnp.bfloat16),
            pltpu.VMEM((TOGETHER, width, width), jnp.float32),
            pltpu.VMEM((TOGETHER, width, width), jnp.bfloat16),
        ],
        name="sum_pairs",
    )(tasks, points, weights, far_points, near_points, near_weights)


def return_kernel(helpers, far_sums, landed, send_sems, recv_sems):
    owner = lax.axis_index("owner")
    helper = lax.axis_index("helper")
    barrier = pltpu.get_barrier_semaphore()
    for distance in range(1, helpers):
        pl.semaphore_signal(
            barrier, inc=1, device_id=(owner, partner_of(helper, distance)), device_id_type=MESH
        )
    pl.semaphore_wait(barrier, helpers - 1)
    copies = []
    for distance in range(1, helpers):
        one = pltpu.make_async_remote_copy(
            src_ref=far_sums.at[distance - 1],
            dst_ref=landed.at[distance - 1],
            send_sem=send_sems.at[distance - 1],
            recv_sem=recv_sems.at[distance - 1],
            device_id=(owner, partner_of(helper, distance)),
            device_id_type=MESH,
        )
        copies.append(one)
    for one in reversed(copies):
        one.start()
    for one in copies:
        one.wait()


def return_sums(helpers, far_sums):
    any_space = pl.BlockSpec(memory_space=pl.ANY)
    return pl.pallas_call(
        functools.partial(return_kernel, helpers),
        out_shape=jax.ShapeDtypeStruct(far_sums.shape, far_sums.dtype),
        in_specs=[any_space],
        out_specs=any_space,
        scratch_shapes=[pltpu.SemaphoreType.DMA((helpers - 1,)), pltpu.SemaphoreType.DMA((helpers - 1,))],
        compiler_params=pltpu.CompilerParams(collective_id=1, has_side_effects=True),
        name="return_sums",
    )(far_sums)


ALONE, FIRST, SECOND, THIRD = 4, 8, 8, 12


def slot_count(local):
    return local + FIRST + SECOND + THIRD


def phase_of(target, source, local):
    half = local // 2
    quarter = half // 2
    first = (target < local) | ((target >= local) & (target < local + quarter))
    first = first | ((target >= 2 * local + half) & (target < 2 * local + half + quarter))
    early = first | ((target >= local) & (target < local + half)) | ((target >= 2 * local + half) & (target < 3 * local))
    phase = jnp.where(target < 3 * local, 2, 3)
    phase = jnp.where(early, 1, phase)
    phase = jnp.where(first & (source < 2 * local), 0, phase)
    return jnp.where((target < local) & ((source < local) | (source >= 2 * local)), 4, phase)


def order_tasks(bases, local, lists):
    group, slots = lists.shape
    count = 3 * local
    length = task_length(group, local)
    lists = jnp.where(lists < 0, -(1 << 20), lists)
    row = lax.broadcasted_iota(jnp.int32, (group, 128), 0)
    column = lax.broadcasted_iota(jnp.int32, (group, 128), 1)
    table = jnp.zeros((group, 128), jnp.float32)
    for source in range(count):
        leaf = bases[source // local] + source % local
        one = jnp.max(jnp.where(lists == leaf, 1.0, 0.0), axis=1, keepdims=True)
        table = jnp.where(column == source, one, table)
    table = jnp.where((row == column) & (row < local), 0.0, table)
    phase = phase_of(row, column, local)
    phased = jnp.concatenate([jnp.where(phase == p, table, 0.0) for p in range(5)], axis=0)
    rows = 5 * group
    counted = phased.astype(jnp.bfloat16)
    above = lax.broadcasted_iota(jnp.int32, (rows, rows), 0) > lax.broadcasted_iota(jnp.int32, (rows, rows), 1)
    left = lax.broadcasted_iota(jnp.int32, (128, 128), 0) < lax.broadcasted_iota(jnp.int32, (128, 128), 1)
    inside = jnp.dot(counted, jnp.where(left, 1.0, 0.0).astype(jnp.bfloat16), preferred_element_type=jnp.float32)
    before = jnp.dot(jnp.where(above, 1.0, 0.0).astype(jnp.bfloat16), counted, preferred_element_type=jnp.float32)
    rank = inside + jnp.sum(before, axis=1, keepdims=True)
    rank = jnp.where(phased > 0.5, rank + 1.0, 0.0)
    rank = sum(rank[p * group:(p + 1) * group] for p in range(5)) - 1.0
    in_row = jnp.sum(phased, axis=1, keepdims=True)
    ends = [jnp.sum(in_row[:(p + 1) * group], axis=0, keepdims=True) for p in range(5)]
    place = lax.broadcasted_iota(jnp.int32, (group, length), 1).astype(jnp.float32)
    code_row = lax.broadcasted_iota(jnp.int32, (group, length), 0).astype(jnp.float32) * 256.0
    codes = jnp.zeros((group, length), jnp.float32)
    for source in range(count):
        codes = jnp.where(place == rank[:, source:source + 1], code_row + float(source), codes)
    codes = jnp.sum(codes, axis=0, keepdims=True)
    codes = jnp.where(place[:1] < ends[4], codes, float(group * 256)).astype(jnp.int32)
    line = lax.broadcasted_iota(jnp.int32, (8, length), 0)
    result = jnp.where(line == 0, codes // 256, codes % 256)
    for p in range(5):
        result = jnp.where(line == 2 + p, ends[p].astype(jnp.int32), result)
    return result


def within(value, last):
    return lax.max(lax.min(value, last), 0)


def slot_starts(tasks):
    second = lax.min(tasks[2, 0], FIRST)
    third = lax.min(tasks[3, 0], second + SECOND)
    rest = lax.min(tasks[4, 0], third + THIRD)
    return 0, second, third, rest


def kept_of(tasks):
    return within(tasks[6, 0] - tasks[5, 0], KEPT)


def slot_task(tasks, group, start, end, slot):
    number = within(start + slot, tasks.shape[1] - 1)
    inside = number < end
    target = jnp.where(inside, tasks[0, number], group)
    return within(tasks[1, number], 3 * group // 4 - 1), within(target, group)


def window_kernel(owners, points, weights, lists, sources, targets, held_weights, task_scalars, results,
                  own_points, own_weights, lists_here, far_lists, far_points, near_points, near_weights,
                  kernels, tasks, send_sems, recv_sems, local_sems):
    local, dims, width = points.shape
    helpers = 4
    group = local * helpers
    half = local // 2
    depth = targets.shape[1]
    owner = lax.axis_index("owner")
    helper = lax.axis_index("helper")
    odd = lax.rem(owner, 2)
    chip_owner = owner + 1 - 2 * odd
    next_owner = owner - 1 + 2 * odd
    has_next = (next_owner >= 0) & (next_owner < owners)

    fetches = [
        pltpu.make_async_copy(src, dst, local_sems.at[i])
        for i, (src, dst) in enumerate(
            ((points, own_points), (weights, own_weights), (lists, lists_here))
        )
    ]
    for one in fetches:
        one.start()

    def beside(distance):
        return (owner, partner_of(helper, distance))

    barrier = pltpu.get_barrier_semaphore()
    for device in [beside(1), beside(2), beside(3), (chip_owner, helper)]:
        pl.semaphore_signal(barrier, inc=1, device_id=device, device_id_type=MESH)

    @pl.when(has_next)
    def _():
        pl.semaphore_signal(barrier, inc=1, device_id=(next_owner, helper), device_id_type=MESH)

    pl.semaphore_wait(barrier, helpers + jnp.where(has_next, 1, 0))

    def copy(number, src, dst, device):
        return pltpu.make_async_remote_copy(
            src_ref=src,
            dst_ref=dst,
            send_sem=send_sems.at[number],
            recv_sem=recv_sems.at[number],
            device_id=device,
            device_id_type=MESH,
        )

    list_copies = [copy(d - 1, lists, far_lists.at[d - 1], beside(d)) for d in (1, 2, 3)]
    quarter = half // 2
    sent = []
    for begin, size in ((0, quarter), (quarter, half - quarter), (half, half)):
        for distance in (1, 2):
            part = pl.ds((begin + half * (distance - 1)) % local, size)
            sent.append(
                copy(3 + len(sent), points.at[part], far_points.at[distance - 1, part], beside(distance))
            )
    relayed = []
    for distance in (1, 2):
        part = pl.ds(half * (distance - 1), half)
        relayed.append(
            copy(12 + distance, far_points.at[distance - 1, part], far_points.at[2, part], beside(3 - distance))
        )
    chip = [
        copy(9, points, near_points.at[0], (chip_owner, helper)),
        copy(10, weights, near_weights.at[0], (chip_owner, helper)),
    ]
    beyond = [
        copy(11, points, near_points.at[1], (next_owner, helper)),
        copy(12, weights, near_weights.at[1], (next_owner, helper)),
    ]
    for one in list_copies + sent[:2] + chip:
        one.start()

    @pl.when(has_next)
    def _():
        for one in beyond:
            one.start()

    for one in sent[2:]:
        one.start()

    ones = [jnp.ones((1, width), jnp.float32)] * 3

    def half_norm(value):
        return pieces_of(-0.5 * jnp.sum(value * value, axis=0, keepdims=True), 3)

    def prepare_target(index, block):
        targets[index, pl.ds(0, dims), :] = block
        targets[index, pl.ds(dims, depth - dims), :] = extra_rows(
            ones, half_norm(block.astype(jnp.float32)), depth - dims, width
        ).astype(jnp.bfloat16)

    def prepare_source(index, block):
        value = block.astype(jnp.float32)
        rows = [value, extra_rows(half_norm(value), ones, depth - dims, width)]
        sources[index] = jnp.concatenate(rows, axis=0).T.astype(jnp.bfloat16)

    waiting = []

    def multiply():
        for source, slot, place in waiting:
            results[place] = jnp.dot(held_weights[source], kernels[slot], preferred_element_type=jnp.float32)
        waiting.clear()

    def work(pairs, base):
        side = base // ALONE % 2 * ALONE
        for i, (source, target) in enumerate(pairs):
            exponents = jnp.dot(sources[source], targets[target], preferred_element_type=jnp.float32)
            kernels[side + i] = jnp.exp(exponents).astype(jnp.bfloat16)
        multiply()
        waiting.extend((source, side + i, base + i) for i, (source, _) in enumerate(pairs))

    def work_slots(start, end, slots, base):
        for first in range(0, slots, ALONE):
            work([slot_task(task_scalars, group, start, end, first + i) for i in range(ALONE)], base + first)

    for one in fetches[:2]:
        one.wait()
    for leaf in range(local):
        prepare_target(leaf, own_points[leaf])
        prepare_source(leaf, own_points[leaf])
        held_weights[leaf] = own_weights[leaf]
    targets[group] = jnp.zeros(targets.shape[1:], jnp.bfloat16)
    work([(leaf, leaf) for leaf in range(local)], 0)

    fetches[2].wait()
    for one in list_copies:
        one.wait_recv()
    whole = jnp.concatenate([lists_here[...]] + [far_lists[i] for i in range(helpers - 1)], axis=0)
    bases = [o * group + helper * local for o in (owner, chip_owner, next_owner)]
    tasks[...] = order_tasks(bases, local, whole)
    to_scalars = pltpu.make_async_copy(tasks, task_scalars, local_sems.at[3])
    to_scalars.start()
    for one in chip:
        one.wait_recv()
    for leaf in range(local):
        prepare_source(local + leaf, near_points[0, leaf])
        held_weights[local + leaf] = near_weights[0, leaf]
    to_scalars.wait()
    starts = slot_starts(task_scalars)
    for one in sent[:2]:
        one.wait_recv()
    for leaf in range(quarter):
        prepare_target(local + leaf, far_points[0, leaf])
        prepare_target(2 * local + half + leaf, far_points[1, half + leaf])
    work_slots(starts[0], task_scalars[2, 0], FIRST, local)

    for place, one in enumerate(relayed):
        sent[2 + place].wait_recv()
        one.start()
    for leaf in range(quarter, half):
        prepare_target(local + leaf, far_points[0, leaf])
        prepare_target(2 * local + half + leaf, far_points[1, half + leaf])

    @pl.when(has_next)
    def _():
        for one in beyond:
            one.wait_recv()
        for leaf in range(local):
            prepare_source(2 * local + leaf, near_points[1, leaf])
            held_weights[2 * local + leaf] = near_weights[1, leaf]

    work_slots(starts[1], task_scalars[3, 0], SECOND, local + FIRST)

    for one in sent[4:]:
        one.wait_recv()
    for leaf in range(half):
        prepare_target(local + half + leaf, far_points[0, half + leaf])
        prepare_target(2 * local + leaf, far_points[1, leaf])
    work_slots(starts[2], task_scalars[4, 0], THIRD, local + FIRST + SECOND)

    for one in relayed:
        one.wait_recv()
    for leaf in range(local):
        prepare_target(3 * local + leaf, far_points[2, leaf])
    multiply()
    for one in list_copies + sent + relayed + chip:
        one.wait_send()

    @pl.when(has_next)
    def _():
        for one in beyond:
            one.wait_send()


def gather_and_begin(owners, points, weights, lists):
    local, dims, width = points.shape
    vectors = weights.shape[1]
    group = 4 * local
    depth = dims + EXTRA
    vmem = pl.BlockSpec(memory_space=pltpu.VMEM)
    hbm = pl.BlockSpec(memory_space=pltpu.HBM)
    length = task_length(group, local)
    return pl.pallas_call(
        functools.partial(window_kernel, owners),
        out_shape=(
            pltpu.VMEM((3 * local, width, depth), jnp.bfloat16),
            pltpu.VMEM((group + 1, depth, width), jnp.bfloat16),
            pltpu.VMEM((3 * local, vectors, width), jnp.bfloat16),
            pltpu.SMEM((8, length), jnp.int32),
            pltpu.VMEM((slot_count(local), vectors, width), jnp.float32),
        ),
        in_specs=[hbm, hbm, hbm],
        out_specs=(vmem,) * 3 + (pl.BlockSpec(memory_space=pltpu.SMEM), vmem),
        scratch_shapes=[
            pltpu.VMEM(points.shape, points.dtype),
            pltpu.VMEM(weights.shape, weights.dtype),
            pltpu.VMEM(lists.shape, lists.dtype),
            pltpu.VMEM((3,) + lists.shape, lists.dtype),
            pltpu.VMEM((3,) + points.shape, points.dtype),
            pltpu.VMEM((2,) + points.shape, points.dtype),
            pltpu.VMEM((2,) + weights.shape, weights.dtype),
            pltpu.VMEM((2 * ALONE, width, width), jnp.bfloat16),
            pltpu.VMEM((8, length), jnp.int32),
            pltpu.SemaphoreType.DMA((15,)),
            pltpu.SemaphoreType.DMA((15,)),
            pltpu.SemaphoreType.DMA((4,)),
        ],
        compiler_params=pltpu.CompilerParams(
            collective_id=2, has_side_effects=True, vmem_limit_bytes=VMEM_BYTES
        ),
        name="gather_and_begin",
    )(*(pltpu.with_memory_space_constraint(one, pltpu.HBM) for one in (points, weights, lists)))


def rest_kernel(local, *refs):
    width = refs[2].shape[2]
    vectors = refs[3].shape[1]
    half = width // 2
    accumulators = [
        pltpu.ACC(unit)((rows, half), jnp.float32)
        for rows in (half, half, vectors, vectors)
        for unit in (0, 1)
    ]
    pl.run_scoped(functools.partial(rest_body, local, *refs), *accumulators)


def rest_body(local, tasks, sources, targets, held_weights, results, own_sums, far_sums, out, kernels, *accumulators):
    width = targets.shape[2]
    half = width // 2
    group = 4 * local
    starts = slot_starts(tasks)
    first = starts[3]
    total = tasks[6, 0] - kept_of(tasks) - first
    units = (0, 1)
    exponents = (accumulators[0:2], accumulators[2:4])
    products = (accumulators[4:6], accumulators[6:8])

    def task(number):
        place = lax.max(number, 0) + first
        return tasks[1, place], jnp.where(number < total, tasks[0, place], group)

    def columns(unit):
        return pl.ds(unit * half, half)

    def widened(value, axis):
        missing = list(value.shape)
        missing[axis] = half - value.shape[axis]
        return jnp.concatenate([value, jnp.zeros(missing, value.dtype)], axis=axis)

    def stage_target(number):
        _, target = task(number)
        for unit in units:
            pltpu.matmul_push_rhs(widened(targets[target, :, columns(unit)], 0), 0, unit)

    def find_exponents(number, part):
        source, _ = task(number)
        for unit in units:
            pltpu.matmul_acc_lhs(
                exponents[part][unit],
                widened(sources[source, pl.ds(part * half, half), :], 1),
                0 if part == 0 else None,
            )

    def take_exponentials(part, slot):
        for unit in units:
            kernels[slot, pl.ds(part * half, half), columns(unit)] = jnp.exp(
                pltpu.matmul_pop(exponents[part][unit])
            ).astype(jnp.bfloat16)

    def stage_kernel(slot, part):
        for unit in units:
            pltpu.matmul_push_rhs(kernels[slot, pl.ds(part * half, half), columns(unit)], 1, unit)

    def multiply(number, part, side):
        source, _ = task(number)
        for unit in units:
            pltpu.matmul_acc_lhs(products[side][unit], held_weights[source, :, pl.ds(part * half, half)], 1)

    def add_product(number, side):
        _, target = task(number)
        for unit in units:
            out[target, :, columns(unit)] += pltpu.matmul_pop(products[side][unit])

    stage_target(0)
    for leaf in range(local):
        out[leaf] = results[leaf]
    out[pl.ds(local, group + 1 - local)] = jnp.zeros((group + 1 - local,) + out.shape[1:], jnp.float32)
    base = local
    for phase, slots in enumerate((FIRST, SECOND, THIRD)):
        for slot in range(slots):
            _, target = slot_task(tasks, group, starts[phase], tasks[2 + phase, 0], slot)
            out[target] += results[base + slot]
        base += slots

    def advance(number, slot, age):
        find_exponents(number, 0)
        if age >= 1:
            take_exponentials(1, (slot - 1) % RING)
        stage_target(number + 1)
        if age >= 2:
            stage_kernel((slot - 2) % RING, 0)
        find_exponents(number, 1)
        if age >= 2:
            multiply(number - 2, 0, slot % 2)
            stage_kernel((slot - 2) % RING, 1)
        take_exponentials(0, slot)
        if age >= 2:
            multiply(number - 2, 1, slot % 2)
        if age >= 3:
            add_product(number - 3, (slot - 1) % 2)

    for number in range(4):
        advance(number, number % RING, number)

    def each_step(step, carry):
        for part in range(RING):
            advance(step * RING + part, part, 4)
        return carry

    begun = 4 // RING
    steps = lax.max(lax.div(total + RING - 1, RING), begun)
    lax.fori_loop(begun, steps, each_step, 0)

    last = steps * RING
    find_exponents(last, 0)
    take_exponentials(1, RING - 1)
    for age in (2, 1):
        slot = RING - age
        stage_kernel(slot, 0)
        multiply(last - age, 0, slot % 2)
        stage_kernel(slot, 1)
        multiply(last - age, 1, slot % 2)
        add_product(last - age - 1, (slot - 1) % 2)
    add_product(last - 1, (RING - 1) % 2)
    for unit in units:
        kernels[0, pl.ds(0, half), columns(unit)] = pltpu.matmul_pop(exponents[0][unit]).astype(jnp.bfloat16)

    own_sums[...] = out[pl.ds(0, local)]
    far_sums[...] = out[pl.ds(local, group - local)].astype(jnp.bfloat16).reshape(far_sums.shape)


def sum_rest(local, sources, targets, held_weights, tasks, results):
    width = targets.shape[2]
    vectors = held_weights.shape[1]
    group = 4 * local
    vmem = pl.BlockSpec(memory_space=pltpu.VMEM)
    smem = pl.BlockSpec(memory_space=pltpu.SMEM)
    return pl.pallas_call(
        functools.partial(rest_kernel, local),
        out_shape=(
            pltpu.VMEM((local, vectors, width), jnp.float32),
            pltpu.VMEM((3, local, vectors, width), jnp.bfloat16),
        ),
        in_specs=[smem] + [vmem] * 4,
        out_specs=(vmem, vmem),
        scratch_shapes=[
            pltpu.VMEM((group + 1, vectors, width), jnp.float32),
            pltpu.VMEM((RING, width, width), jnp.bfloat16),
        ],
        compiler_params=pltpu.CompilerParams(vmem_limit_bytes=VMEM_BYTES),
        name="sum_rest",
    )(tasks, sources, targets, held_weights, results)


def finish_kernel(local, tasks, sources, targets, held_weights, own_sums, far_sums, potential, landed, kernels,
                  products, send_sems, recv_sems):
    owner = lax.axis_index("owner")
    helper = lax.axis_index("helper")
    barrier = pltpu.get_barrier_semaphore()
    devices = [(owner, partner_of(helper, distance)) for distance in (1, 2, 3)]
    for device in devices:
        pl.semaphore_signal(barrier, inc=1, device_id=device, device_id_type=MESH)
    pl.semaphore_wait(barrier, 3)
    copies = [
        pltpu.make_async_remote_copy(
            src_ref=far_sums.at[number],
            dst_ref=landed.at[number],
            send_sem=send_sems.at[number],
            recv_sem=recv_sems.at[number],
            device_id=device,
            device_id_type=MESH,
        )
        for number, device in enumerate(devices)
    ]
    for one in reversed(copies):
        one.start()
    kept = kept_of(tasks)
    begin = tasks[6, 0] - kept
    pairs = [slot_task(tasks, 4 * local, begin, tasks[6, 0], slot) for slot in range(KEPT)]
    for first in range(0, KEPT + ALONE, ALONE):
        for slot in range(first, min(first + ALONE, KEPT)):
            source, target = pairs[slot]
            exponents = jnp.dot(sources[source], targets[target], preferred_element_type=jnp.float32)
            kernels[slot] = jnp.exp(exponents).astype(jnp.bfloat16)
        for slot in range(max(first - ALONE, 0), first):
            source, _ = pairs[slot]
            products[slot] = jnp.dot(held_weights[source], kernels[slot], preferred_element_type=jnp.float32)
    for leaf in range(local):
        total = own_sums[leaf]
        for slot in range(KEPT):
            total = total + jnp.where(pairs[slot][1] == leaf, products[slot], 0.0)
        potential[leaf] = total
    for one in copies:
        one.wait()
    for leaf in range(local):
        parts = [landed[number, leaf].astype(jnp.float32) for number in range(3)]
        potential[leaf] = potential[leaf] + (parts[0] + parts[1] + parts[2])


def finish(local, tasks, sources, targets, held_weights, own_sums, far_sums):
    width = targets.shape[2]
    vectors = held_weights.shape[1]
    vmem = pl.BlockSpec(memory_space=pltpu.VMEM)
    smem = pl.BlockSpec(memory_space=pltpu.SMEM)
    return pl.pallas_call(
        functools.partial(finish_kernel, local),
        out_shape=jax.ShapeDtypeStruct(own_sums.shape, jnp.float32),
        in_specs=[smem] + [vmem] * 5,
        out_specs=vmem,
        scratch_shapes=[
            pltpu.VMEM(far_sums.shape, far_sums.dtype),
            pltpu.VMEM((KEPT, width, width), jnp.bfloat16),
            pltpu.VMEM((KEPT, vectors, width), jnp.float32),
            pltpu.SemaphoreType.DMA((3,)),
            pltpu.SemaphoreType.DMA((3,)),
        ],
        compiler_params=pltpu.CompilerParams(
            collective_id=3, has_side_effects=True, vmem_limit_bytes=VMEM_BYTES
        ),
        name="finish",
    )(tasks, sources, targets, held_weights, own_sums, far_sums)


def on_device(points, weights, neighbours, counts):
    owners = lax.axis_size("owner")
    helpers = lax.axis_size("helper")
    local = points.shape[0]
    if helpers == 4 and local == ALONE and owners % 2 == 0:
        sources, targets, held_weights, tasks, results = gather_and_begin(owners, points, weights, neighbours)
        own_sums, far_sums = sum_rest(local, sources, targets, held_weights, tasks, results)
        return finish(local, tasks, sources, targets, held_weights, own_sums, far_sums)
    far_points, near_points, near_weights, tasks = gather_window(owners, helpers, points, weights, neighbours)
    own_sums, far_sums = sum_pairs(helpers, points, weights, far_points, near_points, near_weights, tasks)
    landed = return_sums(helpers, far_sums)
    return own_sums + jnp.sum(landed.astype(jnp.float32), axis=0)


def solution(mesh):
    placed = (
        P(("owner", "helper"), None, None),
        P(("owner", "helper"), None, None),
        P(("owner", "helper"), None),
        P(("owner", "helper")),
    )
    return jax.shard_map(
        on_device,
        mesh=mesh,
        in_specs=placed,
        out_specs=P(("owner", "helper"), None, None),
        check_vma=False,
    )
```

```python
import functools

import jax
import jax.numpy as jnp
from jax import lax
from jax.experimental import pallas as pl
from jax.experimental.pallas import tpu as pltpu
from jax.sharding import PartitionSpec as P

MESH = pl.DeviceIdType.MESH
EXTRA = 16
TOGETHER = 4
VMEM_BYTES = 40 << 20
RING = 2
KEPT = 8


def partner_of(index, distance):
    result = index
    bit = 1
    while bit <= distance:
        if distance & bit:
            result = result + bit - 2 * bit * ((index // bit) % 2)
        bit *= 2
    return result


def list_tasks(base, helper, local, lists):
    group, slots = lists.shape
    count = 3 * local
    length = task_length(group, local)
    lists = jnp.where(lists < 0, -(1 << 20), lists)
    column = lax.broadcasted_iota(jnp.int32, (group, 128), 1)
    listed = []
    table = jnp.zeros((group, 128), jnp.float32)
    for source in range(count):
        leaf = base + (source // local) * group + helper * local + source % local
        one = jnp.max(jnp.where(lists == leaf, 1.0, 0.0), axis=1, keepdims=True)
        listed.append(one)
        table = jnp.where(column == source, one, table)
    below = lax.broadcasted_iota(jnp.int32, (group, group), 0) > lax.broadcasted_iota(jnp.int32, (group, group), 1)
    ahead = jnp.dot(
        jnp.where(below, 1.0, 0.0).astype(jnp.bfloat16), table.astype(jnp.bfloat16), preferred_element_type=jnp.float32
    )
    place = lax.broadcasted_iota(jnp.int32, (group, length), 1).astype(jnp.float32)
    row = lax.broadcasted_iota(jnp.int32, (group, length), 0).astype(jnp.float32)
    total = jnp.zeros((1, 1), jnp.float32)
    targets = jnp.zeros((group, length), jnp.float32)
    sources = jnp.zeros((group, length), jnp.float32)
    for source in range(count):
        here = jnp.where(listed[source] > 0.5, ahead[:, source:source + 1] + total, -1.0)
        targets = jnp.where(place == here, row, targets)
        sources = jnp.where(place == here, float(source), sources)
        total = total + jnp.sum(listed[source], axis=0, keepdims=True)
    target = jnp.where(place[:1] < total, jnp.sum(targets, axis=0, keepdims=True), float(group))
    source = jnp.sum(sources, axis=0, keepdims=True)
    line = lax.broadcasted_iota(jnp.int32, (8, length), 0)
    result = jnp.where(line == 0, target, jnp.where(line == 1, source, total))
    return result.astype(jnp.int32)


def task_length(group, local):
    return -(-(group * 3 * local + 3 * TOGETHER) // 128) * 128


def gather_kernel(owners, helpers, points, weights, lists, far_points, near_points, near_weights, tasks,
                  far_lists, send_sems, recv_sems):
    local = lists.shape[0]
    owner = lax.axis_index("owner")
    helper = lax.axis_index("helper")
    has_before = owner > 0
    has_after = owner < owners - 1
    barrier = pltpu.get_barrier_semaphore()
    for distance in range(1, helpers):
        pl.semaphore_signal(
            barrier, inc=1, device_id=(owner, partner_of(helper, distance)), device_id_type=MESH
        )

    @pl.when(has_before)
    def _():
        pl.semaphore_signal(barrier, inc=1, device_id=(owner - 1, helper), device_id_type=MESH)

    @pl.when(has_after)
    def _():
        pl.semaphore_signal(barrier, inc=1, device_id=(owner + 1, helper), device_id_type=MESH)

    neighbours = lax.min(owner, 1) + lax.min(owners - 1 - owner, 1)
    pl.semaphore_wait(barrier, helpers - 1 + neighbours)

    def copy(number, src, dst, device):
        return pltpu.make_async_remote_copy(
            src_ref=src,
            dst_ref=dst,
            send_sem=send_sems.at[number],
            recv_sem=recv_sems.at[number],
            device_id=device,
            device_id_type=MESH,
        )

    def beside(distance):
        return (owner, partner_of(helper, distance))

    number = 0
    list_copies = []
    for distance in range(1, helpers):
        list_copies.append(copy(number, lists, far_lists.at[distance - 1], beside(distance)))
        number += 1
    sent, relayed = [], []
    if helpers == 4 and local % 2 == 0:
        half = local // 2
        parts = (pl.ds(0, half), pl.ds(half, half))
        for order in (0, 1):
            for distance in (1, 2):
                part = parts[order if distance == 1 else 1 - order]
                one = copy(number, points.at[part], far_points.at[distance - 1, part], beside(distance))
                number += 1
                sent.append(one)
        for distance in (1, 2):
            part = parts[distance - 1]
            block = far_points.at[distance - 1, part]
            one = copy(number, block, far_points.at[2, part], beside(3 - distance))
            number += 1
            relayed.append(one)
    else:
        for distance in range(1, helpers):
            sent.append(copy(number, points, far_points.at[distance - 1], beside(distance)))
            number += 1
    up = [
        copy(number, points, near_points.at[0], (owner + 1, helper)),
        copy(number + 1, weights, near_weights.at[0], (owner + 1, helper)),
    ]
    down = [
        copy(number + 2, points, near_points.at[1], (owner - 1, helper)),
        copy(number + 3, weights, near_weights.at[1], (owner - 1, helper)),
    ]
    for one in list_copies + sent:
        one.start()

    @pl.when(has_after)
    def _():
        for one in up:
            one.start()

    @pl.when(has_before)
    def _():
        for one in down:
            one.start()

    for place, one in enumerate(relayed):
        sent[place].wait_recv()
        one.start()
    for one in list_copies:
        one.wait_recv()
    whole = jnp.concatenate([lists[...]] + [far_lists[i] for i in range(helpers - 1)], axis=0)
    tasks[...] = list_tasks((owner - 1) * local * helpers, helper, local, whole)
    for one in sent[len(relayed):] + relayed:
        one.wait_recv()
    for one in list_copies + sent + relayed:
        one.wait_send()

    @pl.when(has_after)
    def _():
        for one in up:
            one.wait_send()
        for one in down:
            one.wait_recv()

    @pl.when(has_before)
    def _():
        for one in down:
            one.wait_send()
        for one in up:
            one.wait_recv()


def gather_window(owners, helpers, points, weights, lists):
    local = points.shape[0]
    copies = 2 * (helpers - 1) + 10
    vmem = pl.BlockSpec(memory_space=pltpu.VMEM)
    any_space = pl.BlockSpec(memory_space=pl.ANY)
    return pl.pallas_call(
        functools.partial(gather_kernel, owners, helpers),
        out_shape=(
            jax.ShapeDtypeStruct((helpers - 1,) + points.shape, points.dtype),
            jax.ShapeDtypeStruct((2,) + points.shape, points.dtype),
            jax.ShapeDtypeStruct((2,) + weights.shape, weights.dtype),
            jax.ShapeDtypeStruct((8, task_length(local * helpers, local)), jnp.int32),
        ),
        in_specs=[any_space, any_space, vmem],
        out_specs=(any_space, any_space, any_space, vmem),
        scratch_shapes=[
            pltpu.VMEM((helpers - 1,) + lists.shape, lists.dtype),
            pltpu.SemaphoreType.DMA((copies,)),
            pltpu.SemaphoreType.DMA((copies,)),
        ],
        compiler_params=pltpu.CompilerParams(collective_id=0, has_side_effects=True),
        name="gather_window",
    )(points, weights, lists)


def pieces_of(value, count):
    parts = []
    for _ in range(count):
        part = value.astype(jnp.bfloat16).astype(jnp.float32)
        parts.append(part)
        value = value - part
    return parts


def extra_rows(first, second, rows, width):
    row = lax.broadcasted_iota(jnp.int32, (rows, width), 0)
    result = jnp.zeros((rows, width), jnp.float32)
    for i, value in enumerate(list(first) + list(second)):
        result = jnp.where(row == i, value, result)
    return result


def pairs_kernel(local, helpers, tasks, points, weights, far_points, near_points, near_weights,
                 own_sums, far_sums, out, targets, sources, held_weights, exponents, kernels):
    dims, width = points.shape[1:]
    group = local * helpers
    depth = targets.shape[1]
    ones = [jnp.ones((1, width), jnp.float32)] * 3

    def half_norm(value):
        return pieces_of(-0.5 * jnp.sum(value * value, axis=0, keepdims=True), 3)

    def prepare_target(index, block):
        targets[index, pl.ds(0, dims), :] = block
        targets[index, pl.ds(dims, depth - dims), :] = extra_rows(
            ones, half_norm(block.astype(jnp.float32)), depth - dims, width
        ).astype(jnp.bfloat16)

    def prepare_source(index, block):
        value = block.astype(jnp.float32)
        rows = [value, extra_rows(half_norm(value), ones, depth - dims, width)]
        sources[index] = jnp.concatenate(rows, axis=0).T.astype(jnp.bfloat16)

    def each_leaf(leaf, carry):
        prepare_target(leaf, points[leaf])
        prepare_source(local + leaf, points[leaf])
        prepare_source(leaf, near_points[0, leaf])
        prepare_source(2 * local + leaf, near_points[1, leaf])
        held_weights[leaf] = near_weights[0, leaf]
        held_weights[local + leaf] = weights[leaf]
        held_weights[2 * local + leaf] = near_weights[1, leaf]
        return carry

    for leaf in range(local):
        each_leaf(leaf, 0)

    def each_far(distance, carry):
        for leaf in range(local):
            prepare_target((distance + 1) * local + leaf, far_points[distance, leaf])
        return carry

    lax.fori_loop(0, helpers - 1, each_far, 0)

    total = tasks[2, 0]
    out[...] = jnp.zeros(out.shape, jnp.float32)

    def add_products(step):
        for part in range(TOGETHER):
            number = step * TOGETHER + part
            source, target = tasks[1, number], tasks[0, number]
            out[target] += jnp.dot(held_weights[source], kernels[part], preferred_element_type=jnp.float32)

    def take_exponentials():
        for part in range(TOGETHER):
            kernels[part] = jnp.exp(exponents[part]).astype(jnp.bfloat16)

    def find_exponents(step):
        for part in range(TOGETHER):
            number = step * TOGETHER + part
            source, target = tasks[1, number], tasks[0, number]
            exponents[part] = jnp.dot(sources[source], targets[target], preferred_element_type=jnp.float32)

    find_exponents(0)
    take_exponentials()
    find_exponents(1)

    def each_step(step, carry):
        add_products(step)
        take_exponentials()
        find_exponents(step + 2)
        return carry

    steps = lax.div(total + TOGETHER - 1, TOGETHER)
    lax.fori_loop(0, steps - 1, each_step, 0)

    @pl.when(total > 0)
    def _():
        add_products(steps - 1)

    own_sums[...] = out[pl.ds(0, local)]
    far_sums[...] = out[pl.ds(local, group - local)].astype(jnp.bfloat16).reshape(far_sums.shape)


def sum_pairs(helpers, points, weights, far_points, near_points, near_weights, tasks):
    local, dims, width = points.shape
    vectors = weights.shape[1]
    group = local * helpers
    vmem = pl.BlockSpec(memory_space=pltpu.VMEM)
    smem = pl.BlockSpec(memory_space=pltpu.SMEM)
    return pl.pallas_call(
        functools.partial(pairs_kernel, local, helpers),
        out_shape=(
            jax.ShapeDtypeStruct((local, vectors, width), jnp.float32),
            jax.ShapeDtypeStruct((helpers - 1, local, vectors, width), jnp.bfloat16),
        ),
        in_specs=[smem] + [vmem] * 5,
        out_specs=(vmem, vmem),
        scratch_shapes=[
            pltpu.VMEM((group + 1, vectors, width), jnp.float32),
            pltpu.VMEM((group + 1, dims + EXTRA, width), jnp.bfloat16),
            pltpu.VMEM((3 * local, width, dims + EXTRA), jnp.bfloat16),
            pltpu.VMEM((3 * local, vectors, width), jnp.bfloat16),
            pltpu.VMEM((TOGETHER, width, width), jnp.float32),
            pltpu.VMEM((TOGETHER, width, width), jnp.bfloat16),
        ],
        name="sum_pairs",
    )(tasks, points, weights, far_points, near_points, near_weights)


def return_kernel(helpers, far_sums, landed, send_sems, recv_sems):
    owner = lax.axis_index("owner")
    helper = lax.axis_index("helper")
    barrier = pltpu.get_barrier_semaphore()
    for distance in range(1, helpers):
        pl.semaphore_signal(
            barrier, inc=1, device_id=(owner, partner_of(helper, distance)), device_id_type=MESH
        )
    pl.semaphore_wait(barrier, helpers - 1)
    copies = []
    for distance in range(1, helpers):
        one = pltpu.make_async_remote_copy(
            src_ref=far_sums.at[distance - 1],
            dst_ref=landed.at[distance - 1],
            send_sem=send_sems.at[distance - 1],
            recv_sem=recv_sems.at[distance - 1],
            device_id=(owner, partner_of(helper, distance)),
            device_id_type=MESH,
        )
        copies.append(one)
    for one in reversed(copies):
        one.start()
    for one in copies:
        one.wait()


def return_sums(helpers, far_sums):
    any_space = pl.BlockSpec(memory_space=pl.ANY)
    return pl.pallas_call(
        functools.partial(return_kernel, helpers),
        out_shape=jax.ShapeDtypeStruct(far_sums.shape, far_sums.dtype),
        in_specs=[any_space],
        out_specs=any_space,
        scratch_shapes=[pltpu.SemaphoreType.DMA((helpers - 1,)), pltpu.SemaphoreType.DMA((helpers - 1,))],
        compiler_params=pltpu.CompilerParams(collective_id=1, has_side_effects=True),
        name="return_sums",
    )(far_sums)


ALONE, FIRST, SECOND, THIRD = 4, 8, 8, 12


def slot_count(local):
    return local + FIRST + SECOND + THIRD


def phase_of(target, source, local):
    half = local // 2
    quarter = half // 2
    first = (target < local) | ((target >= local) & (target < local + quarter))
    first = first | ((target >= 2 * local + half) & (target < 2 * local + half + quarter))
    early = first | ((target >= local) & (target < local + half)) | ((target >= 2 * local + half) & (target < 3 * local))
    phase = jnp.where(target < 3 * local, 2, 3)
    phase = jnp.where(early, 1, phase)
    phase = jnp.where(first & (source < 2 * local), 0, phase)
    return jnp.where((target < local) & ((source < local) | (source >= 2 * local)), 4, phase)


def order_tasks(bases, local, lists):
    group, slots = lists.shape
    count = 3 * local
    length = task_length(group, local)
    lists = jnp.where(lists < 0, -(1 << 20), lists)
    row = lax.broadcasted_iota(jnp.int32, (group, 128), 0)
    column = lax.broadcasted_iota(jnp.int32, (group, 128), 1)
    table = jnp.zeros((group, 128), jnp.float32)
    for source in range(count):
        leaf = bases[source // local] + source % local
        one = jnp.max(jnp.where(lists == leaf, 1.0, 0.0), axis=1, keepdims=True)
        table = jnp.where(column == source, one, table)
    table = jnp.where((row == column) & (row < local), 0.0, table)
    phase = phase_of(row, column, local)
    phased = jnp.concatenate([jnp.where(phase == p, table, 0.0) for p in range(5)], axis=0)
    rows = 5 * group
    counted = phased.astype(jnp.bfloat16)
    above = lax.broadcasted_iota(jnp.int32, (rows, rows), 0) > lax.broadcasted_iota(jnp.int32, (rows, rows), 1)
    left = lax.broadcasted_iota(jnp.int32, (128, 128), 0) < lax.broadcasted_iota(jnp.int32, (128, 128), 1)
    inside = jnp.dot(counted, jnp.where(left, 1.0, 0.0).astype(jnp.bfloat16), preferred_element_type=jnp.float32)
    before = jnp.dot(jnp.where(above, 1.0, 0.0).astype(jnp.bfloat16), counted, preferred_element_type=jnp.float32)
    rank = inside + jnp.sum(before, axis=1, keepdims=True)
    rank = jnp.where(phased > 0.5, rank + 1.0, 0.0)
    rank = sum(rank[p * group:(p + 1) * group] for p in range(5)) - 1.0
    in_row = jnp.sum(phased, axis=1, keepdims=True)
    ends = [jnp.sum(in_row[:(p + 1) * group], axis=0, keepdims=True) for p in range(5)]
    place = lax.broadcasted_iota(jnp.int32, (group, length), 1).astype(jnp.float32)
    code_row = lax.broadcasted_iota(jnp.int32, (group, length), 0).astype(jnp.float32) * 256.0
    codes = jnp.zeros((group, length), jnp.float32)
    for source in range(count):
        codes = jnp.where(place == rank[:, source:source + 1], code_row + float(source), codes)
    codes = jnp.sum(codes, axis=0, keepdims=True)
    codes = jnp.where(place[:1] < ends[4], codes, float(group * 256)).astype(jnp.int32)
    line = lax.broadcasted_iota(jnp.int32, (8, length), 0)
    result = jnp.where(line == 0, codes // 256, codes % 256)
    for p in range(5):
        result = jnp.where(line == 2 + p, ends[p].astype(jnp.int32), result)
    return result


def within(value, last):
    return lax.max(lax.min(value, last), 0)


def slot_starts(tasks):
    second = lax.min(tasks[2, 0], FIRST)
    third = lax.min(tasks[3, 0], second + SECOND)
    rest = lax.min(tasks[4, 0], third + THIRD)
    return 0, second, third, rest


def kept_of(tasks):
    return within(tasks[6, 0] - tasks[5, 0], KEPT)


def slot_task(tasks, group, start, end, slot):
    number = within(start + slot, tasks.shape[1] - 1)
    inside = number < end
    target = jnp.where(inside, tasks[0, number], group)
    return within(tasks[1, number], 3 * group // 4 - 1), within(target, group)


def window_kernel(owners, points, weights, lists, sources, targets, held_weights, task_scalars, results,
                  own_points, own_weights, lists_here, far_lists, far_points, near_points, near_weights,
                  kernels, tasks, send_sems, recv_sems, local_sems):
    local, dims, width = points.shape
    helpers = 4
    group = local * helpers
    half = local // 2
    depth = targets.shape[1]
    owner = lax.axis_index("owner")
    helper = lax.axis_index("helper")
    odd = lax.rem(owner, 2)
    chip_owner = owner + 1 - 2 * odd
    next_owner = owner - 1 + 2 * odd
    has_next = (next_owner >= 0) & (next_owner < owners)

    fetches = [
        pltpu.make_async_copy(src, dst, local_sems.at[i])
        for i, (src, dst) in enumerate(
            ((points, own_points), (weights, own_weights), (lists, lists_here))
        )
    ]
    for one in fetches:
        one.start()

    def beside(distance):
        return (owner, partner_of(helper, distance))

    barrier = pltpu.get_barrier_semaphore()
    for device in [beside(1), beside(2), beside(3), (chip_owner, helper)]:
        pl.semaphore_signal(barrier, inc=1, device_id=device, device_id_type=MESH)

    @pl.when(has_next)
    def _():
        pl.semaphore_signal(barrier, inc=1, device_id=(next_owner, helper), device_id_type=MESH)

    pl.semaphore_wait(barrier, helpers + jnp.where(has_next, 1, 0))

    def copy(number, src, dst, device):
        return pltpu.make_async_remote_copy(
            src_ref=src,
            dst_ref=dst,
            send_sem=send_sems.at[number],
            recv_sem=recv_sems.at[number],
            device_id=device,
            device_id_type=MESH,
        )

    list_copies = [copy(d - 1, lists, far_lists.at[d - 1], beside(d)) for d in (1, 2, 3)]
    quarter = half // 2
    sent = []
    for begin, size in ((0, quarter), (quarter, half - quarter), (half, half)):
        for distance in (1, 2):
            part = pl.ds((begin + half * (distance - 1)) % local, size)
            sent.append(
                copy(3 + len(sent), points.at[part], far_points.at[distance - 1, part], beside(distance))
            )
    relayed = []
    for distance in (1, 2):
        part = pl.ds(half * (distance - 1), half)
        relayed.append(
            copy(12 + distance, far_points.at[distance - 1, part], far_points.at[2, part], beside(3 - distance))
        )
    chip = [
        copy(9, points, near_points.at[0], (chip_owner, helper)),
        copy(10, weights, near_weights.at[0], (chip_owner, helper)),
    ]
    beyond = [
        copy(11, points, near_points.at[1], (next_owner, helper)),
        copy(12, weights, near_weights.at[1], (next_owner, helper)),
    ]
    for one in list_copies + sent[:2] + chip:
        one.start()

    @pl.when(has_next)
    def _():
        for one in beyond:
            one.start()

    for one in sent[2:]:
        one.start()

    ones = [jnp.ones((1, width), jnp.float32)] * 3

    def half_norm(value):
        return pieces_of(-0.5 * jnp.sum(value * value, axis=0, keepdims=True), 3)

    def prepare_target(index, block):
        targets[index, pl.ds(0, dims), :] = block
        targets[index, pl.ds(dims, depth - dims), :] = extra_rows(
            ones, half_norm(block.astype(jnp.float32)), depth - dims, width
        ).astype(jnp.bfloat16)

    def prepare_source(index, block):
        value = block.astype(jnp.float32)
        rows = [value, extra_rows(half_norm(value), ones, depth - dims, width)]
        sources[index] = jnp.concatenate(rows, axis=0).T.astype(jnp.bfloat16)

    waiting = []

    def multiply():
        for source, slot, place in waiting:
            results[place] = jnp.dot(held_weights[source], kernels[slot], preferred_element_type=jnp.float32)
        waiting.clear()

    def work(pairs, base):
        side = base // ALONE % 2 * ALONE
        for i, (source, target) in enumerate(pairs):
            exponents = jnp.dot(sources[source], targets[target], preferred_element_type=jnp.float32)
            kernels[side + i] = jnp.exp(exponents).astype(jnp.bfloat16)
        multiply()
        waiting.extend((source, side + i, base + i) for i, (source, _) in enumerate(pairs))

    def work_slots(start, end, slots, base):
        for first in range(0, slots, ALONE):
            work([slot_task(task_scalars, group, start, end, first + i) for i in range(ALONE)], base + first)

    for one in fetches[:2]:
        one.wait()
    for leaf in range(local):
        prepare_target(leaf, own_points[leaf])
        prepare_source(leaf, own_points[leaf])
        held_weights[leaf] = own_weights[leaf]
    targets[group] = jnp.zeros(targets.shape[1:], jnp.bfloat16)
    work([(leaf, leaf) for leaf in range(local)], 0)

    fetches[2].wait()
    for one in list_copies:
        one.wait_recv()
    whole = jnp.concatenate([lists_here[...]] + [far_lists[i] for i in range(helpers - 1)], axis=0)
    bases = [o * group + helper * local for o in (owner, chip_owner, next_owner)]
    tasks[...] = order_tasks(bases, local, whole)
    to_scalars = pltpu.make_async_copy(tasks, task_scalars, local_sems.at[3])
    to_scalars.start()
    for one in chip:
        one.wait_recv()
    for leaf in range(local):
        prepare_source(local + leaf, near_points[0, leaf])
        held_weights[local + leaf] = near_weights[0, leaf]
    to_scalars.wait()
    starts = slot_starts(task_scalars)
    for one in sent[:2]:
        one.wait_recv()
    for leaf in range(quarter):
        prepare_target(local + leaf, far_points[0, leaf])
        prepare_target(2 * local + half + leaf, far_points[1, half + leaf])
    work_slots(starts[0], task_scalars[2, 0], FIRST, local)

    for place, one in enumerate(relayed):
        sent[2 + place].wait_recv()
        one.start()
    for leaf in range(quarter, half):
        prepare_target(local + leaf, far_points[0, leaf])
        prepare_target(2 * local + half + leaf, far_points[1, half + leaf])

    @pl.when(has_next)
    def _():
        for one in beyond:
            one.wait_recv()
        for leaf in range(local):
            prepare_source(2 * local + leaf, near_points[1, leaf])
            held_weights[2 * local + leaf] = near_weights[1, leaf]

    work_slots(starts[1], task_scalars[3, 0], SECOND, local + FIRST)

    for one in sent[4:]:
        one.wait_recv()
    for leaf in range(half):
        prepare_target(local + half + leaf, far_points[0, half + leaf])
        prepare_target(2 * local + leaf, far_points[1, leaf])
    work_slots(starts[2], task_scalars[4, 0], THIRD, local + FIRST + SECOND)

    for one in relayed:
        one.wait_recv()
    for leaf in range(local):
        prepare_target(3 * local + leaf, far_points[2, leaf])
    multiply()
    for one in list_copies + sent + relayed + chip:
        one.wait_send()

    @pl.when(has_next)
    def _():
        for one in beyond:
            one.wait_send()


def gather_and_begin(owners, points, weights, lists):
    local, dims, width = points.shape
    vectors = weights.shape[1]
    group = 4 * local
    depth = dims + EXTRA
    vmem = pl.BlockSpec(memory_space=pltpu.VMEM)
    hbm = pl.BlockSpec(memory_space=pltpu.HBM)
    length = task_length(group, local)
    return pl.pallas_call(
        functools.partial(window_kernel, owners),
        out_shape=(
            pltpu.VMEM((3 * local, width, depth), jnp.bfloat16),
            pltpu.VMEM((group + 1, depth, width), jnp.bfloat16),
            pltpu.VMEM((3 * local, vectors, width), jnp.bfloat16),
            pltpu.SMEM((8, length), jnp.int32),
            pltpu.VMEM((slot_count(local), vectors, width), jnp.float32),
        ),
        in_specs=[hbm, hbm, hbm],
        out_specs=(vmem,) * 3 + (pl.BlockSpec(memory_space=pltpu.SMEM), vmem),
        scratch_shapes=[
            pltpu.VMEM(points.shape, points.dtype),
            pltpu.VMEM(weights.shape, weights.dtype),
            pltpu.VMEM(lists.shape, lists.dtype),
            pltpu.VMEM((3,) + lists.shape, lists.dtype),
            pltpu.VMEM((3,) + points.shape, points.dtype),
            pltpu.VMEM((2,) + points.shape, points.dtype),
            pltpu.VMEM((2,) + weights.shape, weights.dtype),
            pltpu.VMEM((2 * ALONE, width, width), jnp.bfloat16),
            pltpu.VMEM((8, length), jnp.int32),
            pltpu.SemaphoreType.DMA((15,)),
            pltpu.SemaphoreType.DMA((15,)),
            pltpu.SemaphoreType.DMA((4,)),
        ],
        compiler_params=pltpu.CompilerParams(
            collective_id=2, has_side_effects=True, vmem_limit_bytes=VMEM_BYTES
        ),
        name="gather_and_begin",
    )(*(pltpu.with_memory_space_constraint(one, pltpu.HBM) for one in (points, weights, lists)))


def rest_kernel(local, *refs):
    width = refs[2].shape[2]
    vectors = refs[3].shape[1]
    half = width // 2
    accumulators = [
        pltpu.ACC(unit)((rows, half), jnp.float32)
        for rows in (half, half, vectors, vectors)
        for unit in (0, 1)
    ]
    pl.run_scoped(functools.partial(rest_body, local, *refs), *accumulators)


def rest_body(local, tasks, sources, targets, held_weights, results, own_sums, far_sums, out, kernels, *accumulators):
    width = targets.shape[2]
    half = width // 2
    group = 4 * local
    starts = slot_starts(tasks)
    first = starts[3]
    total = tasks[6, 0] - kept_of(tasks) - first
    units = (0, 1)
    exponents = (accumulators[0:2], accumulators[2:4])
    products = (accumulators[4:6], accumulators[6:8])

    def task(number):
        place = lax.max(number, 0) + first
        return tasks[1, place], jnp.where(number < total, tasks[0, place], group)

    def columns(unit):
        return pl.ds(unit * half, half)

    def widened(value, axis):
        missing = list(value.shape)
        missing[axis] = half - value.shape[axis]
        return jnp.concatenate([value, jnp.zeros(missing, value.dtype)], axis=axis)

    def stage_target(number):
        _, target = task(number)
        for unit in units:
            pltpu.matmul_push_rhs(widened(targets[target, :, columns(unit)], 0), 0, unit)

    def find_exponents(number, part):
        source, _ = task(number)
        for unit in units:
            pltpu.matmul_acc_lhs(
                exponents[part][unit],
                widened(sources[source, pl.ds(part * half, half), :], 1),
                0 if part == 0 else None,
            )

    def take_exponentials(part, slot):
        for unit in units:
            kernels[slot, pl.ds(part * half, half), columns(unit)] = jnp.exp(
                pltpu.matmul_pop(exponents[part][unit])
            ).astype(jnp.bfloat16)

    def stage_kernel(slot, part):
        for unit in units:
            pltpu.matmul_push_rhs(kernels[slot, pl.ds(part * half, half), columns(unit)], 1, unit)

    def multiply(number, part, side):
        source, _ = task(number)
        for unit in units:
            pltpu.matmul_acc_lhs(products[side][unit], held_weights[source, :, pl.ds(part * half, half)], 1)

    def add_product(number, side):
        _, target = task(number)
        for unit in units:
            out[target, :, columns(unit)] += pltpu.matmul_pop(products[side][unit])

    stage_target(0)
    for leaf in range(local):
        out[leaf] = results[leaf]
    out[pl.ds(local, group + 1 - local)] = jnp.zeros((group + 1 - local,) + out.shape[1:], jnp.float32)
    base = local
    for phase, slots in enumerate((FIRST, SECOND, THIRD)):
        for slot in range(slots):
            _, target = slot_task(tasks, group, starts[phase], tasks[2 + phase, 0], slot)
            out[target] += results[base + slot]
        base += slots

    def advance(number, slot, age):
        find_exponents(number, 0)
        if age >= 1:
            take_exponentials(1, (slot - 1) % RING)
        stage_target(number + 1)
        if age >= 2:
            stage_kernel((slot - 2) % RING, 0)
        find_exponents(number, 1)
        if age >= 2:
            multiply(number - 2, 0, slot % 2)
            stage_kernel((slot - 2) % RING, 1)
        take_exponentials(0, slot)
        if age >= 2:
            multiply(number - 2, 1, slot % 2)
        if age >= 3:
            add_product(number - 3, (slot - 1) % 2)

    for number in range(4):
        advance(number, number % RING, number)

    def each_step(step, carry):
        for part in range(RING):
            advance(step * RING + part, part, 4)
        return carry

    begun = 4 // RING
    steps = lax.max(lax.div(total + RING - 1, RING), begun)
    lax.fori_loop(begun, steps, each_step, 0)

    last = steps * RING
    find_exponents(last, 0)
    take_exponentials(1, RING - 1)
    for age in (2, 1):
        slot = RING - age
        stage_kernel(slot, 0)
        multiply(last - age, 0, slot % 2)
        stage_kernel(slot, 1)
        multiply(last - age, 1, slot % 2)
        add_product(last - age - 1, (slot - 1) % 2)
    add_product(last - 1, (RING - 1) % 2)
    for unit in units:
        kernels[0, pl.ds(0, half), columns(unit)] = pltpu.matmul_pop(exponents[0][unit]).astype(jnp.bfloat16)

    own_sums[...] = out[pl.ds(0, local)]
    far_sums[...] = out[pl.ds(local, group - local)].astype(jnp.bfloat16).reshape(far_sums.shape)


def sum_rest(local, sources, targets, held_weights, tasks, results):
    width = targets.shape[2]
    vectors = held_weights.shape[1]
    group = 4 * local
    vmem = pl.BlockSpec(memory_space=pltpu.VMEM)
    smem = pl.BlockSpec(memory_space=pltpu.SMEM)
    return pl.pallas_call(
        functools.partial(rest_kernel, local),
        out_shape=(
            pltpu.VMEM((local, vectors, width), jnp.float32),
            pltpu.VMEM((3, local, vectors, width), jnp.bfloat16),
        ),
        in_specs=[smem] + [vmem] * 4,
        out_specs=(vmem, vmem),
        scratch_shapes=[
            pltpu.VMEM((group + 1, vectors, width), jnp.float32),
            pltpu.VMEM((RING, width, width), jnp.bfloat16),
        ],
        compiler_params=pltpu.CompilerParams(vmem_limit_bytes=VMEM_BYTES),
        name="sum_rest",
    )(tasks, sources, targets, held_weights, results)


def finish_kernel(local, tasks, sources, targets, held_weights, own_sums, far_sums, potential, landed, kernels,
                  products, send_sems, recv_sems):
    owner = lax.axis_index("owner")
    helper = lax.axis_index("helper")
    barrier = pltpu.get_barrier_semaphore()
    devices = [(owner, partner_of(helper, distance)) for distance in (1, 2, 3)]
    for device in devices:
        pl.semaphore_signal(barrier, inc=1, device_id=device, device_id_type=MESH)
    pl.semaphore_wait(barrier, 3)
    copies = [
        pltpu.make_async_remote_copy(
            src_ref=far_sums.at[number],
            dst_ref=landed.at[number],
            send_sem=send_sems.at[number],
            recv_sem=recv_sems.at[number],
            device_id=device,
            device_id_type=MESH,
        )
        for number, device in enumerate(devices)
    ]
    for one in reversed(copies):
        one.start()
    kept = kept_of(tasks)
    begin = tasks[6, 0] - kept
    pairs = [slot_task(tasks, 4 * local, begin, tasks[6, 0], slot) for slot in range(KEPT)]
    for first in range(0, KEPT + ALONE, ALONE):
        for slot in range(first, min(first + ALONE, KEPT)):
            source, target = pairs[slot]
            exponents = jnp.dot(sources[source], targets[target], preferred_element_type=jnp.float32)
            kernels[slot] = jnp.exp(exponents).astype(jnp.bfloat16)
        for slot in range(max(first - ALONE, 0), first):
            source, _ = pairs[slot]
            products[slot] = jnp.dot(held_weights[source], kernels[slot], preferred_element_type=jnp.float32)
    for leaf in range(local):
        total = own_sums[leaf]
        for slot in range(KEPT):
            total = total + jnp.where(pairs[slot][1] == leaf, products[slot], 0.0)
        potential[leaf] = total
    for one in copies:
        one.wait()


def finish(local, tasks, sources, targets, held_weights, own_sums, far_sums):
    width = targets.shape[2]
    vectors = held_weights.shape[1]
    vmem = pl.BlockSpec(memory_space=pltpu.VMEM)
    smem = pl.BlockSpec(memory_space=pltpu.SMEM)
    return pl.pallas_call(
        functools.partial(finish_kernel, local),
        out_shape=(pltpu.VMEM(own_sums.shape, jnp.float32), pltpu.VMEM(far_sums.shape, far_sums.dtype)),
        in_specs=[smem] + [vmem] * 5,
        out_specs=(vmem, vmem),
        scratch_shapes=[
            pltpu.VMEM((KEPT, width, width), jnp.bfloat16),
            pltpu.VMEM((KEPT, vectors, width), jnp.float32),
            pltpu.SemaphoreType.DMA((3,)),
            pltpu.SemaphoreType.DMA((3,)),
        ],
        compiler_params=pltpu.CompilerParams(
            collective_id=3, has_side_effects=True, vmem_limit_bytes=VMEM_BYTES
        ),
        name="finish",
    )(tasks, sources, targets, held_weights, own_sums, far_sums)


def on_device(points, weights, neighbours, counts):
    owners = lax.axis_size("owner")
    helpers = lax.axis_size("helper")
    local = points.shape[0]
    if helpers == 4 and local == ALONE and owners % 2 == 0:
        sources, targets, held_weights, tasks, results = gather_and_begin(owners, points, weights, neighbours)
        own_sums, far_sums = sum_rest(local, sources, targets, held_weights, tasks, results)
        own_sums, landed = finish(local, tasks, sources, targets, held_weights, own_sums, far_sums)
        parts = [landed[i].astype(jnp.float32) for i in range(3)]
        return own_sums + (parts[0] + parts[1] + parts[2])
    far_points, near_points, near_weights, tasks = gather_window(owners, helpers, points, weights, neighbours)
    own_sums, far_sums = sum_pairs(helpers, points, weights, far_points, near_points, near_weights, tasks)
    landed = return_sums(helpers, far_sums)
    return own_sums + jnp.sum(landed.astype(jnp.float32), axis=0)


def solution(mesh):
    placed = (
        P(("owner", "helper"), None, None),
        P(("owner", "helper"), None, None),
        P(("owner", "helper"), None),
        P(("owner", "helper")),
    )
    return jax.shard_map(
        on_device,
        mesh=mesh,
        in_specs=placed,
        out_specs=P(("owner", "helper"), None, None),
        check_vma=False,
    )
```

```python
import functools

import jax
import jax.numpy as jnp
from jax import lax
from jax.experimental import pallas as pl
from jax.experimental.pallas import tpu as pltpu
from jax.sharding import PartitionSpec as P

MESH = pl.DeviceIdType.MESH
EXTRA = 16
TOGETHER = 4
VMEM_BYTES = 40 << 20
RING = 2
KEPT = 12


def partner_of(index, distance):
    result = index
    bit = 1
    while bit <= distance:
        if distance & bit:
            result = result + bit - 2 * bit * ((index // bit) % 2)
        bit *= 2
    return result


def list_tasks(base, helper, local, lists):
    group, slots = lists.shape
    count = 3 * local
    length = task_length(group, local)
    lists = jnp.where(lists < 0, -(1 << 20), lists)
    column = lax.broadcasted_iota(jnp.int32, (group, 128), 1)
    listed = []
    table = jnp.zeros((group, 128), jnp.float32)
    for source in range(count):
        leaf = base + (source // local) * group + helper * local + source % local
        one = jnp.max(jnp.where(lists == leaf, 1.0, 0.0), axis=1, keepdims=True)
        listed.append(one)
        table = jnp.where(column == source, one, table)
    below = lax.broadcasted_iota(jnp.int32, (group, group), 0) > lax.broadcasted_iota(jnp.int32, (group, group), 1)
    ahead = jnp.dot(
        jnp.where(below, 1.0, 0.0).astype(jnp.bfloat16), table.astype(jnp.bfloat16), preferred_element_type=jnp.float32
    )
    place = lax.broadcasted_iota(jnp.int32, (group, length), 1).astype(jnp.float32)
    row = lax.broadcasted_iota(jnp.int32, (group, length), 0).astype(jnp.float32)
    total = jnp.zeros((1, 1), jnp.float32)
    targets = jnp.zeros((group, length), jnp.float32)
    sources = jnp.zeros((group, length), jnp.float32)
    for source in range(count):
        here = jnp.where(listed[source] > 0.5, ahead[:, source:source + 1] + total, -1.0)
        targets = jnp.where(place == here, row, targets)
        sources = jnp.where(place == here, float(source), sources)
        total = total + jnp.sum(listed[source], axis=0, keepdims=True)
    target = jnp.where(place[:1] < total, jnp.sum(targets, axis=0, keepdims=True), float(group))
    source = jnp.sum(sources, axis=0, keepdims=True)
    line = lax.broadcasted_iota(jnp.int32, (8, length), 0)
    result = jnp.where(line == 0, target, jnp.where(line == 1, source, total))
    return result.astype(jnp.int32)


def task_length(group, local):
    return -(-(group * 3 * local + 3 * TOGETHER) // 128) * 128


def gather_kernel(owners, helpers, points, weights, lists, far_points, near_points, near_weights, tasks,
                  far_lists, send_sems, recv_sems):
    local = lists.shape[0]
    owner = lax.axis_index("owner")
    helper = lax.axis_index("helper")
    has_before = owner > 0
    has_after = owner < owners - 1
    barrier = pltpu.get_barrier_semaphore()
    for distance in range(1, helpers):
        pl.semaphore_signal(
            barrier, inc=1, device_id=(owner, partner_of(helper, distance)), device_id_type=MESH
        )

    @pl.when(has_before)
    def _():
        pl.semaphore_signal(barrier, inc=1, device_id=(owner - 1, helper), device_id_type=MESH)

    @pl.when(has_after)
    def _():
        pl.semaphore_signal(barrier, inc=1, device_id=(owner + 1, helper), device_id_type=MESH)

    neighbours = lax.min(owner, 1) + lax.min(owners - 1 - owner, 1)
    pl.semaphore_wait(barrier, helpers - 1 + neighbours)

    def copy(number, src, dst, device):
        return pltpu.make_async_remote_copy(
            src_ref=src,
            dst_ref=dst,
            send_sem=send_sems.at[number],
            recv_sem=recv_sems.at[number],
            device_id=device,
            device_id_type=MESH,
        )

    def beside(distance):
        return (owner, partner_of(helper, distance))

    number = 0
    list_copies = []
    for distance in range(1, helpers):
        list_copies.append(copy(number, lists, far_lists.at[distance - 1], beside(distance)))
        number += 1
    sent, relayed = [], []
    if helpers == 4 and local % 2 == 0:
        half = local // 2
        parts = (pl.ds(0, half), pl.ds(half, half))
        for order in (0, 1):
            for distance in (1, 2):
                part = parts[order if distance == 1 else 1 - order]
                one = copy(number, points.at[part], far_points.at[distance - 1, part], beside(distance))
                number += 1
                sent.append(one)
        for distance in (1, 2):
            part = parts[distance - 1]
            block = far_points.at[distance - 1, part]
            one = copy(number, block, far_points.at[2, part], beside(3 - distance))
            number += 1
            relayed.append(one)
    else:
        for distance in range(1, helpers):
            sent.append(copy(number, points, far_points.at[distance - 1], beside(distance)))
            number += 1
    up = [
        copy(number, points, near_points.at[0], (owner + 1, helper)),
        copy(number + 1, weights, near_weights.at[0], (owner + 1, helper)),
    ]
    down = [
        copy(number + 2, points, near_points.at[1], (owner - 1, helper)),
        copy(number + 3, weights, near_weights.at[1], (owner - 1, helper)),
    ]
    for one in list_copies + sent:
        one.start()

    @pl.when(has_after)
    def _():
        for one in up:
            one.start()

    @pl.when(has_before)
    def _():
        for one in down:
            one.start()

    for place, one in enumerate(relayed):
        sent[place].wait_recv()
        one.start()
    for one in list_copies:
        one.wait_recv()
    whole = jnp.concatenate([lists[...]] + [far_lists[i] for i in range(helpers - 1)], axis=0)
    tasks[...] = list_tasks((owner - 1) * local * helpers, helper, local, whole)
    for one in sent[len(relayed):] + relayed:
        one.wait_recv()
    for one in list_copies + sent + relayed:
        one.wait_send()

    @pl.when(has_after)
    def _():
        for one in up:
            one.wait_send()
        for one in down:
            one.wait_recv()

    @pl.when(has_before)
    def _():
        for one in down:
            one.wait_send()
        for one in up:
            one.wait_recv()


def gather_window(owners, helpers, points, weights, lists):
    local = points.shape[0]
    copies = 2 * (helpers - 1) + 10
    vmem = pl.BlockSpec(memory_space=pltpu.VMEM)
    any_space = pl.BlockSpec(memory_space=pl.ANY)
    return pl.pallas_call(
        functools.partial(gather_kernel, owners, helpers),
        out_shape=(
            jax.ShapeDtypeStruct((helpers - 1,) + points.shape, points.dtype),
            jax.ShapeDtypeStruct((2,) + points.shape, points.dtype),
            jax.ShapeDtypeStruct((2,) + weights.shape, weights.dtype),
            jax.ShapeDtypeStruct((8, task_length(local * helpers, local)), jnp.int32),
        ),
        in_specs=[any_space, any_space, vmem],
        out_specs=(any_space, any_space, any_space, vmem),
        scratch_shapes=[
            pltpu.VMEM((helpers - 1,) + lists.shape, lists.dtype),
            pltpu.SemaphoreType.DMA((copies,)),
            pltpu.SemaphoreType.DMA((copies,)),
        ],
        compiler_params=pltpu.CompilerParams(collective_id=0, has_side_effects=True),
        name="gather_window",
    )(points, weights, lists)


def pieces_of(value, count):
    parts = []
    for _ in range(count):
        part = value.astype(jnp.bfloat16).astype(jnp.float32)
        parts.append(part)
        value = value - part
    return parts


def extra_rows(first, second, rows, width):
    row = lax.broadcasted_iota(jnp.int32, (rows, width), 0)
    result = jnp.zeros((rows, width), jnp.float32)
    for i, value in enumerate(list(first) + list(second)):
        result = jnp.where(row == i, value, result)
    return result


def pairs_kernel(local, helpers, tasks, points, weights, far_points, near_points, near_weights,
                 own_sums, far_sums, out, targets, sources, held_weights, exponents, kernels):
    dims, width = points.shape[1:]
    group = local * helpers
    depth = targets.shape[1]
    ones = [jnp.ones((1, width), jnp.float32)] * 3

    def half_norm(value):
        return pieces_of(-0.5 * jnp.sum(value * value, axis=0, keepdims=True), 3)

    def prepare_target(index, block):
        targets[index, pl.ds(0, dims), :] = block
        targets[index, pl.ds(dims, depth - dims), :] = extra_rows(
            ones, half_norm(block.astype(jnp.float32)), depth - dims, width
        ).astype(jnp.bfloat16)

    def prepare_source(index, block):
        value = block.astype(jnp.float32)
        rows = [value, extra_rows(half_norm(value), ones, depth - dims, width)]
        sources[index] = jnp.concatenate(rows, axis=0).T.astype(jnp.bfloat16)

    def each_leaf(leaf, carry):
        prepare_target(leaf, points[leaf])
        prepare_source(local + leaf, points[leaf])
        prepare_source(leaf, near_points[0, leaf])
        prepare_source(2 * local + leaf, near_points[1, leaf])
        held_weights[leaf] = near_weights[0, leaf]
        held_weights[local + leaf] = weights[leaf]
        held_weights[2 * local + leaf] = near_weights[1, leaf]
        return carry

    for leaf in range(local):
        each_leaf(leaf, 0)

    def each_far(distance, carry):
        for leaf in range(local):
            prepare_target((distance + 1) * local + leaf, far_points[distance, leaf])
        return carry

    lax.fori_loop(0, helpers - 1, each_far, 0)

    total = tasks[2, 0]
    out[...] = jnp.zeros(out.shape, jnp.float32)

    def add_products(step):
        for part in range(TOGETHER):
            number = step * TOGETHER + part
            source, target = tasks[1, number], tasks[0, number]
            out[target] += jnp.dot(held_weights[source], kernels[part], preferred_element_type=jnp.float32)

    def take_exponentials():
        for part in range(TOGETHER):
            kernels[part] = jnp.exp(exponents[part]).astype(jnp.bfloat16)

    def find_exponents(step):
        for part in range(TOGETHER):
            number = step * TOGETHER + part
            source, target = tasks[1, number], tasks[0, number]
            exponents[part] = jnp.dot(sources[source], targets[target], preferred_element_type=jnp.float32)

    find_exponents(0)
    take_exponentials()
    find_exponents(1)

    def each_step(step, carry):
        add_products(step)
        take_exponentials()
        find_exponents(step + 2)
        return carry

    steps = lax.div(total + TOGETHER - 1, TOGETHER)
    lax.fori_loop(0, steps - 1, each_step, 0)

    @pl.when(total > 0)
    def _():
        add_products(steps - 1)

    own_sums[...] = out[pl.ds(0, local)]
    far_sums[...] = out[pl.ds(local, group - local)].astype(jnp.bfloat16).reshape(far_sums.shape)


def sum_pairs(helpers, points, weights, far_points, near_points, near_weights, tasks):
    local, dims, width = points.shape
    vectors = weights.shape[1]
    group = local * helpers
    vmem = pl.BlockSpec(memory_space=pltpu.VMEM)
    smem = pl.BlockSpec(memory_space=pltpu.SMEM)
    return pl.pallas_call(
        functools.partial(pairs_kernel, local, helpers),
        out_shape=(
            jax.ShapeDtypeStruct((local, vectors, width), jnp.float32),
            jax.ShapeDtypeStruct((helpers - 1, local, vectors, width), jnp.bfloat16),
        ),
        in_specs=[smem] + [vmem] * 5,
        out_specs=(vmem, vmem),
        scratch_shapes=[
            pltpu.VMEM((group + 1, vectors, width), jnp.float32),
            pltpu.VMEM((group + 1, dims + EXTRA, width), jnp.bfloat16),
            pltpu.VMEM((3 * local, width, dims + EXTRA), jnp.bfloat16),
            pltpu.VMEM((3 * local, vectors, width), jnp.bfloat16),
            pltpu.VMEM((TOGETHER, width, width), jnp.float32),
            pltpu.VMEM((TOGETHER, width, width), jnp.bfloat16),
        ],
        name="sum_pairs",
    )(tasks, points, weights, far_points, near_points, near_weights)


def return_kernel(helpers, far_sums, landed, send_sems, recv_sems):
    owner = lax.axis_index("owner")
    helper = lax.axis_index("helper")
    barrier = pltpu.get_barrier_semaphore()
    for distance in range(1, helpers):
        pl.semaphore_signal(
            barrier, inc=1, device_id=(owner, partner_of(helper, distance)), device_id_type=MESH
        )
    pl.semaphore_wait(barrier, helpers - 1)
    copies = []
    for distance in range(1, helpers):
        one = pltpu.make_async_remote_copy(
            src_ref=far_sums.at[distance - 1],
            dst_ref=landed.at[distance - 1],
            send_sem=send_sems.at[distance - 1],
            recv_sem=recv_sems.at[distance - 1],
            device_id=(owner, partner_of(helper, distance)),
            device_id_type=MESH,
        )
        copies.append(one)
    for one in reversed(copies):
        one.start()
    for one in copies:
        one.wait()


def return_sums(helpers, far_sums):
    any_space = pl.BlockSpec(memory_space=pl.ANY)
    return pl.pallas_call(
        functools.partial(return_kernel, helpers),
        out_shape=jax.ShapeDtypeStruct(far_sums.shape, far_sums.dtype),
        in_specs=[any_space],
        out_specs=any_space,
        scratch_shapes=[pltpu.SemaphoreType.DMA((helpers - 1,)), pltpu.SemaphoreType.DMA((helpers - 1,))],
        compiler_params=pltpu.CompilerParams(collective_id=1, has_side_effects=True),
        name="return_sums",
    )(far_sums)


ALONE, FIRST, SECOND, THIRD = 4, 8, 8, 12


def slot_count(local):
    return local + FIRST + SECOND + THIRD


def phase_of(target, source, local):
    half = local // 2
    quarter = half // 2
    first = (target < local) | ((target >= local) & (target < local + quarter))
    first = first | ((target >= 2 * local + half) & (target < 2 * local + half + quarter))
    early = first | ((target >= local) & (target < local + half)) | ((target >= 2 * local + half) & (target < 3 * local))
    phase = jnp.where(target < 3 * local, 2, 3)
    phase = jnp.where(early, 1, phase)
    phase = jnp.where(first & (source < 2 * local), 0, phase)
    return jnp.where((target < local) & ((source < local) | (source >= 2 * local)), 4, phase)


def order_tasks(bases, local, lists):
    group, slots = lists.shape
    count = 3 * local
    length = task_length(group, local)
    lists = jnp.where(lists < 0, -(1 << 20), lists)
    row = lax.broadcasted_iota(jnp.int32, (group, 128), 0)
    column = lax.broadcasted_iota(jnp.int32, (group, 128), 1)
    table = jnp.zeros((group, 128), jnp.float32)
    for source in range(count):
        leaf = bases[source // local] + source % local
        one = jnp.max(jnp.where(lists == leaf, 1.0, 0.0), axis=1, keepdims=True)
        table = jnp.where(column == source, one, table)
    table = jnp.where((row == column) & (row < local), 0.0, table)
    phase = phase_of(row, column, local)
    phased = jnp.concatenate([jnp.where(phase == p, table, 0.0) for p in range(5)], axis=0)
    rows = 5 * group
    counted = phased.astype(jnp.bfloat16)
    above = lax.broadcasted_iota(jnp.int32, (rows, rows), 0) > lax.broadcasted_iota(jnp.int32, (rows, rows), 1)
    left = lax.broadcasted_iota(jnp.int32, (128, 128), 0) < lax.broadcasted_iota(jnp.int32, (128, 128), 1)
    inside = jnp.dot(counted, jnp.where(left, 1.0, 0.0).astype(jnp.bfloat16), preferred_element_type=jnp.float32)
    before = jnp.dot(jnp.where(above, 1.0, 0.0).astype(jnp.bfloat16), counted, preferred_element_type=jnp.float32)
    rank = inside + jnp.sum(before, axis=1, keepdims=True)
    rank = jnp.where(phased > 0.5, rank + 1.0, 0.0)
    rank = sum(rank[p * group:(p + 1) * group] for p in range(5)) - 1.0
    in_row = jnp.sum(phased, axis=1, keepdims=True)
    ends = [jnp.sum(in_row[:(p + 1) * group], axis=0, keepdims=True) for p in range(5)]
    place = lax.broadcasted_iota(jnp.int32, (group, length), 1).astype(jnp.float32)
    code_row = lax.broadcasted_iota(jnp.int32, (group, length), 0).astype(jnp.float32) * 256.0
    codes = jnp.zeros((group, length), jnp.float32)
    for source in range(count):
        codes = jnp.where(place == rank[:, source:source + 1], code_row + float(source), codes)
    codes = jnp.sum(codes, axis=0, keepdims=True)
    codes = jnp.where(place[:1] < ends[4], codes, float(group * 256)).astype(jnp.int32)
    line = lax.broadcasted_iota(jnp.int32, (8, length), 0)
    result = jnp.where(line == 0, codes // 256, codes % 256)
    for p in range(5):
        result = jnp.where(line == 2 + p, ends[p].astype(jnp.int32), result)
    return result


def within(value, last):
    return lax.max(lax.min(value, last), 0)


def slot_starts(tasks):
    second = lax.min(tasks[2, 0], FIRST)
    third = lax.min(tasks[3, 0], second + SECOND)
    rest = lax.min(tasks[4, 0], third + THIRD)
    return 0, second, third, rest


def kept_of(tasks):
    return within(tasks[6, 0] - tasks[5, 0], KEPT)


def slot_task(tasks, group, start, end, slot):
    number = within(start + slot, tasks.shape[1] - 1)
    inside = number < end
    target = jnp.where(inside, tasks[0, number], group)
    return within(tasks[1, number], 3 * group // 4 - 1), within(target, group)


def window_kernel(owners, points, weights, lists, sources, targets, held_weights, task_scalars, results,
                  own_points, own_weights, lists_here, far_lists, far_points, near_points, near_weights,
                  kernels, tasks, send_sems, recv_sems, local_sems):
    local, dims, width = points.shape
    helpers = 4
    group = local * helpers
    half = local // 2
    depth = targets.shape[1]
    owner = lax.axis_index("owner")
    helper = lax.axis_index("helper")
    odd = lax.rem(owner, 2)
    chip_owner = owner + 1 - 2 * odd
    next_owner = owner - 1 + 2 * odd
    has_next = (next_owner >= 0) & (next_owner < owners)

    fetches = [
        pltpu.make_async_copy(src, dst, local_sems.at[i])
        for i, (src, dst) in enumerate(
            ((points, own_points), (weights, own_weights), (lists, lists_here))
        )
    ]
    for one in fetches:
        one.start()

    def beside(distance):
        return (owner, partner_of(helper, distance))

    barrier = pltpu.get_barrier_semaphore()
    for device in [beside(1), beside(2), beside(3), (chip_owner, helper)]:
        pl.semaphore_signal(barrier, inc=1, device_id=device, device_id_type=MESH)

    @pl.when(has_next)
    def _():
        pl.semaphore_signal(barrier, inc=1, device_id=(next_owner, helper), device_id_type=MESH)

    pl.semaphore_wait(barrier, helpers + jnp.where(has_next, 1, 0))

    def copy(number, src, dst, device):
        return pltpu.make_async_remote_copy(
            src_ref=src,
            dst_ref=dst,
            send_sem=send_sems.at[number],
            recv_sem=recv_sems.at[number],
            device_id=device,
            device_id_type=MESH,
        )

    list_copies = [copy(d - 1, lists, far_lists.at[d - 1], beside(d)) for d in (1, 2, 3)]
    quarter = half // 2
    sent = []
    for begin, size in ((0, quarter), (quarter, half - quarter), (half, half)):
        for distance in (1, 2):
            part = pl.ds((begin + half * (distance - 1)) % local, size)
            sent.append(
                copy(3 + len(sent), points.at[part], far_points.at[distance - 1, part], beside(distance))
            )
    relayed = []
    for distance in (1, 2):
        part = pl.ds(half * (distance - 1), half)
        relayed.append(
            copy(12 + distance, far_points.at[distance - 1, part], far_points.at[2, part], beside(3 - distance))
        )
    chip = [
        copy(9, points, near_points.at[0], (chip_owner, helper)),
        copy(10, weights, near_weights.at[0], (chip_owner, helper)),
    ]
    beyond = [
        copy(11, points, near_points.at[1], (next_owner, helper)),
        copy(12, weights, near_weights.at[1], (next_owner, helper)),
    ]
    for one in list_copies + sent[:2] + chip:
        one.start()

    @pl.when(has_next)
    def _():
        for one in beyond:
            one.start()

    for one in sent[2:]:
        one.start()

    ones = [jnp.ones((1, width), jnp.float32)] * 3

    def half_norm(value):
        return pieces_of(-0.5 * jnp.sum(value * value, axis=0, keepdims=True), 3)

    def prepare_target(index, block):
        targets[index, pl.ds(0, dims), :] = block
        targets[index, pl.ds(dims, depth - dims), :] = extra_rows(
            ones, half_norm(block.astype(jnp.float32)), depth - dims, width
        ).astype(jnp.bfloat16)

    def prepare_source(index, block):
        value = block.astype(jnp.float32)
        rows = [value, extra_rows(half_norm(value), ones, depth - dims, width)]
        sources[index] = jnp.concatenate(rows, axis=0).T.astype(jnp.bfloat16)

    waiting = []

    def multiply():
        for source, slot, place in waiting:
            results[place] = jnp.dot(held_weights[source], kernels[slot], preferred_element_type=jnp.float32)
        waiting.clear()

    def work(pairs, base):
        side = base // ALONE % 2 * ALONE
        for i, (source, target) in enumerate(pairs):
            exponents = jnp.dot(sources[source], targets[target], preferred_element_type=jnp.float32)
            kernels[side + i] = jnp.exp(exponents).astype(jnp.bfloat16)
        multiply()
        waiting.extend((source, side + i, base + i) for i, (source, _) in enumerate(pairs))

    def work_slots(start, end, slots, base):
        for first in range(0, slots, ALONE):
            work([slot_task(task_scalars, group, start, end, first + i) for i in range(ALONE)], base + first)

    for one in fetches[:2]:
        one.wait()
    for leaf in range(local):
        prepare_target(leaf, own_points[leaf])
        prepare_source(leaf, own_points[leaf])
        held_weights[leaf] = own_weights[leaf]
    targets[group] = jnp.zeros(targets.shape[1:], jnp.bfloat16)
    work([(leaf, leaf) for leaf in range(local)], 0)

    fetches[2].wait()
    for one in list_copies:
        one.wait_recv()
    whole = jnp.concatenate([lists_here[...]] + [far_lists[i] for i in range(helpers - 1)], axis=0)
    bases = [o * group + helper * local for o in (owner, chip_owner, next_owner)]
    tasks[...] = order_tasks(bases, local, whole)
    to_scalars = pltpu.make_async_copy(tasks, task_scalars, local_sems.at[3])
    to_scalars.start()
    for one in chip:
        one.wait_recv()
    for leaf in range(local):
        prepare_source(local + leaf, near_points[0, leaf])
        held_weights[local + leaf] = near_weights[0, leaf]
    to_scalars.wait()
    starts = slot_starts(task_scalars)
    for one in sent[:2]:
        one.wait_recv()
    for leaf in range(quarter):
        prepare_target(local + leaf, far_points[0, leaf])
        prepare_target(2 * local + half + leaf, far_points[1, half + leaf])
    work_slots(starts[0], task_scalars[2, 0], FIRST, local)

    for place, one in enumerate(relayed):
        sent[2 + place].wait_recv()
        one.start()
    for leaf in range(quarter, half):
        prepare_target(local + leaf, far_points[0, leaf])
        prepare_target(2 * local + half + leaf, far_points[1, half + leaf])

    @pl.when(has_next)
    def _():
        for one in beyond:
            one.wait_recv()
        for leaf in range(local):
            prepare_source(2 * local + leaf, near_points[1, leaf])
            held_weights[2 * local + leaf] = near_weights[1, leaf]

    work_slots(starts[1], task_scalars[3, 0], SECOND, local + FIRST)

    for one in sent[4:]:
        one.wait_recv()
    for leaf in range(half):
        prepare_target(local + half + leaf, far_points[0, half + leaf])
        prepare_target(2 * local + leaf, far_points[1, leaf])
    work_slots(starts[2], task_scalars[4, 0], THIRD, local + FIRST + SECOND)

    for one in relayed:
        one.wait_recv()
    for leaf in range(local):
        prepare_target(3 * local + leaf, far_points[2, leaf])
    multiply()
    for one in list_copies + sent + relayed + chip:
        one.wait_send()

    @pl.when(has_next)
    def _():
        for one in beyond:
            one.wait_send()


def gather_and_begin(owners, points, weights, lists):
    local, dims, width = points.shape
    vectors = weights.shape[1]
    group = 4 * local
    depth = dims + EXTRA
    vmem = pl.BlockSpec(memory_space=pltpu.VMEM)
    hbm = pl.BlockSpec(memory_space=pltpu.HBM)
    length = task_length(group, local)
    return pl.pallas_call(
        functools.partial(window_kernel, owners),
        out_shape=(
            pltpu.VMEM((3 * local, width, depth), jnp.bfloat16),
            pltpu.VMEM((group + 1, depth, width), jnp.bfloat16),
            pltpu.VMEM((3 * local, vectors, width), jnp.bfloat16),
            pltpu.SMEM((8, length), jnp.int32),
            pltpu.VMEM((slot_count(local), vectors, width), jnp.float32),
        ),
        in_specs=[hbm, hbm, hbm],
        out_specs=(vmem,) * 3 + (pl.BlockSpec(memory_space=pltpu.SMEM), vmem),
        scratch_shapes=[
            pltpu.VMEM(points.shape, points.dtype),
            pltpu.VMEM(weights.shape, weights.dtype),
            pltpu.VMEM(lists.shape, lists.dtype),
            pltpu.VMEM((3,) + lists.shape, lists.dtype),
            pltpu.VMEM((3,) + points.shape, points.dtype),
            pltpu.VMEM((2,) + points.shape, points.dtype),
            pltpu.VMEM((2,) + weights.shape, weights.dtype),
            pltpu.VMEM((2 * ALONE, width, width), jnp.bfloat16),
            pltpu.VMEM((8, length), jnp.int32),
            pltpu.SemaphoreType.DMA((15,)),
            pltpu.SemaphoreType.DMA((15,)),
            pltpu.SemaphoreType.DMA((4,)),
        ],
        compiler_params=pltpu.CompilerParams(
            collective_id=2, has_side_effects=True, vmem_limit_bytes=VMEM_BYTES
        ),
        name="gather_and_begin",
    )(*(pltpu.with_memory_space_constraint(one, pltpu.HBM) for one in (points, weights, lists)))


def rest_kernel(local, *refs):
    width = refs[2].shape[2]
    vectors = refs[3].shape[1]
    half = width // 2
    accumulators = [
        pltpu.ACC(unit)((rows, half), jnp.float32)
        for rows in (half, half, vectors, vectors)
        for unit in (0, 1)
    ]
    pl.run_scoped(functools.partial(rest_body, local, *refs), *accumulators)


def rest_body(local, tasks, sources, targets, held_weights, results, own_sums, far_sums, out, kernels, *accumulators):
    width = targets.shape[2]
    half = width // 2
    group = 4 * local
    starts = slot_starts(tasks)
    first = starts[3]
    total = tasks[6, 0] - kept_of(tasks) - first
    units = (0, 1)
    exponents = (accumulators[0:2], accumulators[2:4])
    products = (accumulators[4:6], accumulators[6:8])

    def task(number):
        place = lax.max(number, 0) + first
        return tasks[1, place], jnp.where(number < total, tasks[0, place], group)

    def columns(unit):
        return pl.ds(unit * half, half)

    def widened(value, axis):
        missing = list(value.shape)
        missing[axis] = half - value.shape[axis]
        return jnp.concatenate([value, jnp.zeros(missing, value.dtype)], axis=axis)

    def stage_target(number):
        _, target = task(number)
        for unit in units:
            pltpu.matmul_push_rhs(widened(targets[target, :, columns(unit)], 0), 0, unit)

    def find_exponents(number, part):
        source, _ = task(number)
        for unit in units:
            pltpu.matmul_acc_lhs(
                exponents[part][unit],
                widened(sources[source, pl.ds(part * half, half), :], 1),
                0 if part == 0 else None,
            )

    def take_exponentials(part, slot):
        for unit in units:
            kernels[slot, pl.ds(part * half, half), columns(unit)] = jnp.exp(
                pltpu.matmul_pop(exponents[part][unit])
            ).astype(jnp.bfloat16)

    def stage_kernel(slot, part):
        for unit in units:
            pltpu.matmul_push_rhs(kernels[slot, pl.ds(part * half, half), columns(unit)], 1, unit)

    def multiply(number, part, side):
        source, _ = task(number)
        for unit in units:
            pltpu.matmul_acc_lhs(products[side][unit], held_weights[source, :, pl.ds(part * half, half)], 1)

    def add_product(number, side):
        _, target = task(number)
        for unit in units:
            out[target, :, columns(unit)] += pltpu.matmul_pop(products[side][unit])

    stage_target(0)
    for leaf in range(local):
        out[leaf] = results[leaf]
    out[pl.ds(local, group + 1 - local)] = jnp.zeros((group + 1 - local,) + out.shape[1:], jnp.float32)
    base = local
    for phase, slots in enumerate((FIRST, SECOND, THIRD)):
        for slot in range(slots):
            _, target = slot_task(tasks, group, starts[phase], tasks[2 + phase, 0], slot)
            out[target] += results[base + slot]
        base += slots

    def advance(number, slot, age):
        find_exponents(number, 0)
        if age >= 1:
            take_exponentials(1, (slot - 1) % RING)
        stage_target(number + 1)
        if age >= 2:
            stage_kernel((slot - 2) % RING, 0)
        find_exponents(number, 1)
        if age >= 2:
            multiply(number - 2, 0, slot % 2)
            stage_kernel((slot - 2) % RING, 1)
        take_exponentials(0, slot)
        if age >= 2:
            multiply(number - 2, 1, slot % 2)
        if age >= 3:
            add_product(number - 3, (slot - 1) % 2)

    for number in range(4):
        advance(number, number % RING, number)

    def each_step(step, carry):
        for part in range(RING):
            advance(step * RING + part, part, 4)
        return carry

    begun = 4 // RING
    steps = lax.max(lax.div(total + RING - 1, RING), begun)
    lax.fori_loop(begun, steps, each_step, 0)

    last = steps * RING
    find_exponents(last, 0)
    take_exponentials(1, RING - 1)
    for age in (2, 1):
        slot = RING - age
        stage_kernel(slot, 0)
        multiply(last - age, 0, slot % 2)
        stage_kernel(slot, 1)
        multiply(last - age, 1, slot % 2)
        add_product(last - age - 1, (slot - 1) % 2)
    add_product(last - 1, (RING - 1) % 2)
    for unit in units:
        kernels[0, pl.ds(0, half), columns(unit)] = pltpu.matmul_pop(exponents[0][unit]).astype(jnp.bfloat16)

    own_sums[...] = out[pl.ds(0, local)]
    far_sums[...] = out[pl.ds(local, group - local)].astype(jnp.bfloat16).reshape(far_sums.shape)


def sum_rest(local, sources, targets, held_weights, tasks, results):
    width = targets.shape[2]
    vectors = held_weights.shape[1]
    group = 4 * local
    vmem = pl.BlockSpec(memory_space=pltpu.VMEM)
    smem = pl.BlockSpec(memory_space=pltpu.SMEM)
    return pl.pallas_call(
        functools.partial(rest_kernel, local),
        out_shape=(
            pltpu.VMEM((local, vectors, width), jnp.float32),
            pltpu.VMEM((3, local, vectors, width), jnp.bfloat16),
        ),
        in_specs=[smem] + [vmem] * 4,
        out_specs=(vmem, vmem),
        scratch_shapes=[
            pltpu.VMEM((group + 1, vectors, width), jnp.float32),
            pltpu.VMEM((RING, width, width), jnp.bfloat16),
        ],
        compiler_params=pltpu.CompilerParams(vmem_limit_bytes=VMEM_BYTES),
        name="sum_rest",
    )(tasks, sources, targets, held_weights, results)


def finish_kernel(local, tasks, sources, targets, held_weights, own_sums, far_sums, potential, landed, kernels,
                  products, send_sems, recv_sems):
    owner = lax.axis_index("owner")
    helper = lax.axis_index("helper")
    barrier = pltpu.get_barrier_semaphore()
    devices = [(owner, partner_of(helper, distance)) for distance in (1, 2, 3)]
    for device in devices:
        pl.semaphore_signal(barrier, inc=1, device_id=device, device_id_type=MESH)
    pl.semaphore_wait(barrier, 3)
    copies = [
        pltpu.make_async_remote_copy(
            src_ref=far_sums.at[number],
            dst_ref=landed.at[number],
            send_sem=send_sems.at[number],
            recv_sem=recv_sems.at[number],
            device_id=device,
            device_id_type=MESH,
        )
        for number, device in enumerate(devices)
    ]
    for one in reversed(copies):
        one.start()
    kept = kept_of(tasks)
    begin = tasks[6, 0] - kept
    pairs = [slot_task(tasks, 4 * local, begin, tasks[6, 0], slot) for slot in range(KEPT)]
    for first in range(0, KEPT + ALONE, ALONE):
        for slot in range(first, min(first + ALONE, KEPT)):
            source, target = pairs[slot]
            exponents = jnp.dot(sources[source], targets[target], preferred_element_type=jnp.float32)
            kernels[slot] = jnp.exp(exponents).astype(jnp.bfloat16)
        for slot in range(max(first - ALONE, 0), first):
            source, _ = pairs[slot]
            products[slot] = jnp.dot(held_weights[source], kernels[slot], preferred_element_type=jnp.float32)
    for leaf in range(local):
        total = own_sums[leaf]
        for slot in range(KEPT):
            total = total + jnp.where(pairs[slot][1] == leaf, products[slot], 0.0)
        potential[leaf] = total
    for one in copies:
        one.wait()


def finish(local, tasks, sources, targets, held_weights, own_sums, far_sums):
    width = targets.shape[2]
    vectors = held_weights.shape[1]
    vmem = pl.BlockSpec(memory_space=pltpu.VMEM)
    smem = pl.BlockSpec(memory_space=pltpu.SMEM)
    return pl.pallas_call(
        functools.partial(finish_kernel, local),
        out_shape=(pltpu.VMEM(own_sums.shape, jnp.float32), pltpu.VMEM(far_sums.shape, far_sums.dtype)),
        in_specs=[smem] + [vmem] * 5,
        out_specs=(vmem, vmem),
        scratch_shapes=[
            pltpu.VMEM((KEPT, width, width), jnp.bfloat16),
            pltpu.VMEM((KEPT, vectors, width), jnp.float32),
            pltpu.SemaphoreType.DMA((3,)),
            pltpu.SemaphoreType.DMA((3,)),
        ],
        compiler_params=pltpu.CompilerParams(
            collective_id=3, has_side_effects=True, vmem_limit_bytes=VMEM_BYTES
        ),
        name="finish",
    )(tasks, sources, targets, held_weights, own_sums, far_sums)


def on_device(points, weights, neighbours, counts):
    owners = lax.axis_size("owner")
    helpers = lax.axis_size("helper")
    local = points.shape[0]
    if helpers == 4 and local == ALONE and owners % 2 == 0:
        sources, targets, held_weights, tasks, results = gather_and_begin(owners, points, weights, neighbours)
        own_sums, far_sums = sum_rest(local, sources, targets, held_weights, tasks, results)
        own_sums, landed = finish(local, tasks, sources, targets, held_weights, own_sums, far_sums)
        parts = [landed[i].astype(jnp.float32) for i in range(3)]
        return own_sums + (parts[0] + parts[1] + parts[2])
    far_points, near_points, near_weights, tasks = gather_window(owners, helpers, points, weights, neighbours)
    own_sums, far_sums = sum_pairs(helpers, points, weights, far_points, near_points, near_weights, tasks)
    landed = return_sums(helpers, far_sums)
    return own_sums + jnp.sum(landed.astype(jnp.float32), axis=0)


def solution(mesh):
    placed = (
        P(("owner", "helper"), None, None),
        P(("owner", "helper"), None, None),
        P(("owner", "helper"), None),
        P(("owner", "helper")),
    )
    return jax.shard_map(
        on_device,
        mesh=mesh,
        in_specs=placed,
        out_specs=P(("owner", "helper"), None, None),
        check_vma=False,
    )
```
